128 devices in a mesh: row: 16 (over y, z), col: 8 (over x, core).
Axes of the slice: x: 4, y: 4, z: 4, core: 2. Of those that a mesh axis runs over, the one named last changes fastest.
Arguments:
- coords: float32 [4, 3, 8, 16384], P(None, None, None, ('row', 'col')), may hold values from -6 to 6
- chrom_lengths: int32 [46], replicated, may hold values from 1 to 8192, 131072 in all
- band_counts: int32 [4, 8, 128, 32], P(None, None, ('row', 'col')), may hold values from 16 to 111
- inter_pairs: int32 [4, 4096, 2], replicated, may hold values from 0 to 1023, as said below
- inter_counts: int32 [4, 4096], replicated, may hold values from 16 to 111
Outputs:
- grad: float32 [4, 3, 8, 16384], P(None, None, None, ('row', 'col'))
The draws below stay inside these ranges and needn't reach their ends.
Inputs may be any that keep to these rules, and one draw needn't show every extreme that they name: `inter_pairs`: every entry names two blocks of the structure. for every g in 0 to 15 and h in 0 to 7, at most 64 entries of one structure have (I mod 128) div 8 = g and J mod 8 = h, and one such (g, h) has exactly 64; the same holds with the roles of I and J exchanged.
All inputs are finite; a program needn't handle non-finite values.
Results may differ from the reference program's by a relative error of at most 0.0003.
Values sent between devices are 32-bit elements; how exact they have to be, the bound alone decides.
A program may use at most 64 MiB of HBM per device.

```python
import math
import jax
import jax.numpy as jnp
import numpy as np
from jax import lax

STRUCTURES = 4
BLOCK = 128
BAND_BLOCKS = 31
SWEEPS = 8
CHROMOSOMES = 46
LIST_CAP = 64
GROUPS = 128
SWEEP_BEADS = 16384
BLOCKS = 1024
BEADS = 131072
LISTED = 4096
N_COL = 8


def draw_inter_pairs(key, part):
    slot_count = GROUPS * LIST_CAP

    def owners(owner_key):
        key_order, key_favor = jax.random.split(owner_key)
        slot_order = jax.random.permutation(key_order, slot_count).astype(jnp.int32)
        favored = jax.random.randint(key_favor, (), 0, GROUPS)
        slot_score = slot_order + jnp.where(jnp.arange(slot_count) // LIST_CAP == favored, slot_count, 0).astype(jnp.int32)
        top_score, picked = lax.top_k(slot_score, LISTED)
        return (picked // LIST_CAP).astype(jnp.int32)

    def one_structure(member_key):
        key_first, key_second, key_mix, key_sweep_first, key_sweep_second = jax.random.split(member_key, 5)
        first_owner = owners(key_first)
        second_owner = jax.random.permutation(key_mix, owners(key_second))
        first_sweep = jax.random.randint(key_sweep_first, (LISTED,), 0, SWEEPS)
        second_sweep = jax.random.randint(key_sweep_second, (LISTED,), 0, SWEEPS)
        first_row = first_owner // N_COL
        first_col = first_owner % N_COL
        second_row = second_owner // N_COL
        second_col = second_owner % N_COL
        first_block = first_sweep * GROUPS + first_row * N_COL + second_col
        second_block = second_sweep * GROUPS + second_row * N_COL + first_col
        return jnp.stack([first_block, second_block], axis=-1)
    structure_keys = jax.random.split(jax.random.fold_in(key, 7), STRUCTURES)
    return jax.vmap(one_structure)(structure_keys).astype(jnp.int32)


def touch_ends(array, stream_key, low, largest):
    place = [jax.random.randint(jax.random.fold_in(stream_key, axis), (), 0, length) for axis, length in enumerate(array.shape)]
    widest = array.shape.index(max(array.shape))
    next_to = place[:widest] + [(place[widest] + 1) % array.shape[widest]] + place[widest + 1:]
    return array.at[tuple(place)].set(low).at[tuple(next_to)].set(largest)


def block_scale(rng, dims, cuts, low, largest):
    factor_of, own = 1.0, jax.random.fold_in(rng, 6)
    for position, parts in cuts:
        heights = jnp.exp(jax.random.uniform(jax.random.fold_in(own, position), (parts,), jnp.float32, low / len(cuts), largest / len(cuts)))
        factor_of = factor_of * jnp.repeat(heights, dims[position] // parts).reshape([-1 if axis == position else 1 for axis in range(len(dims))])
    return factor_of


def split_up(amount, total, bound, lean):
    loads = [(1 << 20) // math.isqrt(grade ** lean) + 1 for grade in range(2, amount + 1)]
    spare, counts = total - bound - (amount - 1), [1] * (amount - 1)
    while spare > 0:
        movable = [i for i in range(amount - 1) if counts[i] < bound]
        mass, left = sum([loads[i] for i in movable]), spare
        for i in movable:
            more = min(bound - counts[i], max(1, left * loads[i] // mass), spare)
            counts[i] = counts[i] + more
            spare = spare - more
    return np.array([bound] + counts)


def ragged_sizes(own_key, count, total, bound, lean):
    if count == 2:
        one = jax.random.randint(own_key, (), max(1, total - bound), min(bound, total - 1) + 1)
        return jnp.stack([one, total - one])
    sizes = jnp.asarray(split_up(count, total, bound, lean), jnp.int32)
    couples = (count - 1) // 2
    source_of, sink = sizes[1:1 + 2 * couples:2], sizes[2:2 + 2 * couples:2]
    margin = jnp.minimum(source_of - 1, bound - sink)
    moved = jax.random.randint(jax.random.fold_in(own_key, 1), (couples,), 0, 1 << 20) % (margin + 1)
    sizes = sizes.at[1:1 + 2 * couples:2].set(source_of - moved).at[2:2 + 2 * couples:2].set(sink + moved)
    return sizes[jax.random.permutation(jax.random.fold_in(own_key, 2), count)]


def gaussian(rng, dims, width, bound, cuts=(), held_as=jnp.bfloat16):
    drawn = width * jax.random.normal(rng, dims, jnp.float32)
    if cuts:
        drawn = drawn * block_scale(rng, dims, cuts, -0.22, 0.18)
    return jnp.clip(drawn, -bound, bound).astype(held_as)


def setup_inputs(seed: int = 0) -> dict:
    arg_keys = jax.random.split(jax.random.key(seed), 6)
    return {
        "coords": gaussian(arg_keys[0], (STRUCTURES, 3, SWEEPS, SWEEP_BEADS), 1.0, 6.0, ((3, 128),), jnp.float32),
        "chrom_lengths": ragged_sizes(arg_keys[1], CHROMOSOMES, BEADS, BEADS // 16, 2).astype(jnp.int32),
        "band_counts": touch_ends(jax.random.randint(arg_keys[2], (STRUCTURES, SWEEPS, GROUPS, BAND_BLOCKS + 1), 16, 112), jax.random.fold_in(arg_keys[2], 1), 16, 111).astype(jnp.int32),
        "inter_pairs": draw_inter_pairs(jax.random.fold_in(arg_keys[5], 71), 0),
        "inter_counts": touch_ends(jax.random.randint(arg_keys[4], (STRUCTURES, LISTED), 16, 112), jax.random.fold_in(arg_keys[4], 1), 16, 111).astype(jnp.int32),
    }


CONTACT_SHIFT = 3.0
CONTACT_SLOPE = 0.5
BACKGROUND = 0.5

def chromosome(beads, chrom_ends):
    return lax.optimization_barrier(jnp.sum((chrom_ends <= beads[..., None]).astype(jnp.int32), axis=-1)).astype(jnp.int32)

def pair_terms(first_points, second_points, pair_mask, tile_counts, tile_number):
    rows_here = first_points.shape[1]
    difference = first_points[:, :, None] - second_points[:, None, :]
    distance = lax.optimization_barrier(jnp.sum(difference * difference, axis=0))
    chance = jax.nn.sigmoid(CONTACT_SHIFT - CONTACT_SLOPE * distance)
    masked = chance * pair_mask
    expect = BACKGROUND + lax.optimization_barrier(jnp.sum(masked.reshape(rows_here, tile_number, BLOCK), axis=(0, 2))) / BLOCK
    weight = 1.0 - tile_counts.astype(jnp.float32) / expect
    factor = -2.0 * CONTACT_SLOPE / BLOCK * (masked * (1.0 - chance)).reshape(rows_here, tile_number, BLOCK) * weight[None, :, None]
    factor = factor.reshape(rows_here, tile_number * BLOCK)
    pair_force = factor[None] * difference
    return (lax.optimization_barrier(jnp.sum(pair_force, axis=2)), -lax.optimization_barrier(jnp.sum(pair_force, axis=1)))

def add_at(grad_total, block_start, addition):
    current = lax.dynamic_slice_in_dim(grad_total, block_start, addition.shape[1], 1)
    return lax.dynamic_update_slice_in_dim(grad_total, current + addition, block_start, 1)

def structure_grad(positions, labels, band, pair_ids, listed):
    band_span = (BAND_BLOCKS + 1) * BLOCK
    pad_extra = BAND_BLOCKS * BLOCK
    padded = jnp.concatenate([positions, jnp.zeros((3, pad_extra), jnp.float32)], axis=1)
    padded_labels = jnp.concatenate([labels, jnp.full((pad_extra,), -1, jnp.int32)])
    later_pair = jnp.arange(band_span)[None, :] > jnp.arange(BLOCK)[:, None]

    def band_step(grad_total, block_id):
        block_start = (block_id * BLOCK).astype(jnp.int32)
        first_points = lax.dynamic_slice_in_dim(padded, block_start, BLOCK, 1)
        second_points = lax.dynamic_slice_in_dim(padded, block_start, band_span, 1)
        left_chrom = lax.dynamic_slice_in_dim(padded_labels, block_start, BLOCK, 0)
        right_chrom = lax.dynamic_slice_in_dim(padded_labels, block_start, band_span, 0)
        pair_mask = ((left_chrom[:, None] == right_chrom[None, :]) & later_pair).astype(jnp.float32)
        gain_first, gain_second = pair_terms(first_points, second_points, pair_mask, band[block_id], BAND_BLOCKS + 1)
        grad_total = add_at(grad_total, block_start, gain_second)
        grad_total = add_at(grad_total, block_start, gain_first)
        return (grad_total, None)
    grad_total = jnp.zeros((3, BEADS + pad_extra), jnp.float32)
    grad_total, _ = lax.scan(band_step, grad_total, jnp.arange(BLOCKS, dtype=jnp.int32))
    grad_total = grad_total[:, :BEADS]

    def inter_step(grad_total, list_entry):
        block_pair, tile_count = list_entry
        first_start = (block_pair[0] * BLOCK).astype(jnp.int32)
        second_start = (block_pair[1] * BLOCK).astype(jnp.int32)
        first_points = lax.dynamic_slice_in_dim(positions, first_start, BLOCK, 1)
        second_points = lax.dynamic_slice_in_dim(positions, second_start, BLOCK, 1)
        left_chrom = lax.dynamic_slice_in_dim(labels, first_start, BLOCK, 0)
        right_chrom = lax.dynamic_slice_in_dim(labels, second_start, BLOCK, 0)
        pair_mask = (left_chrom[:, None] != right_chrom[None, :]).astype(jnp.float32)
        gain_first, gain_second = pair_terms(first_points, second_points, pair_mask, tile_count[None], 1)
        grad_total = add_at(grad_total, first_start, gain_first)
        grad_total = add_at(grad_total, second_start, gain_second)
        return (grad_total, None)
    grad_total, _ = lax.scan(inter_step, grad_total, (pair_ids, listed))
    return grad_total

def reference(coords, chrom_lengths, band_counts, inter_pairs, inter_counts):
    chrom_ends = jnp.cumsum(chrom_lengths).astype(jnp.int32)
    labels = chromosome(jnp.arange(BEADS, dtype=jnp.int32), chrom_ends)
    results = []
    for member in range(STRUCTURES):
        positions = coords[member].reshape(3, BEADS)
        band = band_counts[member].reshape(BLOCKS, BAND_BLOCKS + 1)
        member_grad = structure_grad(positions, labels, band, inter_pairs[member], inter_counts[member])
        results.append(member_grad.reshape(3, SWEEPS, SWEEP_BEADS))
    return jnp.stack(results)
```

```python
import functools

import jax
import jax.numpy as jnp
from jax import lax
from jax.experimental import pallas as pl
from jax.experimental.pallas import tpu as pltpu
from jax.sharding import PartitionSpec as P

MESH = pl.DeviceIdType.MESH
ROWS, COLS = 16, 8
S, U, BEADS = 4, 8, 128
CAP = 64
LABELS = 48
NR, NC = COLS * U, ROWS * U
PAD = 4
BIG = 64.0
F32, BF16, I32 = jnp.float32, jnp.bfloat16, jnp.int32
ANY = pl.BlockSpec(memory_space=pl.ANY)
VMEM = pl.BlockSpec(memory_space=pltpu.VMEM)
SMEM = pl.BlockSpec(memory_space=pltpu.SMEM)
NT = (((1,), (1,)), ((), ()))


def iota(shape, axis):
    return lax.broadcasted_iota(I32, shape, axis)


def chrom_bounds(lens_ref):
    lens = jnp.broadcast_to(lens_ref[...], (LABELS, lens_ref.shape[1]))
    sub, lane = iota(lens.shape, 0), iota(lens.shape, 1)
    ends = jnp.sum(jnp.where(lane <= sub, lens, 0), axis=1, keepdims=True)
    starts = jnp.sum(jnp.where(lane < sub, lens, 0), axis=1, keepdims=True)
    return starts, ends


def list_kernel(me_ref, lens_ref, first_ref, second_ref, count_ref, out_ref):
    row, col = me_ref[0], me_ref[1]
    first, second, counts = first_ref[...], second_ref[...], count_ref[...]
    mine = (((first & 127) >> 3) == row) & ((second & 7) == col)
    mask = mine.astype(F32).astype(BF16)
    a, b = iota((128, 128), 0), iota((128, 128), 1)
    upper = (a <= b).astype(F32).astype(BF16)
    within = jnp.dot(mask, upper, preferred_element_type=F32)
    total = jnp.dot(mask, jnp.ones((128, 128), BF16), preferred_element_type=F32)
    lower = ((b < a) & ((a >> 5) == (b >> 5))).astype(F32).astype(BF16)
    offset = jnp.dot(lower, total.astype(BF16), preferred_element_type=F32)
    place = jnp.where(mine, (offset + within).astype(I32) - 1, -1)
    row_at = (first & 7) * U + (first >> 7)
    values = [row_at, second >> 3, counts, mine.astype(I32)]
    values = [v.astype(F32) for v in values]
    slots = iota((CAP, 128), 0)
    for s in range(S):
        acc = jnp.zeros((16, CAP), F32)
        for t in range(32):
            e = s * 32 + t
            hot = (place[e:e + 1] == slots).astype(F32).astype(BF16)
            rows = [v[e:e + 1] for v in values] + [jnp.zeros((12, 128), F32)]
            rows = jnp.concatenate(rows, axis=0).astype(BF16)
            acc = acc + lax.dot_general(rows, hot, NT, preferred_element_type=F32)
        out_ref[s * 8:s * 8 + 8, 0:CAP] = acc[0:8].astype(I32)
        amount = jnp.sum(acc[3:4], axis=1, keepdims=True).astype(I32)
        out_ref[s * 8 + 4:s * 8 + 5, :] = jnp.broadcast_to(amount, (1, 128))
    starts, ends = chrom_bounds(lens_ref)
    lane = iota((1, 128), 1)
    block = (lane & 7) * 128 + row * 8 + ((lane >> 3) & 7)
    last = jnp.broadcast_to(block * 128 + 127, (LABELS, 128))
    stop = jnp.min(jnp.where(ends > last, ends, 1 << 20), axis=0, keepdims=True)
    gap = (col - ((lane >> 3) & 7)) & 7
    far = jnp.minimum(jnp.minimum((stop - 1) >> 7, block + 31), 1023)
    width = ((far - block - gap) >> 3) + 1
    out_ref[32:40, :] = jnp.broadcast_to(jnp.clip(width, 0, 4), (8, 128))


def gather_kernel(coords, counts, rows, cols, tallies, send, recv):
    r, c = lax.axis_index("row"), lax.axis_index("col")
    barrier = pltpu.get_barrier_semaphore()
    for d in range(1, COLS):
        pl.semaphore_signal(barrier, 1, device_id=(r, lax.rem(c + d, COLS)), device_id_type=MESH)
    for d in range(1, ROWS):
        pl.semaphore_signal(barrier, 1, device_id=(lax.rem(r + d, ROWS), c), device_id_type=MESH)
    pl.semaphore_wait(barrier, COLS + ROWS - 2)
    copies = []
    for d in range(1, ROWS):
        copies.append(pltpu.make_async_remote_copy(
            coords, cols.at[r], send.at[d], recv.at[d],
            device_id=(lax.rem(r + d, ROWS), c), device_id_type=MESH))
    for d in range(1, COLS):
        peer = (r, lax.rem(c + d, COLS))
        copies.append(pltpu.make_async_remote_copy(
            coords, rows.at[c], send.at[ROWS + d], recv.at[ROWS + d],
            device_id=peer, device_id_type=MESH))
        copies.append(pltpu.make_async_remote_copy(
            counts, tallies.at[c], send.at[ROWS + COLS + d], recv.at[ROWS + COLS + d],
            device_id=peer, device_id_type=MESH))
    for copy in copies:
        copy.start()
    for copy in copies:
        copy.wait()


def scatter_kernel(rows, cols, out, land, own, send, recv, local):
    r, c = lax.axis_index("row"), lax.axis_index("col")
    first = pltpu.make_async_copy(rows.at[c], own.at[0], local.at[0])
    second = pltpu.make_async_copy(cols.at[r], own.at[1], local.at[1])
    first.start()
    second.start()
    barrier = pltpu.get_barrier_semaphore()
    for d in range(1, COLS):
        pl.semaphore_signal(barrier, 1, device_id=(r, lax.rem(c + d, COLS)), device_id_type=MESH)
    for d in range(1, ROWS):
        pl.semaphore_signal(barrier, 1, device_id=(lax.rem(r + d, ROWS), c), device_id_type=MESH)
    pl.semaphore_wait(barrier, COLS + ROWS - 2)
    copies = []
    for d in range(1, ROWS):
        to = lax.rem(r + d, ROWS)
        copies.append(pltpu.make_async_remote_copy(
            cols.at[to], land.at[d - 1], send.at[d], recv.at[d],
            device_id=(to, c), device_id_type=MESH))
    for d in range(1, COLS):
        to = lax.rem(c + d, COLS)
        copies.append(pltpu.make_async_remote_copy(
            rows.at[to], land.at[ROWS - 2 + d], send.at[ROWS + d], recv.at[ROWS + d],
            device_id=(r, to), device_id_type=MESH))
    for copy in copies:
        copy.start()
    first.wait()
    second.wait()
    for copy in copies:
        copy.wait()
    for s in range(S):
        total = own[0, s] + own[1, s]
        for d in range(ROWS + COLS - 2):
            total = total + land[d, s]
        out[s] = total


def split3(x):
    a = x.astype(BF16).astype(F32)
    b = (x - a).astype(BF16).astype(F32)
    return a, b, (x - a) - b


def points_of(x, y, z):
    c = 0.75 - 0.25 * (x * x + y * y + z * z)
    return split3(x), split3(y), split3(z), split3(c)


def pair_kernel(me_ref, list_ref, tally_ref, count_ref, lens_ref, coords_ref, rows_ref, cols_ref,
                prow_ref, pcol_ref,
                tile_ref, left_ref, lrow_ref, right_ref, same_ref, differ_ref,
                sum_ref, num_ref, gcol_ref, grow_ref, lsum_ref, lnum_ref, lgcol_ref, lgrow_ref,
                arow_ref, acol_ref):
    r, c = me_ref[0], me_ref[1]
    rows_ref[c] = coords_ref[...]
    cols_ref[r] = coords_ref[...]
    starts, ends = chrom_bounds(lens_ref)
    starts = jnp.broadcast_to(starts, (LABELS, BEADS))
    ends = jnp.broadcast_to(ends, (LABELS, BEADS))
    lanes = iota((LABELS, BEADS), 1)
    eye = (iota((128, 128), 0) == iota((128, 128), 1)).astype(F32).astype(BF16)
    one = jnp.ones((8, 128), F32)
    nil = jnp.zeros((8, 128), F32)
    for v in range(2):
        for u in range(U):
            for q in range(3):
                tile_ref[v, u, 8 * q:8 * q + 8] = nil

    def hot_of(block):
        bead = lanes + block * BEADS
        return (bead >= starts) & (bead < ends)

    @pl.loop(0, COLS)
    def _(k):
        for s in range(S):
            x, y, z = rows_ref[k, s, 0], rows_ref[k, s, 1], rows_ref[k, s, 2]
            parts = points_of(x, y, z)
            v = s % 2
            for q in range(3):
                for w in range(4):
                    value = parts[w][q]
                    tile_ref[v, :, 8 * q + w, :] = 0.5 * value if w < 3 else value
            tile_ref[v, :, 4, :] = one
            for u in range(U):
                tiles = [tile_ref[v, u, 8 * q:8 * q + 8] for q in range(3)]
                hot = jnp.where(hot_of(u * 128 + r * 8 + k), 1.0, 0.0)
                full = jnp.concatenate(
                    [tiles[i] for i in (0, 0, 1, 0, 2, 1)] + [hot, jnp.zeros((32, 128), F32)], axis=0)
                flipped = lax.dot_general(eye, full.astype(BF16), NT, preferred_element_type=F32)
                left_ref[s * NR + k * U + u] = flipped.astype(BF16)
                lrow_ref[s * NR + k * U + u] = jnp.concatenate(tiles[:2], axis=0).astype(BF16)

    tile_ref[0, :, 3, :] = one
    tile_ref[1, :, 3, :] = one
    for v in range(2):
        tile_ref[v, :, 11, :] = nil
        tile_ref[v, :, 19, :] = nil

    @pl.loop(0, ROWS)
    def _(k):
        for s in range(S):
            x, y, z = cols_ref[k, s, 0], cols_ref[k, s, 1], cols_ref[k, s, 2]
            parts = points_of(x, y, z)
            v = s % 2
            for q in range(3):
                for w in range(4):
                    tile_ref[v, :, 8 * q + (w if w < 3 else 4), :] = parts[w][q]
            for u in range(U):
                tiles = [tile_ref[v, u, 8 * q:8 * q + 8] for q in range(3)]
                full = jnp.concatenate([tiles[i] for i in (0, 1, 0, 2, 0, 1)], axis=0)
                right_ref[s, u * ROWS + k] = full.astype(BF16)
        for u in range(U):
            hot = hot_of((u * ROWS + k) * 8 + c)
            same_ref[u * ROWS + k] = jnp.where(hot, 0.0, -BIG).astype(BF16)
            differ_ref[u * ROWS + k] = jnp.where(hot, -BIG, 0.0).astype(BF16)
    for p in range(PAD):
        same_ref[NC + p] = jnp.full((LABELS, BEADS), -BIG, BF16)
        for s in range(S):
            right_ref[s, NC + p] = jnp.zeros((LABELS, BEADS), BF16)

    @pl.loop(0, NC + PAD)
    def _(i):
        for s in range(S):
            acol_ref[s, i] = nil

    @pl.loop(0, NR)
    def _(i):
        for s in range(S):
            arow_ref[s, i] = nil

    triangle = iota((128, 128), 0) < iota((128, 128), 1)

    def chances(left, blocks, labels, diagonal=False):
        right = [jnp.concatenate([b, l], axis=0) for b, l in zip(blocks, labels)]
        right = jnp.concatenate(right, axis=1)
        z = jnp.dot(left[:, :2 * LABELS], right, preferred_element_type=F32)
        t = jnp.tanh(z)
        if diagonal:
            t = jnp.concatenate([jnp.where(triangle, t[:, :128], -1.0), t[:, 128:]], axis=1)
        return jnp.sum(t, axis=0, keepdims=True), (1.0 - t * t).astype(BF16)

    def pull(g, near, blocks):
        o = jnp.dot(near, g, preferred_element_type=F32)
        rows = []
        for j, b in enumerate(blocks):
            p = lax.dot_general(b[0:16], g[:, j * 128:j * 128 + 128], NT, preferred_element_type=F32)
            rows.append(p[0:8] + p[8:16])
        return o[0:8] + o[8:16], jnp.concatenate(rows, axis=1)

    def window(k, u, width, diagonal):
        at = k * U + u
        start = u * ROWS + r + jnp.where(k > c, 1, 0)
        gap = (c - k) & 7
        labels = [same_ref[start + m] for m in range(width)]
        held = None
        for s in range(S + 1):
            if s < S:
                blocks = [right_ref[s, start + m] for m in range(width)]
                sums, g = chances(left_ref[s * NR + at], blocks, labels, diagonal)
            if held is not None:
                q = at * S + s - 1
                o, p = pull(held[1], lrow_ref[(s - 1) * NR + at], held[2])
                gcol_ref[q, :, 0:width * 128] = o
                grow_ref[q, :, 0:width * 128] = p
                for m in range(width):
                    sum_ref[m, pl.ds(q, 1), :] = held[0][:, m * 128:m * 128 + 128]
                if width < 4:
                    gcol_ref[q, :, width * 128:] = jnp.zeros((8, 512 - width * 128), F32)
                    grow_ref[q, :, width * 128:] = jnp.zeros((8, 512 - width * 128), F32)
                    for m in range(width, 4):
                        sum_ref[m, pl.ds(q, 1), :] = jnp.zeros((1, 128), F32)
                        num_ref[m, pl.ds(q, 1), :] = jnp.zeros((1, 128), F32)
            held = (sums, g, blocks)
        for s in range(S):
            q = at * S + s
            for m in range(width):
                line, lane = s * 2 + (u >> 2), (u & 3) * 32 + gap + 8 * m
                n = count_ref[line, lane] if diagonal else tally_ref[k, line, lane]
                num_ref[m, pl.ds(q, 1), :] = jnp.full((1, 128), n, I32).astype(F32)

    @pl.loop(0, U)
    def _(u):
        window(c, u, 4, True)

    @pl.loop(0, U)
    def _(u):
        @pl.loop(1, COLS)
        def _(d):
            k = (c + d) & 7
            width = list_ref[32, k * U + u]

            @pl.when(width > 2)
            def _():
                window(k, u, 4, False)

            @pl.when((width > 0) & (width <= 2))
            def _():
                window(k, u, 2, False)

    most = jnp.maximum(jnp.maximum(list_ref[4, 0], list_ref[12, 0]),
                       jnp.maximum(list_ref[20, 0], list_ref[28, 0]))

    @pl.loop(0, (most + 1) >> 1)
    def _(half):
        held = None
        for turn in range(2 * S + 1):
            if turn < 2 * S:
                s, slot = turn % S, half * 2 + turn // S
                i, j = list_ref[s * 8, slot], list_ref[s * 8 + 1, slot]
                block = right_ref[s, j]
                sums, g = chances(left_ref[s * NR + i], [block], [differ_ref[j]])
                lnum_ref[0, pl.ds(s * CAP + slot, 1), :] = jnp.full(
                    (1, 128), list_ref[s * 8 + 2, slot], I32).astype(F32)
            if held is not None:
                o, p = pull(held[1], lrow_ref[held[3]], [held[2]])
                lgcol_ref[held[4]] = o
                lgrow_ref[held[4]] = p
                lsum_ref[0, pl.ds(held[4], 1), :] = held[0]
            held = (sums, g, block, s * NR + i, s * CAP + slot)

    def weights(sums_ref, nums_ref, lo, width):
        for m in range(width):
            at = (m, pl.ds(lo, 8), slice(None))
            total = jnp.sum(sums_ref[at], axis=1, keepdims=True)
            expect = 0.5 + (0.5 * (16384.0 + total)) / 128.0
            nums_ref[at] = 1.0 - nums_ref[at] / jnp.broadcast_to(expect, (8, 128))

    @pl.loop(0, NR * S // 8)
    def _(i):
        weights(sum_ref, num_ref, pl.multiple_of(i * 8, 8), 4)

    @pl.loop(0, CAP * S // 8)
    def _(i):
        weights(lsum_ref, lnum_ref, pl.multiple_of(i * 8, 8), 1)

    @pl.loop(0, U)
    def _(u):
        @pl.loop(0, COLS)
        def _(k):
            at = k * U + u
            start = u * ROWS + r + jnp.where(k > c, 1, 0)

            @pl.when((k == c) | (list_ref[32, at] > 0))
            def _():
                for s in range(S):
                    q = at * S + s
                    total = nil
                    for m in range(4):
                        lane = slice(m * 128, m * 128 + 128)
                        w = jnp.broadcast_to(num_ref[m, pl.ds(q, 1), :], (8, 128))
                        total = total + w * grow_ref[q, :, lane]
                        acol_ref[s, start + m] += w * gcol_ref[q, :, lane]
                    arow_ref[s, at] = total

    for s in range(S):
        @pl.loop(0, list_ref[s * 8 + 4, 0])
        def _(slot):
            i, j = list_ref[s * 8, slot], list_ref[s * 8 + 1, slot]
            q = s * CAP + slot
            w = jnp.broadcast_to(lnum_ref[0, pl.ds(q, 1), :], (8, 128))
            arow_ref[s, i] += w * lgrow_ref[q]
            acol_ref[s, j] += w * lgcol_ref[q]

    @pl.loop(0, COLS)
    def _(k):
        for s in range(S):
            here = pl.ds(k * U, U)
            mass = arow_ref[s, here, 3, :]
            for w in range(3):
                pulled = rows_ref[k, s, w] * mass - arow_ref[s, here, w, :]
                prow_ref[k, s, w] = pulled * (-1.0 / 512.0)

    @pl.loop(0, ROWS)
    def _(k):
        for s in range(S):
            here = pl.ds(k, U, stride=ROWS)
            mass = acol_ref[s, here, 4, :]
            for w in range(3):
                pulled = cols_ref[k, s, w] * mass - 2.0 * acol_ref[s, here, w, :]
                pcol_ref[k, s, w] = pulled * (-1.0 / 512.0)


def on_device(coords, chrom_lengths, band_counts, inter_pairs, inter_counts):
    shard = coords.shape
    me = jnp.stack([lax.axis_index("row"), lax.axis_index("col")]).astype(I32)
    lens = chrom_lengths.reshape(1, -1)
    counts = band_counts.reshape(8, 128)
    listing = pl.pallas_call(
        list_kernel,
        out_shape=jax.ShapeDtypeStruct((40, 128), I32),
        in_specs=[SMEM] + [VMEM] * 4, out_specs=VMEM, name="listing",
    )(me, lens, inter_pairs[:, :, 0].reshape(128, 128), inter_pairs[:, :, 1].reshape(128, 128),
      inter_counts.reshape(128, 128))
    rows, cols, tallies = pl.pallas_call(
        gather_kernel,
        out_shape=[jax.ShapeDtypeStruct((COLS,) + shard, F32), jax.ShapeDtypeStruct((ROWS,) + shard, F32),
                   jax.ShapeDtypeStruct((COLS, 8, 128), I32)],
        in_specs=[ANY] * 2, out_specs=[ANY] * 3,
        scratch_shapes=[pltpu.SemaphoreType.DMA((ROWS + 2 * COLS,))] * 2,
        compiler_params=pltpu.CompilerParams(collective_id=0, has_side_effects=True),
        name="gather",
    )(coords, counts)
    prow, pcol = pl.pallas_call(
        pair_kernel,
        out_shape=[jax.ShapeDtypeStruct((COLS,) + shard, F32), jax.ShapeDtypeStruct((ROWS,) + shard, F32)],
        in_specs=[SMEM] * 4 + [VMEM] * 4, out_specs=[VMEM] * 2,
        scratch_shapes=[
            pltpu.VMEM((2, U, 24, BEADS), F32),
            pltpu.VMEM((S * NR, BEADS, 128), BF16),
            pltpu.VMEM((S * NR, 16, BEADS), BF16),
            pltpu.VMEM((S, NC + PAD, LABELS, BEADS), BF16),
            pltpu.VMEM((NC + PAD, LABELS, BEADS), BF16),
            pltpu.VMEM((NC, LABELS, BEADS), BF16),
            pltpu.VMEM((4, NR * S, 128), F32),
            pltpu.VMEM((4, NR * S, 128), F32),
            pltpu.VMEM((NR * S, 8, 512), F32),
            pltpu.VMEM((NR * S, 8, 512), F32),
            pltpu.VMEM((1, CAP * S, 128), F32),
            pltpu.VMEM((1, CAP * S, 128), F32),
            pltpu.VMEM((CAP * S, 8, 128), F32),
            pltpu.VMEM((CAP * S, 8, 128), F32),
            pltpu.VMEM((S, NR, 8, BEADS), F32),
            pltpu.VMEM((S, NC + PAD, 8, BEADS), F32),
        ],
        compiler_params=pltpu.CompilerParams(vmem_limit_bytes=60 << 20),
        name="pairs",
    )(me, listing, tallies, counts, lens, coords, rows, cols)
    return pl.pallas_call(
        scatter_kernel,
        out_shape=jax.ShapeDtypeStruct(shard, F32),
        in_specs=[ANY] * 2, out_specs=VMEM,
        scratch_shapes=[
            pltpu.VMEM((ROWS + COLS - 2,) + shard, F32),
            pltpu.VMEM((2,) + shard, F32),
            pltpu.SemaphoreType.DMA((ROWS + COLS,)),
            pltpu.SemaphoreType.DMA((ROWS + COLS,)),
            pltpu.SemaphoreType.DMA((2,)),
        ],
        compiler_params=pltpu.CompilerParams(collective_id=1, has_side_effects=True),
        name="scatter",
    )(prow, pcol)


def solution(mesh):
    placed = (P(None, None, None, ("row", "col")), P(), P(None, None, ("row", "col"), None), P(), P())
    return jax.shard_map(on_device, mesh=mesh, in_specs=placed,
                         out_specs=P(None, None, None, ("row", "col")), check_vma=False)
```

```python
import functools

import jax
import jax.numpy as jnp
from jax import lax
from jax.experimental import pallas as pl
from jax.experimental.pallas import tpu as pltpu
from jax.sharding import PartitionSpec as P

MESH = pl.DeviceIdType.MESH
ROWS, COLS = 16, 8
S, U, BEADS = 4, 8, 128
CAP = 64
LABELS = 48
NR, NC = COLS * U, ROWS * U
PAD = 4
WIDE = 4
BIG = 64.0
F32, BF16, I32 = jnp.float32, jnp.bfloat16, jnp.int32
ANY = pl.BlockSpec(memory_space=pl.ANY)
VMEM = pl.BlockSpec(memory_space=pltpu.VMEM)
SMEM = pl.BlockSpec(memory_space=pltpu.SMEM)
NT = (((1,), (1,)), ((), ()))


def iota(shape, axis):
    return lax.broadcasted_iota(I32, shape, axis)


def chrom_bounds(lens_ref):
    lens = jnp.broadcast_to(lens_ref[...], (LABELS, lens_ref.shape[1]))
    sub, lane = iota(lens.shape, 0), iota(lens.shape, 1)
    ends = jnp.sum(jnp.where(lane <= sub, lens, 0), axis=1, keepdims=True)
    starts = jnp.sum(jnp.where(lane < sub, lens, 0), axis=1, keepdims=True)
    return starts, ends


def list_kernel(me_ref, lens_ref, first_ref, second_ref, count_ref, out_ref):
    row, col = me_ref[0], me_ref[1]
    first, second, counts = first_ref[...], second_ref[...], count_ref[...]
    mine = (((first & 127) >> 3) == row) & ((second & 7) == col)
    mask = mine.astype(F32).astype(BF16)
    a, b = iota((128, 128), 0), iota((128, 128), 1)
    upper = (a <= b).astype(F32).astype(BF16)
    within = jnp.dot(mask, upper, preferred_element_type=F32)
    total = jnp.dot(mask, jnp.ones((128, 128), BF16), preferred_element_type=F32)
    lower = ((b < a) & ((a >> 5) == (b >> 5))).astype(F32).astype(BF16)
    offset = jnp.dot(lower, total.astype(BF16), preferred_element_type=F32)
    place = jnp.where(mine, (offset + within).astype(I32) - 1, -1)
    row_at = (first & 7) * U + (first >> 7)
    values = [row_at, second >> 3, counts, mine.astype(I32)]
    values = [v.astype(F32) for v in values]
    slots = iota((CAP, 128), 0)
    for s in range(S):
        acc = jnp.zeros((16, CAP), F32)
        for t in range(32):
            e = s * 32 + t
            hot = (place[e:e + 1] == slots).astype(F32).astype(BF16)
            rows = [v[e:e + 1] for v in values] + [jnp.zeros((12, 128), F32)]
            rows = jnp.concatenate(rows, axis=0).astype(BF16)
            acc = acc + lax.dot_general(rows, hot, NT, preferred_element_type=F32)
        spare = jnp.where(iota((8, CAP), 0) == 1, NC * (1.0 - acc[3:4]), 0.0)
        out_ref[s * 8:s * 8 + 8, 0:CAP] = (acc[0:8] + spare).astype(I32)
        amount = jnp.sum(acc[3:4], axis=1, keepdims=True).astype(I32)
        out_ref[s * 8 + 4:s * 8 + 5, :] = jnp.broadcast_to(amount, (1, 128))
    starts, ends = chrom_bounds(lens_ref)
    lane = iota((1, 128), 1)
    block = (lane & 7) * 128 + row * 8 + ((lane >> 3) & 7)
    last = jnp.broadcast_to(block * 128 + 127, (LABELS, 128))
    stop = jnp.min(jnp.where(ends > last, ends, 1 << 20), axis=0, keepdims=True)
    gap = (col - ((lane >> 3) & 7)) & 7
    far = jnp.minimum(jnp.minimum((stop - 1) >> 7, block + 31), 1023)
    width = ((far - block - gap) >> 3) + 1
    out_ref[32:40, :] = jnp.broadcast_to(jnp.clip(width, 0, 4), (8, 128))


def gather_kernel(coords, counts, rows, cols, tallies, send, recv, local):
    r, c = lax.axis_index("row"), lax.axis_index("col")
    kept = [pltpu.make_async_copy(coords, rows.at[c], local.at[0]),
            pltpu.make_async_copy(coords, cols.at[r], local.at[1]),
            pltpu.make_async_copy(counts, tallies.at[c], local.at[2])]
    for copy in kept:
        copy.start()
    barrier = pltpu.get_barrier_semaphore()
    for d in range(1, COLS):
        pl.semaphore_signal(barrier, 1, device_id=(r, lax.rem(c + d, COLS)), device_id_type=MESH)
    for d in range(1, ROWS):
        pl.semaphore_signal(barrier, 1, device_id=(lax.rem(r + d, ROWS), c), device_id_type=MESH)
    pl.semaphore_wait(barrier, COLS + ROWS - 2)
    copies = []
    for d in range(1, ROWS):
        copies.append(pltpu.make_async_remote_copy(
            coords, cols.at[r], send.at[d], recv.at[d],
            device_id=(lax.rem(r + d, ROWS), c), device_id_type=MESH))
    for d in range(1, COLS):
        peer = (r, lax.rem(c + d, COLS))
        copies.append(pltpu.make_async_remote_copy(
            coords, rows.at[c], send.at[ROWS + d], recv.at[ROWS + d],
            device_id=peer, device_id_type=MESH))
        copies.append(pltpu.make_async_remote_copy(
            counts, tallies.at[c], send.at[ROWS + COLS + d], recv.at[ROWS + COLS + d],
            device_id=peer, device_id_type=MESH))
    for copy in copies:
        copy.start()
    for copy in kept + copies:
        copy.wait()


def scatter_kernel(rows, cols, out, land, own, send, recv, local):
    r, c = lax.axis_index("row"), lax.axis_index("col")
    first = pltpu.make_async_copy(rows.at[c], own.at[0], local.at[0])
    second = pltpu.make_async_copy(cols.at[r], own.at[1], local.at[1])
    first.start()
    second.start()
    barrier = pltpu.get_barrier_semaphore()
    for d in range(1, COLS):
        pl.semaphore_signal(barrier, 1, device_id=(r, lax.rem(c + d, COLS)), device_id_type=MESH)
    for d in range(1, ROWS):
        pl.semaphore_signal(barrier, 1, device_id=(lax.rem(r + d, ROWS), c), device_id_type=MESH)
    pl.semaphore_wait(barrier, COLS + ROWS - 2)
    copies = []
    for d in range(1, ROWS):
        to = lax.rem(r + d, ROWS)
        copies.append(pltpu.make_async_remote_copy(
            cols.at[to], land.at[d - 1], send.at[d], recv.at[d],
            device_id=(to, c), device_id_type=MESH))
    for d in range(1, COLS):
        to = lax.rem(c + d, COLS)
        copies.append(pltpu.make_async_remote_copy(
            rows.at[to], land.at[ROWS - 2 + d], send.at[ROWS + d], recv.at[ROWS + d],
            device_id=(r, to), device_id_type=MESH))
    for copy in copies:
        copy.start()
    first.wait()
    second.wait()
    for copy in copies:
        copy.wait()
    for s in range(S):
        total = own[0, s] + own[1, s]
        for d in range(ROWS + COLS - 2):
            total = total + land[d, s]
        out[s] = total


def split3(x):
    a = x.astype(BF16).astype(F32)
    b = (x - a).astype(BF16).astype(F32)
    return a, b, (x - a) - b


def points_of(x, y, z):
    c = 0.75 - 0.25 * (x * x + y * y + z * z)
    return split3(x), split3(y), split3(z), split3(c)


def pair_kernel(me_ref, list_ref, tally_ref, lens_ref, rows_ref, cols_ref,
                prow_ref, pcol_ref,
                unit_ref, tile_ref, left_ref, lrow_ref, right_ref, same_ref, differ_ref,
                sum_ref, num_ref, gcol_ref, grow_ref, lsum_ref, lnum_ref, lgcol_ref, lgrow_ref,
                arow_ref, acol_ref):
    r, c = me_ref[0], me_ref[1]
    starts, ends = chrom_bounds(lens_ref)
    starts = jnp.broadcast_to(starts, (LABELS, BEADS))
    ends = jnp.broadcast_to(ends, (LABELS, BEADS))
    lanes = iota((LABELS, BEADS), 1)
    eye = (iota((128, 128), 0) == iota((128, 128), 1)).astype(F32).astype(BF16)
    one = jnp.ones((8, 128), F32)
    nil = jnp.zeros((8, 128), F32)
    for v in range(S):
        for u in range(U):
            for q in range(3):
                tile_ref[v, u, 8 * q:8 * q + 8] = nil

    def hot_of(block):
        bead = lanes + block * BEADS
        return (bead >= starts) & (bead < ends)

    for v in range(S):
        tile_ref[v, :, 4, :] = one

    @pl.loop(0, COLS)
    def _(k):
        for s in range(S):
            x, y, z = rows_ref[k, s, 0], rows_ref[k, s, 1], rows_ref[k, s, 2]
            parts = points_of(x, y, z)
            for q in range(3):
                for w in range(4):
                    value = parts[w][q]
                    tile_ref[s, :, 8 * q + w, :] = 0.5 * value if w < 3 else value
        for u in range(0, U, 2):
            hots = [jnp.where(hot_of((u + i) * 128 + r * 8 + k), 1.0, 0.0).astype(BF16) for i in range(2)]
            for s in range(S):
                fulls = []
                for i in range(2):
                    tiles = [tile_ref[s, u + i, 8 * q:8 * q + 8] for q in range(3)]
                    full = jnp.concatenate([tiles[j] for j in (0, 0, 1, 0, 2, 1)], axis=0).astype(BF16)
                    fulls += [full, hots[i], jnp.zeros((32, 128), BF16)]
                    lrow_ref[s * NR + k * U + u + i] = jnp.concatenate(tiles[:2], axis=0).astype(BF16)
                flipped = lax.dot_general(eye, jnp.concatenate(fulls, axis=0), NT, preferred_element_type=F32)
                for i in range(2):
                    left_ref[s * NR + k * U + u + i] = flipped[:, i * 128:i * 128 + 128].astype(BF16)

    for v in range(S):
        tile_ref[v, :, 3, :] = one
        tile_ref[v, :, 11, :] = nil
        tile_ref[v, :, 19, :] = nil

    @pl.loop(0, ROWS)
    def _(k):
        for s in range(S):
            x, y, z = cols_ref[k, s, 0], cols_ref[k, s, 1], cols_ref[k, s, 2]
            parts = points_of(x, y, z)
            for q in range(3):
                for w in range(4):
                    tile_ref[s, :, 8 * q + (w if w < 3 else 4), :] = parts[w][q]
        for s in range(S):
            for u in range(U):
                tiles = [tile_ref[s, u, 8 * q:8 * q + 8] for q in range(3)]
                full = jnp.concatenate([tiles[i] for i in (0, 1, 0, 2, 0, 1)], axis=0)
                right_ref[s, u * ROWS + k] = full.astype(BF16)
        for u in range(U):
            hot = hot_of((u * ROWS + k) * 8 + c)
            same_ref[u * ROWS + k] = jnp.where(hot, 0.0, -BIG).astype(BF16)
            differ_ref[u * ROWS + k] = jnp.where(hot, -BIG, 0.0).astype(BF16)
    for p in range(PAD):
        same_ref[NC + p] = jnp.full((LABELS, BEADS), -BIG, BF16)
        for s in range(S):
            right_ref[s, NC + p] = jnp.zeros((LABELS, BEADS), BF16)
    differ_ref[NC] = jnp.full((LABELS, BEADS), -BIG, BF16)

    @pl.loop(0, (NC + PAD) // 4)
    def _(i):
        for s in range(S):
            for j in range(4):
                acol_ref[s, i * 4 + j] = nil

    @pl.loop(0, NR // 4)
    def _(i):
        for s in range(S):
            for j in range(4):
                arow_ref[s, i * 4 + j] = nil

    def collect(i, filled):
        k = i >> 3
        width = list_ref[32, i]
        unit_ref[filled] = i * 2
        filled = filled + jnp.where((width > 0) & (k != c), 1, 0)
        unit_ref[filled] = i * 2 + 1
        return filled + jnp.where(width > 2, 1, 0)

    units = lax.fori_loop(0, NR, collect, jnp.int32(0))
    unit_ref[units] = unit_ref[jnp.maximum(units - 1, 0)]
    triangle = iota((128, 128), 0) < iota((128, 128), 1)
    empty = jnp.zeros((16, 128), BF16)

    def chances(left, blocks, labels, diagonal=False):
        right = [jnp.concatenate([b, l], axis=0) for b, l in zip(blocks, labels)]
        right = jnp.concatenate(right, axis=1)
        return jnp.dot(left[:, :2 * LABELS], right, preferred_element_type=F32)

    def finish(z, diagonal=False):
        t = jnp.tanh(z)
        if diagonal:
            t = jnp.concatenate([jnp.where(triangle, t[:, :128], -1.0), t[:, 128:]], axis=1)
        return jnp.sum(t, axis=0, keepdims=True), (1.0 - t * t).astype(BF16)

    def pull(g, near, far):
        o = jnp.dot(near, g, preferred_element_type=F32)
        spread = jnp.concatenate([jnp.concatenate([far[0], empty], axis=1),
                                  jnp.concatenate([empty, far[1]], axis=1)], axis=0)
        p = lax.dot_general(spread, g, NT, preferred_element_type=F32)
        return o[0:8] + o[8:16], p[0:8] + p[8:16], p[16:24] + p[24:32]

    def window_pull(g, sums, at, start, out):
        o, p0, p1 = pull(g, lrow_ref[at], [right_ref[at >> 6, start + m, 0:16] for m in range(2)])
        gcol_ref[out] = o
        grow_ref[out, :, 0:128] = p0
        grow_ref[out, :, 128:256] = p1
        for m in range(2):
            sum_ref[m, pl.ds(out, 1), :] = sums[:, m * 128:m * 128 + 128]

    def locate(unit):
        at = unit >> 1
        k, u = at >> 3, at & 7
        start = u * ROWS + r + jnp.where(k > c, 1, 0) + 2 * (unit & 1)
        gap = ((c - k) & 7) + 16 * (unit & 1)
        return at, start, k, u >> 2, (u & 3) * 32 + gap

    def run(unit_at, count, diagonal):
        def drain(held):
            for entry in held:
                window_pull(*entry)

        def body(it, held):
            for q in range(2):
                unit = unit_at(it * 2 + q)
                here, begin, k, line, lane = locate(unit)
                labels = [same_ref[begin + m] for m in range(2)]
                for s0 in range(0, S, WIDE):
                    group = range(s0, s0 + WIDE)
                    zs = [chances(left_ref[s * NR + here], [right_ref[s, begin + m] for m in range(2)], labels)
                          for s in group]
                    drain(held)
                    done = [finish(z, diagonal) for z in zs]
                    held = [(done[i][1], done[i][0], s * NR + here, begin, unit * S + s)
                            for i, s in enumerate(group)]
                for s in range(S):
                    for m in range(2):
                        n = tally_ref[k, s * 2 + line, lane + 8 * m]
                        num_ref[m, pl.ds(unit * S + s, 1), :] = jnp.full((1, 128), n, I32).astype(F32)
            return held

        first = [(jnp.zeros((128, 256), BF16), jnp.zeros((1, 256), F32),
                  jnp.int32(0), jnp.int32(0), jnp.int32(NR * S * 2 + i)) for i in range(WIDE)]
        drain(lax.fori_loop(0, count, body, first))

    run(lambda i: (c * U + i) * 2, U // 2, True)
    run(lambda i: unit_ref[i], (units + 1) >> 1, False)

    most = jnp.maximum(jnp.maximum(list_ref[4, 0], list_ref[12, 0]),
                       jnp.maximum(list_ref[20, 0], list_ref[28, 0]))

    def listed_pull(g, sums, places):
        near = jnp.concatenate([lrow_ref[p[0]] for p in places], axis=0)
        o = jnp.dot(near, jnp.concatenate(g, axis=1), preferred_element_type=F32)
        far = jnp.concatenate([right_ref[p[0] >> 6, p[1], 0:16] for p in places], axis=0)
        w = lax.dot_general(far, jnp.concatenate(g, axis=0), NT, preferred_element_type=F32)
        for m, p in enumerate(places):
            lane = slice(m * 128, m * 128 + 128)
            lgcol_ref[p[2]] = o[m * 16:m * 16 + 8, lane] + o[m * 16 + 8:m * 16 + 16, lane]
            lgrow_ref[p[2]] = w[m * 16:m * 16 + 8, lane] + w[m * 16 + 8:m * 16 + 16, lane]
            lsum_ref[0, pl.ds(p[2], 1), :] = sums[m]

    def listed_body(it, carry):
        g, sums, places = carry
        for turn in range(2):
            slot = it * 2 + turn
            for s0 in range(0, S, 2):
                zs, now = [], []
                for s in (s0, s0 + 1):
                    i, j = list_ref[s * 8, slot], list_ref[s * 8 + 1, slot]
                    zs.append(chances(left_ref[s * NR + i], [right_ref[s, j]], [differ_ref[j]]))
                    now.append((s * NR + i, j, s * CAP + slot))
                    lnum_ref[0, pl.ds(s * CAP + slot, 1), :] = jnp.full(
                        (1, 128), list_ref[s * 8 + 2, slot], I32).astype(F32)
                listed_pull(g, sums, places)
                done = [finish(z) for z in zs]
                sums, g, places = [d[0] for d in done], [d[1] for d in done], now
        return g, sums, places

    idle = (jnp.int32(0), jnp.int32(0))
    first = ([jnp.zeros((128, 128), BF16)] * 2, [jnp.zeros((1, 128), F32)] * 2,
             [idle + (jnp.int32(CAP * S),), idle + (jnp.int32(CAP * S + 1),)])
    listed_pull(*lax.fori_loop(0, (most + 1) >> 1, listed_body, first))

    def weights(sums_ref, nums_ref, lo, width):
        for m in range(width):
            at = (m, pl.ds(lo, 8), slice(None))
            total = jnp.sum(sums_ref[at], axis=1, keepdims=True)
            expect = 0.5 + (0.5 * (16384.0 + total)) / 128.0
            nums_ref[at] = 1.0 - nums_ref[at] / jnp.broadcast_to(expect, (8, 128))

    @pl.loop(0, NR * S * 2 // 32)
    def _(i):
        for j in range(4):
            weights(sum_ref, num_ref, pl.multiple_of(i * 32 + j * 8, 8), 2)

    @pl.loop(0, CAP * S // 32)
    def _(i):
        for j in range(4):
            weights(lsum_ref, lnum_ref, pl.multiple_of(i * 32 + j * 8, 8), 1)

    def deposit(unit):
        at, start = locate(unit)[:2]
        held = []
        for s in range(S):
            out = unit * S + s
            w = [jnp.broadcast_to(num_ref[m, pl.ds(out, 1), :], (8, 128)) for m in range(2)]
            row = arow_ref[s, at] + (w[0] * grow_ref[out, :, 0:128] + w[1] * grow_ref[out, :, 128:256])
            col = [acol_ref[s, start + m] + w[m] * gcol_ref[out, :, m * 128:m * 128 + 128] for m in range(2)]
            held.append((row, col))
        for s in range(S):
            arow_ref[s, at] = held[s][0]
            for m in range(2):
                acol_ref[s, start + m] = held[s][1][m]

    @pl.loop(0, U)
    def _(u):
        deposit((c * U + u) * 2)

    @pl.loop(0, units)
    def _(i):
        deposit(unit_ref[i])

    @pl.loop(0, most)
    def _(slot):
        held = []
        for s in range(S):
            i, j, q = list_ref[s * 8, slot], list_ref[s * 8 + 1, slot], s * CAP + slot
            w = jnp.broadcast_to(lnum_ref[0, pl.ds(q, 1), :], (8, 128))
            held.append((i, j, arow_ref[s, i] + w * lgrow_ref[q], acol_ref[s, j] + w * lgcol_ref[q]))
        for s in range(S):
            i, j, row, col = held[s]
            arow_ref[s, i] = row
            acol_ref[s, j] = col

    @pl.loop(0, COLS)
    def _(k):
        for s in range(S):
            here = pl.ds(k * U, U)
            mass = arow_ref[s, here, 3, :]
            for w in range(3):
                pulled = rows_ref[k, s, w] * mass - arow_ref[s, here, w, :]
                prow_ref[k, s, w] = pulled * (-1.0 / 512.0)

    @pl.loop(0, ROWS)
    def _(k):
        for s in range(S):
            here = pl.ds(k, U, stride=ROWS)
            mass = acol_ref[s, here, 4, :]
            for w in range(3):
                pulled = cols_ref[k, s, w] * mass - 2.0 * acol_ref[s, here, w, :]
                pcol_ref[k, s, w] = pulled * (-1.0 / 512.0)


def pairs_call(me, listing, tallies, lens, rows, cols):
    shard = rows.shape[1:]
    return pl.pallas_call(
        pair_kernel,
        out_shape=[jax.ShapeDtypeStruct((COLS,) + shard, F32), jax.ShapeDtypeStruct((ROWS,) + shard, F32)],
        in_specs=[SMEM] * 3 + [VMEM] * 3, out_specs=[VMEM] * 2,
        scratch_shapes=[
            pltpu.SMEM((2 * NR + 2,), I32),
            pltpu.VMEM((S, U, 24, BEADS), F32),
            pltpu.VMEM((S * NR, BEADS, 128), BF16),
            pltpu.VMEM((S * NR, 16, BEADS), BF16),
            pltpu.VMEM((S, NC + PAD, LABELS, BEADS), BF16),
            pltpu.VMEM((NC + PAD, LABELS, BEADS), BF16),
            pltpu.VMEM((NC + 1, LABELS, BEADS), BF16),
            pltpu.VMEM((2, NR * S * 2 + 8, 128), F32),
            pltpu.VMEM((2, NR * S * 2 + 8, 128), F32),
            pltpu.VMEM((NR * S * 2 + 4, 8, 256), F32),
            pltpu.VMEM((NR * S * 2 + 4, 8, 256), F32),
            pltpu.VMEM((1, CAP * S + 8, 128), F32),
            pltpu.VMEM((1, CAP * S + 8, 128), F32),
            pltpu.VMEM((CAP * S + 2, 8, 128), F32),
            pltpu.VMEM((CAP * S + 2, 8, 128), F32),
            pltpu.VMEM((S, NR, 8, BEADS), F32),
            pltpu.VMEM((S, NC + PAD, 8, BEADS), F32),
        ],
        compiler_params=pltpu.CompilerParams(vmem_limit_bytes=60 << 20),
        name="pairs",
    )(me, listing, tallies, lens, rows, cols)


def on_device(coords, chrom_lengths, band_counts, inter_pairs, inter_counts):
    shard = coords.shape
    me = jnp.stack([lax.axis_index("row"), lax.axis_index("col")]).astype(I32)
    lens = chrom_lengths.reshape(1, -1)
    counts = band_counts.reshape(8, 128)
    listing = pl.pallas_call(
        list_kernel,
        out_shape=jax.ShapeDtypeStruct((40, 128), I32),
        in_specs=[SMEM] + [VMEM] * 4, out_specs=VMEM, name="listing",
    )(me, lens, inter_pairs[:, :, 0].reshape(128, 128), inter_pairs[:, :, 1].reshape(128, 128),
      inter_counts.reshape(128, 128))
    rows, cols, tallies = pl.pallas_call(
        gather_kernel,
        out_shape=[jax.ShapeDtypeStruct((COLS,) + shard, F32), jax.ShapeDtypeStruct((ROWS,) + shard, F32),
                   jax.ShapeDtypeStruct((COLS, 8, 128), I32)],
        in_specs=[ANY] * 2, out_specs=[ANY] * 3,
        scratch_shapes=[pltpu.SemaphoreType.DMA((ROWS + 2 * COLS,))] * 2 + [pltpu.SemaphoreType.DMA((3,))],
        compiler_params=pltpu.CompilerParams(collective_id=0, has_side_effects=True),
        name="gather",
    )(coords, counts)
    prow, pcol = pairs_call(me, listing, tallies, lens, rows, cols)
    return pl.pallas_call(
        scatter_kernel,
        out_shape=jax.ShapeDtypeStruct(shard, F32),
        in_specs=[ANY] * 2, out_specs=VMEM,
        scratch_shapes=[
            pltpu.VMEM((ROWS + COLS - 2,) + shard, F32),
            pltpu.VMEM((2,) + shard, F32),
            pltpu.SemaphoreType.DMA((ROWS + COLS,)),
            pltpu.SemaphoreType.DMA((ROWS + COLS,)),
            pltpu.SemaphoreType.DMA((2,)),
        ],
        compiler_params=pltpu.CompilerParams(collective_id=1, has_side_effects=True),
        name="scatter",
    )(prow, pcol)


def solution(mesh):
    placed = (P(None, None, None, ("row", "col")), P(), P(None, None, ("row", "col"), None), P(), P())
    return jax.shard_map(on_device, mesh=mesh, in_specs=placed,
                         out_specs=P(None, None, None, ("row", "col")), check_vma=False)
```

```python
import functools

import jax
import jax.numpy as jnp
from jax import lax
from jax.experimental import pallas as pl
from jax.experimental.pallas import tpu as pltpu
from jax.sharding import PartitionSpec as P

MESH = pl.DeviceIdType.MESH
ROWS, COLS, SIDE = 16, 8, 4
S, U, BEADS = 4, 8, 128
CAP = 64
LABELS = 48
NR, NC = COLS * U, ROWS * U
PAD = 4
WIDE = 4
BIG = 64.0
F32, BF16, I32 = jnp.float32, jnp.bfloat16, jnp.int32
ANY = pl.BlockSpec(memory_space=pl.ANY)
VMEM = pl.BlockSpec(memory_space=pltpu.VMEM)
SMEM = pl.BlockSpec(memory_space=pltpu.SMEM)
NT = (((1,), (1,)), ((), ()))


def iota(shape, axis):
    return lax.broadcasted_iota(I32, shape, axis)


def chrom_bounds(lens_ref):
    lens = jnp.broadcast_to(lens_ref[...], (LABELS, lens_ref.shape[1]))
    sub, lane = iota(lens.shape, 0), iota(lens.shape, 1)
    ends = jnp.sum(jnp.where(lane <= sub, lens, 0), axis=1, keepdims=True)
    starts = jnp.sum(jnp.where(lane < sub, lens, 0), axis=1, keepdims=True)
    return starts, ends


def make_list(row, col, lens_ref, pairs_ref, count_ref, stage_ref, out_ref):
    for s in range(S):
        for t in range(32):
            e, lane = s * 32 + t, slice(t * 128, t * 128 + 128)
            stage_ref[0, e:e + 1, :] = pairs_ref[s, 0:1, lane]
            stage_ref[1, e:e + 1, :] = pairs_ref[s, 1:2, lane]
            stage_ref[2, e:e + 1, :] = count_ref[s:s + 1, lane]
    first, second, counts = stage_ref[0], stage_ref[1], stage_ref[2]
    mine = (((first & 127) >> 3) == row) & ((second & 7) == col)
    mask = mine.astype(F32).astype(BF16)
    a, b = iota((128, 128), 0), iota((128, 128), 1)
    upper = (a <= b).astype(F32).astype(BF16)
    within = jnp.dot(mask, upper, preferred_element_type=F32)
    total = jnp.dot(mask, jnp.ones((128, 128), BF16), preferred_element_type=F32)
    lower = ((b < a) & ((a >> 5) == (b >> 5))).astype(F32).astype(BF16)
    offset = jnp.dot(lower, total.astype(BF16), preferred_element_type=F32)
    place = jnp.where(mine, (offset + within).astype(I32) - 1, -1)
    row_at = (first & 7) * U + (first >> 7)
    for i, v in enumerate([row_at, second >> 3, counts, mine.astype(I32), place]):
        stage_ref[i] = v
    slots = iota((CAP, 128), 0)
    pad = jnp.zeros((12, 128), F32)
    for s in range(S):
        def gather_slots(t, acc):
            e = s * 32 + t
            hot = (stage_ref[4, pl.ds(e, 1), :] == slots).astype(F32).astype(BF16)
            rows = [stage_ref[i, pl.ds(e, 1), :].astype(F32) for i in range(4)]
            rows = jnp.concatenate(rows + [pad], axis=0).astype(BF16)
            return acc + lax.dot_general(rows, hot, NT, preferred_element_type=F32)

        acc = lax.fori_loop(0, 32, gather_slots, jnp.zeros((16, CAP), F32))
        spare = jnp.where(iota((8, CAP), 0) == 1, NC * (1.0 - acc[3:4]), 0.0)
        out_ref[s * 8:s * 8 + 8, 0:CAP] = (acc[0:8] + spare).astype(I32)
        amount = jnp.sum(acc[3:4], axis=1, keepdims=True).astype(I32)
        out_ref[s * 8 + 4:s * 8 + 5, :] = jnp.broadcast_to(amount, (1, 128))
    starts, ends = chrom_bounds(lens_ref)
    lane = iota((1, 128), 1)
    block = (lane & 7) * 128 + row * 8 + ((lane >> 3) & 7)
    last = jnp.broadcast_to(block * 128 + 127, (LABELS, 128))
    stop = jnp.min(jnp.where(ends > last, ends, 1 << 20), axis=0, keepdims=True)
    gap = (col - ((lane >> 3) & 7)) & 7
    far = jnp.minimum(jnp.minimum((stop - 1) >> 7, block + 31), 1023)
    width = jnp.clip(((far - block - gap) >> 3) + 1, 0, 4)
    out_ref[32:33, :] = width
    out_ref[33:34, :] = jnp.full((1, 128), row, I32)
    out_ref[34:35, :] = jnp.full((1, 128), col, I32)
    out_ref[35:40, :] = jnp.zeros((5, 128), I32)


def greet(r, c):
    y, z = r // SIDE, lax.rem(r, SIDE)
    peers = [(r, lax.rem(c + d, COLS)) for d in range(1, COLS)]
    peers += [(lax.rem(y + d, SIDE) * SIDE + z, c) for d in range(1, SIDE)]
    peers += [(y * SIDE + lax.rem(z + d, SIDE), c) for d in range(1, SIDE)]
    barrier = pltpu.get_barrier_semaphore()
    for peer in peers:
        pl.semaphore_signal(barrier, 1, device_id=peer, device_id_type=MESH)
    pl.semaphore_wait(barrier, len(peers))


def gather_kernel(coords, counts, lens_ref, pairs, inter, rows, cols, tallies, list_ref,
                  pairs_ref, inter_ref, stage_ref, send, recv, local):
    r, c = lax.axis_index("row"), lax.axis_index("col")
    y, z = r // SIDE, lax.rem(r, SIDE)
    taken = [pltpu.make_async_copy(pairs, pairs_ref, local.at[3]),
             pltpu.make_async_copy(inter, inter_ref, local.at[4])]
    kept = [pltpu.make_async_copy(coords, rows.at[c], local.at[0]),
            pltpu.make_async_copy(coords, cols.at[r], local.at[1]),
            pltpu.make_async_copy(counts, tallies.at[c], local.at[2])]
    for copy in taken + kept:
        copy.start()
    greet(r, c)
    half = (pl.ds(0, S // 2), pl.ds(S // 2, S // 2))

    def along(axis, d):
        return (lax.rem(y + d, SIDE) * SIDE + z, c) if axis == 0 else (y * SIDE + lax.rem(z + d, SIDE), c)

    def relay(h, step, d):
        back = (lax.rem(y + SIDE - step, SIDE) * SIDE + z) if h == 0 else y * SIDE + lax.rem(z + SIDE - step, SIDE)
        source = coords.at[half[h]] if step == 0 else cols.at[back, half[h]]
        n = (h * SIDE + step) * SIDE + d
        return pltpu.make_async_remote_copy(
            source, cols.at[back, half[h]], send.at[n], recv.at[n],
            device_id=along(1 - h, d), device_id_type=MESH)

    early, base = [], 2 * SIDE * SIDE
    for d in (1, 3, 2):
        for h in range(2):
            n = base + h * SIDE + d
            early.append((h, d, pltpu.make_async_remote_copy(
                coords.at[half[h]], cols.at[r, half[h]], send.at[n], recv.at[n],
                device_id=along(h, d), device_id_type=MESH)))
    base += 2 * SIDE
    across = []
    for d in range(1, COLS):
        peer = (r, lax.rem(c + d, COLS))
        across.append(pltpu.make_async_remote_copy(
            coords, rows.at[c], send.at[base + d], recv.at[base + d], device_id=peer, device_id_type=MESH))
        across.append(pltpu.make_async_remote_copy(
            counts, tallies.at[c], send.at[base + COLS + d], recv.at[base + COLS + d],
            device_id=peer, device_id_type=MESH))
    for _, _, copy in early:
        copy.start()
    late = [relay(h, 0, d) for d in (1, 3, 2) for h in range(2)]
    for copy in late + across:
        copy.start()
    for h, step, copy in early:
        copy.wait_recv()
        passed = [relay(h, step, d) for d in (1, 3, 2)]
        for forward in passed:
            forward.start()
        late += passed
    for copy in taken:
        copy.wait()
    make_list(r, c, lens_ref, pairs_ref, inter_ref, stage_ref, list_ref)
    for _, _, copy in early:
        copy.wait_send()
    for copy in kept + across + late:
        copy.wait()


def scatter_kernel(rows, cols, out, land_a, land_b, sum_a, sum_b, last_a, last_b, land, own, send, recv, local):
    r, c = lax.axis_index("row"), lax.axis_index("col")
    y, z = r // SIDE, lax.rem(r, SIDE)
    a, b = pl.ds(0, S // 2), pl.ds(S // 2, S // 2)
    kept = [pltpu.make_async_copy(rows.at[c], own, local.at[0]),
            pltpu.make_async_copy(cols.at[:, z, a], sum_a, local.at[1]),
            pltpu.make_async_copy(cols.at[y, :, b], sum_b, local.at[2])]
    for copy in kept:
        copy.start()
    greet(r, c)
    first_a, first_b, across = [], [], []
    for d in (1, 3, 2):
        to = lax.rem(z + d, SIDE)
        first_a.append(pltpu.make_async_remote_copy(
            cols.at[:, to, a], land_a.at[d - 1], send.at[d], recv.at[d],
            device_id=(y * SIDE + to, c), device_id_type=MESH))
        to = lax.rem(y + d, SIDE)
        first_b.append(pltpu.make_async_remote_copy(
            cols.at[to, :, b], land_b.at[d - 1], send.at[SIDE + d], recv.at[SIDE + d],
            device_id=(to * SIDE + z, c), device_id_type=MESH))
    for d in range(1, COLS):
        to = lax.rem(c + d, COLS)
        n = 4 * SIDE + d
        across.append(pltpu.make_async_remote_copy(
            rows.at[to], land.at[d - 1], send.at[n], recv.at[n],
            device_id=(r, to), device_id_type=MESH))
    for one, two in zip(first_a, first_b):
        one.start()
        two.start()
    for copy in across:
        copy.start()
    second = []
    for turn, (first, total, landed, last) in enumerate(
            [(first_a, sum_a, land_a, last_a), (first_b, sum_b, land_b, last_b)]):
        kept[1 + turn].wait()
        for copy in first:
            copy.wait_recv()
        for i in range(SIDE):
            for s in range(S // 2):
                total[i, s] = (total[i, s] + landed[0, i, s]) + (landed[1, i, s] + landed[2, i, s])
        for d in (1, 3, 2):
            here = y if turn == 0 else z
            to = lax.rem(here + d, SIDE)
            n = (2 + turn) * SIDE + d
            peer = (to * SIDE + z, c) if turn == 0 else (y * SIDE + to, c)
            copy = pltpu.make_async_remote_copy(
                total.at[to], last.at[d - 1], send.at[n], recv.at[n], device_id=peer, device_id_type=MESH)
            copy.start()
            second.append(copy)
    kept[0].wait()
    for copy in across:
        copy.wait_recv()
    for s in range(S):
        total = own[s]
        for d in range(COLS - 1):
            total = total + land[d, s]
        out[s] = total
    for copy in second:
        copy.wait_recv()
    for s in range(S // 2):
        out[s] = out[s] + (sum_a[y, s] + last_a[0, s]) + (last_a[1, s] + last_a[2, s])
        out[s + S // 2] = out[s + S // 2] + (sum_b[z, s] + last_b[0, s]) + (last_b[1, s] + last_b[2, s])
    for copy in first_a + first_b + across + second:
        copy.wait_send()


def split3(x):
    a = x.astype(BF16).astype(F32)
    b = (x - a).astype(BF16).astype(F32)
    return a, b, (x - a) - b


def points_of(x, y, z):
    c = 0.75 - 0.25 * (x * x + y * y + z * z)
    return split3(x), split3(y), split3(z), split3(c)


def pair_kernel(list_ref, tally_ref, lens_ref, rows_ref, cols_ref,
                prow_ref, pcol_ref,
                unit_ref, tile_ref, left_ref, lrow_ref, right_ref, same_ref, differ_ref,
                sum_ref, num_ref, gcol_ref, grow_ref, lsum_ref, lnum_ref, lgcol_ref, lgrow_ref,
                arow_ref, acol_ref):
    r, c = list_ref[33, 0], list_ref[34, 0]
    starts, ends = chrom_bounds(lens_ref)
    starts = jnp.broadcast_to(starts, (LABELS, BEADS))
    ends = jnp.broadcast_to(ends, (LABELS, BEADS))
    lanes = iota((LABELS, BEADS), 1)
    eye = (iota((128, 128), 0) == iota((128, 128), 1)).astype(F32).astype(BF16)
    one = jnp.ones((8, 128), F32)
    nil = jnp.zeros((8, 128), F32)
    for v in range(S):
        for u in range(U):
            for q in range(3):
                tile_ref[v, u, 8 * q:8 * q + 8] = nil

    def hot_of(block):
        bead = lanes + block * BEADS
        return (bead >= starts) & (bead < ends)

    for v in range(S):
        tile_ref[v, :, 4, :] = one

    @pl.loop(0, COLS)
    def _(k):
        for s in range(S):
            x, y, z = rows_ref[k, s, 0], rows_ref[k, s, 1], rows_ref[k, s, 2]
            parts = points_of(x, y, z)
            for q in range(3):
                for w in range(4):
                    value = parts[w][q]
                    tile_ref[s, :, 8 * q + w, :] = 0.5 * value if w < 3 else value
        for u in range(0, U, 2):
            hots = [jnp.where(hot_of((u + i) * 128 + r * 8 + k), 1.0, 0.0).astype(BF16) for i in range(2)]
            for s in range(S):
                fulls = []
                for i in range(2):
                    tiles = [tile_ref[s, u + i, 8 * q:8 * q + 8] for q in range(3)]
                    full = jnp.concatenate([tiles[j] for j in (0, 0, 1, 0, 2, 1)], axis=0).astype(BF16)
                    fulls += [full, hots[i], jnp.zeros((32, 128), BF16)]
                    lrow_ref[s * NR + k * U + u + i] = jnp.concatenate(tiles[:2], axis=0).astype(BF16)
                flipped = lax.dot_general(eye, jnp.concatenate(fulls, axis=0), NT, preferred_element_type=F32)
                for i in range(2):
                    left_ref[s * NR + k * U + u + i] = flipped[:, i * 128:i * 128 + 128].astype(BF16)

    for v in range(S):
        tile_ref[v, :, 3, :] = one
        tile_ref[v, :, 11, :] = nil
        tile_ref[v, :, 19, :] = nil

    @pl.loop(0, ROWS)
    def _(k):
        for s in range(S):
            x, y, z = cols_ref[k, s, 0], cols_ref[k, s, 1], cols_ref[k, s, 2]
            parts = points_of(x, y, z)
            for q in range(3):
                for w in range(4):
                    tile_ref[s, :, 8 * q + (w if w < 3 else 4), :] = parts[w][q]
        for s in range(S):
            for u in range(U):
                tiles = [tile_ref[s, u, 8 * q:8 * q + 8] for q in range(3)]
                full = jnp.concatenate([tiles[i] for i in (0, 1, 0, 2, 0, 1)], axis=0)
                right_ref[s, u * ROWS + k] = full.astype(BF16)
        for u in range(U):
            hot = hot_of((u * ROWS + k) * 8 + c)
            same_ref[u * ROWS + k] = jnp.where(hot, 0.0, -BIG).astype(BF16)
            differ_ref[u * ROWS + k] = jnp.where(hot, -BIG, 0.0).astype(BF16)
    for p in range(PAD):
        same_ref[NC + p] = jnp.full((LABELS, BEADS), -BIG, BF16)
        for s in range(S):
            right_ref[s, NC + p] = jnp.zeros((LABELS, BEADS), BF16)
    differ_ref[NC] = jnp.full((LABELS, BEADS), -BIG, BF16)

    @pl.loop(0, (NC + PAD) // 4)
    def _(i):
        for s in range(S):
            for j in range(4):
                acol_ref[s, i * 4 + j] = nil

    @pl.loop(0, NR // 4)
    def _(i):
        for s in range(S):
            for j in range(4):
                arow_ref[s, i * 4 + j] = nil

    def collect(i, filled):
        k = i >> 3
        width = list_ref[32, i]
        unit_ref[filled] = i * 2
        filled = filled + jnp.where((width > 0) & (k != c), 1, 0)
        unit_ref[filled] = i * 2 + 1
        return filled + jnp.where(width > 2, 1, 0)

    units = lax.fori_loop(0, NR, collect, jnp.int32(0))
    unit_ref[units] = unit_ref[jnp.maximum(units - 1, 0)]
    triangle = iota((128, 128), 0) < iota((128, 128), 1)
    empty = jnp.zeros((16, 128), BF16)

    def chances(left, blocks, labels, diagonal=False):
        right = [jnp.concatenate([b, l], axis=0) for b, l in zip(blocks, labels)]
        right = jnp.concatenate(right, axis=1)
        return jnp.dot(left[:, :2 * LABELS], right, preferred_element_type=F32)

    def finish(z, diagonal=False):
        t = jnp.tanh(z)
        if diagonal:
            t = jnp.concatenate([jnp.where(triangle, t[:, :128], -1.0), t[:, 128:]], axis=1)
        return jnp.sum(t, axis=0, keepdims=True), (1.0 - t * t).astype(BF16)

    def pull(g, near, far):
        o = jnp.dot(near, g, preferred_element_type=F32)
        spread = jnp.concatenate([jnp.concatenate([far[0], empty], axis=1),
                                  jnp.concatenate([empty, far[1]], axis=1)], axis=0)
        p = lax.dot_general(spread, g, NT, preferred_element_type=F32)
        return o[0:8] + o[8:16], p[0:8] + p[8:16], p[16:24] + p[24:32]

    def window_pull(g, sums, at, start, out):
        o, p0, p1 = pull(g, lrow_ref[at], [right_ref[at >> 6, start + m, 0:16] for m in range(2)])
        gcol_ref[out] = o
        grow_ref[out, :, 0:128] = p0
        grow_ref[out, :, 128:256] = p1
        for m in range(2):
            sum_ref[m, pl.ds(out, 1), :] = sums[:, m * 128:m * 128 + 128]

    def locate(unit):
        at = unit >> 1
        k, u = at >> 3, at & 7
        start = u * ROWS + r + jnp.where(k > c, 1, 0) + 2 * (unit & 1)
        gap = ((c - k) & 7) + 16 * (unit & 1)
        return at, start, k, u, gap

    def run(unit_at, count, diagonal):
        def drain(held):
            for entry in held:
                window_pull(*entry)

        def body(it, held):
            for q in range(2):
                unit = unit_at(it * 2 + q)
                here, begin, k, u, gap = locate(unit)
                labels = [same_ref[begin + m] for m in range(2)]
                for s0 in range(0, S, WIDE):
                    group = range(s0, s0 + WIDE)
                    zs = [chances(left_ref[s * NR + here], [right_ref[s, begin + m] for m in range(2)], labels)
                          for s in group]
                    drain(held)
                    done = [finish(z, diagonal) for z in zs]
                    held = [(done[i][1], done[i][0], s * NR + here, begin, unit * S + s)
                            for i, s in enumerate(group)]
                for s in range(S):
                    for m in range(2):
                        n = tally_ref[k, s, u, 0, gap + 8 * m]
                        num_ref[m, pl.ds(unit * S + s, 1), :] = jnp.full((1, 128), n, I32).astype(F32)
            return held

        first = [(jnp.zeros((128, 256), BF16), jnp.zeros((1, 256), F32),
                  jnp.int32(0), jnp.int32(0), jnp.int32(NR * S * 2 + i)) for i in range(WIDE)]
        drain(lax.fori_loop(0, count, body, first))

    run(lambda i: (c * U + i) * 2, U // 2, True)
    run(lambda i: unit_ref[i], (units + 1) >> 1, False)

    most = jnp.maximum(jnp.maximum(list_ref[4, 0], list_ref[12, 0]),
                       jnp.maximum(list_ref[20, 0], list_ref[28, 0]))

    def listed_pull(g, sums, places):
        near = jnp.concatenate([lrow_ref[p[0]] for p in places], axis=0)
        o = jnp.dot(near, jnp.concatenate(g, axis=1), preferred_element_type=F32)
        far = jnp.concatenate([right_ref[p[0] >> 6, p[1], 0:16] for p in places], axis=0)
        w = lax.dot_general(far, jnp.concatenate(g, axis=0), NT, preferred_element_type=F32)
        for m, p in enumerate(places):
            lane = slice(m * 128, m * 128 + 128)
            lgcol_ref[p[2]] = o[m * 16:m * 16 + 8, lane] + o[m * 16 + 8:m * 16 + 16, lane]
            lgrow_ref[p[2]] = w[m * 16:m * 16 + 8, lane] + w[m * 16 + 8:m * 16 + 16, lane]
            lsum_ref[0, pl.ds(p[2], 1), :] = sums[m]

    def listed_body(it, carry):
        g, sums, places = carry
        for turn in range(2):
            slot = it * 2 + turn
            for s0 in range(0, S, 2):
                zs, now = [], []
                for s in (s0, s0 + 1):
                    i, j = list_ref[s * 8, slot], list_ref[s * 8 + 1, slot]
                    zs.append(chances(left_ref[s * NR + i], [right_ref[s, j]], [differ_ref[j]]))
                    now.append((s * NR + i, j, s * CAP + slot))
                    lnum_ref[0, pl.ds(s * CAP + slot, 1), :] = jnp.full(
                        (1, 128), list_ref[s * 8 + 2, slot], I32).astype(F32)
                listed_pull(g, sums, places)
                done = [finish(z) for z in zs]
                sums, g, places = [d[0] for d in done], [d[1] for d in done], now
        return g, sums, places

    idle = (jnp.int32(0), jnp.int32(0))
    first = ([jnp.zeros((128, 128), BF16)] * 2, [jnp.zeros((1, 128), F32)] * 2,
             [idle + (jnp.int32(CAP * S),), idle + (jnp.int32(CAP * S + 1),)])
    listed_pull(*lax.fori_loop(0, (most + 1) >> 1, listed_body, first))

    def weights(sums_ref, nums_ref, lo, width):
        for m in range(width):
            at = (m, pl.ds(lo, 8), slice(None))
            total = jnp.sum(sums_ref[at], axis=1, keepdims=True)
            expect = 0.5 + (0.5 * (16384.0 + total)) / 128.0
            nums_ref[at] = 1.0 - nums_ref[at] / jnp.broadcast_to(expect, (8, 128))

    @pl.loop(0, NR * S * 2 // 32)
    def _(i):
        for j in range(4):
            weights(sum_ref, num_ref, pl.multiple_of(i * 32 + j * 8, 8), 2)

    @pl.loop(0, CAP * S // 32)
    def _(i):
        for j in range(4):
            weights(lsum_ref, lnum_ref, pl.multiple_of(i * 32 + j * 8, 8), 1)

    def deposit(unit):
        at, start = locate(unit)[:2]
        held = []
        for s in range(S):
            out = unit * S + s
            w = [jnp.broadcast_to(num_ref[m, pl.ds(out, 1), :], (8, 128)) for m in range(2)]
            row = arow_ref[s, at] + (w[0] * grow_ref[out, :, 0:128] + w[1] * grow_ref[out, :, 128:256])
            col = [acol_ref[s, start + m] + w[m] * gcol_ref[out, :, m * 128:m * 128 + 128] for m in range(2)]
            held.append((row, col))
        for s in range(S):
            arow_ref[s, at] = held[s][0]
            for m in range(2):
                acol_ref[s, start + m] = held[s][1][m]

    @pl.loop(0, U)
    def _(u):
        deposit((c * U + u) * 2)

    @pl.loop(0, units)
    def _(i):
        deposit(unit_ref[i])

    @pl.loop(0, most)
    def _(slot):
        held = []
        for s in range(S):
            i, j, q = list_ref[s * 8, slot], list_ref[s * 8 + 1, slot], s * CAP + slot
            w = jnp.broadcast_to(lnum_ref[0, pl.ds(q, 1), :], (8, 128))
            held.append((i, j, arow_ref[s, i] + w * lgrow_ref[q], acol_ref[s, j] + w * lgcol_ref[q]))
        for s in range(S):
            i, j, row, col = held[s]
            arow_ref[s, i] = row
            acol_ref[s, j] = col

    @pl.loop(0, COLS)
    def _(k):
        for s in range(S):
            here = pl.ds(k * U, U)
            mass = arow_ref[s, here, 3, :]
            for w in range(3):
                pulled = rows_ref[k, s, w] * mass - arow_ref[s, here, w, :]
                prow_ref[k, s, w] = pulled * (-1.0 / 512.0)

    @pl.loop(0, ROWS)
    def _(k):
        for s in range(S):
            here = pl.ds(k, U, stride=ROWS)
            mass = acol_ref[s, here, 4, :]
            for w in range(3):
                pulled = cols_ref[k, s, w] * mass - 2.0 * acol_ref[s, here, w, :]
                pcol_ref[k, s, w] = pulled * (-1.0 / 512.0)


def pairs_call(listing, tallies, lens, rows, cols):
    shard = rows.shape[1:]
    return pl.pallas_call(
        pair_kernel,
        out_shape=[jax.ShapeDtypeStruct((COLS,) + shard, F32), jax.ShapeDtypeStruct((ROWS,) + shard, F32)],
        in_specs=[SMEM] * 2 + [VMEM] * 3, out_specs=[VMEM] * 2,
        scratch_shapes=[
            pltpu.SMEM((2 * NR + 2,), I32),
            pltpu.VMEM((S, U, 24, BEADS), F32),
            pltpu.VMEM((S * NR, BEADS, 128), BF16),
            pltpu.VMEM((S * NR, 16, BEADS), BF16),
            pltpu.VMEM((S, NC + PAD, LABELS, BEADS), BF16),
            pltpu.VMEM((NC + PAD, LABELS, BEADS), BF16),
            pltpu.VMEM((NC + 1, LABELS, BEADS), BF16),
            pltpu.VMEM((2, NR * S * 2 + 8, 128), F32),
            pltpu.VMEM((2, NR * S * 2 + 8, 128), F32),
            pltpu.VMEM((NR * S * 2 + 4, 8, 256), F32),
            pltpu.VMEM((NR * S * 2 + 4, 8, 256), F32),
            pltpu.VMEM((1, CAP * S + 8, 128), F32),
            pltpu.VMEM((1, CAP * S + 8, 128), F32),
            pltpu.VMEM((CAP * S + 2, 8, 128), F32),
            pltpu.VMEM((CAP * S + 2, 8, 128), F32),
            pltpu.VMEM((S, NR, 8, BEADS), F32),
            pltpu.VMEM((S, NC + PAD, 8, BEADS), F32),
        ],
        compiler_params=pltpu.CompilerParams(vmem_limit_bytes=60 << 20),
        name="pairs",
    )(listing, tallies, lens, rows, cols)


def on_device(coords, chrom_lengths, band_counts, inter_pairs, inter_counts):
    shard = coords.shape
    lens = chrom_lengths.reshape(1, -1)
    flipped = jnp.transpose(inter_pairs, (0, 2, 1))
    rows, cols, tallies, listing = pl.pallas_call(
        gather_kernel,
        out_shape=[jax.ShapeDtypeStruct((COLS,) + shard, F32), jax.ShapeDtypeStruct((ROWS,) + shard, F32),
                   jax.ShapeDtypeStruct((COLS,) + band_counts.shape, I32),
                   jax.ShapeDtypeStruct((40, 128), I32)],
        in_specs=[ANY] * 2 + [VMEM] + [ANY] * 2, out_specs=[ANY] * 3 + [VMEM],
        scratch_shapes=[
            pltpu.VMEM(flipped.shape, I32),
            pltpu.VMEM(inter_counts.shape, I32),
            pltpu.VMEM((5, 128, 128), I32),
            pltpu.SemaphoreType.DMA((2 * SIDE * SIDE + 2 * SIDE + 2 * COLS,)),
            pltpu.SemaphoreType.DMA((2 * SIDE * SIDE + 2 * SIDE + 2 * COLS,)),
            pltpu.SemaphoreType.DMA((5,)),
        ],
        compiler_params=pltpu.CompilerParams(collective_id=0, has_side_effects=True),
        name="gather",
    )(coords, band_counts, lens, flipped, inter_counts)
    prow, pcol = pairs_call(listing, tallies, lens, rows, cols)
    part = shard[1:]
    return pl.pallas_call(
        scatter_kernel,
        out_shape=jax.ShapeDtypeStruct(shard, F32),
        in_specs=[ANY] * 2, out_specs=VMEM,
        scratch_shapes=[
            pltpu.VMEM((SIDE - 1, SIDE, S // 2) + part, F32),
            pltpu.VMEM((SIDE - 1, SIDE, S // 2) + part, F32),
            pltpu.VMEM((SIDE, S // 2) + part, F32),
            pltpu.VMEM((SIDE, S // 2) + part, F32),
            pltpu.VMEM((SIDE - 1, S // 2) + part, F32),
            pltpu.VMEM((SIDE - 1, S // 2) + part, F32),
            pltpu.VMEM((COLS - 1,) + shard, F32),
            pltpu.VMEM(shard, F32),
            pltpu.SemaphoreType.DMA((4 * SIDE + COLS,)),
            pltpu.SemaphoreType.DMA((4 * SIDE + COLS,)),
            pltpu.SemaphoreType.DMA((3,)),
        ],
        compiler_params=pltpu.CompilerParams(collective_id=1, has_side_effects=True),
        name="scatter",
    )(prow, pcol.reshape((SIDE, SIDE) + shard))


def solution(mesh):
    placed = (P(None, None, None, ("row", "col")), P(), P(None, None, ("row", "col"), None), P(), P())
    return jax.shard_map(on_device, mesh=mesh, in_specs=placed,
                         out_specs=P(None, None, None, ("row", "col")), check_vma=False)
```

```python
import jax
import jax.numpy as jnp
from jax import lax
from jax.experimental import pallas as pl
from jax.experimental.pallas import tpu as pltpu
from jax.sharding import PartitionSpec as P

MESH = pl.DeviceIdType.MESH
ROWS, COLS, SIDE = 16, 8, 4
U, BEADS = 8, 128
CAP = 256
LABELS = 48
NR, NC = SIDE * COLS * U, ROWS * U
UNITS = 2 * NR
PAD = 4
WIDE = 4
BIG = 64.0
F32, BF16, I32 = jnp.float32, jnp.bfloat16, jnp.int32
ANY = pl.BlockSpec(memory_space=pl.ANY)
VMEM = pl.BlockSpec(memory_space=pltpu.VMEM)
SMEM = pl.BlockSpec(memory_space=pltpu.SMEM)
NT = (((1,), (1,)), ((), ()))
LISTED, TOTALS, WIDTHS, PLACE, TALLY, UNIT, LINES = 0, 16, 17, 19, 24, 88, 96


def iota(shape, axis):
    return lax.broadcasted_iota(I32, shape, axis)


def flag(x):
    return x.astype(F32).astype(BF16)


def chrom_bounds(lens_ref):
    lens = jnp.broadcast_to(lens_ref[...], (LABELS, lens_ref.shape[1]))
    sub, lane = iota(lens.shape, 0), iota(lens.shape, 1)
    ends = jnp.sum(jnp.where(lane <= sub, lens, 0), axis=1, keepdims=True)
    starts = jnp.sum(jnp.where(lane < sub, lens, 0), axis=1, keepdims=True)
    return starts, ends


def compact(mine, values, slots):
    count = mine.shape[0]
    a, b = iota((128, 128), 0), iota((128, 128), 1)
    within = jnp.dot(flag(mine), flag(a <= b), preferred_element_type=F32)
    total = jnp.dot(flag(mine), jnp.ones((128, 128), BF16), preferred_element_type=F32)
    lower = flag(iota((count, count), 1) < iota((count, count), 0))
    offset = jnp.dot(lower, total.astype(BF16), preferred_element_type=F32)
    place = jnp.where(mine, (offset + within).astype(I32) - 1, -1)
    values = [v.astype(F32) for v in values] + [mine.astype(F32)]
    slot = iota((slots, 128), 0)
    pad = jnp.zeros((16 - len(values), 128), F32)
    acc = jnp.zeros((16, slots), F32)
    for lo in range(0, count, 8):
        span = range(lo, min(lo + 8, count))
        hot = jnp.concatenate([flag(place[e:e + 1] == slot) for e in span], axis=1)
        rows = [jnp.concatenate([v[e:e + 1] for v in values] + [pad], axis=0) for e in span]
        acc = acc + lax.dot_general(jnp.concatenate(rows, axis=1).astype(BF16), hot, NT,
                                    preferred_element_type=F32)
    return acc[0:8]


def make_list(y, z, c, lens_ref, pairs_ref, count_ref, stage_ref, out_ref):
    for t in range(32):
        lane = slice(t * 128, t * 128 + 128)
        stage_ref[0, t:t + 1, :] = pairs_ref[0:1, lane]
        stage_ref[1, t:t + 1, :] = pairs_ref[1:2, lane]
        block = count_ref[:, lane]
        stage_ref[2, t:t + 1, :] = jnp.sum(jnp.where(iota(block.shape, 0) == y, block, 0), axis=0, keepdims=True)
    first, second, counts = stage_ref[0], stage_ref[1], stage_ref[2]
    mine = (((first >> 3) & 3) == z) & ((second & 7) == c)
    at = (first & 7) * 32 + ((first >> 5) & 3) * 8 + (first >> 7)
    acc = compact(mine, [at, second >> 3, counts], CAP)
    spare = jnp.where(iota((8, CAP), 0) == 1, NC * (1.0 - acc[3:4]), 0.0)
    found = (acc + spare).astype(I32)
    out_ref[LISTED:LISTED + 8, :] = found[:, 0:128]
    out_ref[LISTED + 8:LISTED + 16, :] = found[:, 128:256]

    starts, ends = chrom_bounds(lens_ref)
    widths = []
    for i in range(2):
        at = iota((1, 128), 1) + i * 128
        k = at >> 5
        block = (at & 7) * 128 + (((at >> 3) & 3) * 4 + z) * 8 + k
        last = jnp.broadcast_to(block * 128 + 127, (LABELS, 128))
        stop = jnp.min(jnp.where(ends > last, ends, 1 << 20), axis=0, keepdims=True)
        far = jnp.minimum(jnp.minimum((stop - 1) >> 7, block + 31), 1023)
        widths.append(((far - block - ((c - k) & 7)) >> 3) + 1)
    width = jnp.concatenate(widths + widths, axis=0)
    entry = iota((4, 128), 0) * 128 + iota((4, 128), 1)
    near = (entry < NR) & (width > 0) & (((entry >> 5) & 7) != c)
    live = near | ((entry >= NR) & (width > 2))
    acc = compact(live, [entry >> 2, entry & 3], UNITS)
    units = acc[0:1] * 4.0 + acc[1:2] + UNITS * (1.0 - acc[2:3])
    for i in range(4):
        out_ref[UNIT + i:UNIT + i + 1, :] = units[:, i * 128:i * 128 + 128].astype(I32)
    out_ref[UNIT + 4:UNIT + 8, :] = jnp.zeros((4, 128), I32)
    listed = jnp.sum(found[3:4].astype(F32), axis=1, keepdims=True).astype(I32)
    active = jnp.sum(acc[2:3], axis=1, keepdims=True).astype(I32)
    lane = iota((1, 128), 1)
    out_ref[TOTALS:TOTALS + 1, :] = jnp.where(lane == 0, listed, active)
    out_ref[WIDTHS:WIDTHS + 2, :] = jnp.zeros((2, 128), I32)
    out_ref[PLACE:PLACE + 1, :] = jnp.where(lane == 0, z, c)
    out_ref[PLACE + 1:TALLY, :] = jnp.zeros((4, 128), I32)


def greet(r, c):
    y, z = r // SIDE, lax.rem(r, SIDE)
    peers = [(r, lax.rem(c + d, COLS)) for d in range(1, COLS)]
    peers += [(lax.rem(y + d, SIDE) * SIDE + z, c) for d in range(1, SIDE)]
    peers += [(y * SIDE + lax.rem(z + d, SIDE), c) for d in range(1, SIDE)]
    barrier = pltpu.get_barrier_semaphore()
    for peer in peers:
        pl.semaphore_signal(barrier, 1, device_id=peer, device_id_type=MESH)
    pl.semaphore_wait(barrier, len(peers))


def gather_kernel(coords, counts, lens_ref, pairs, inter, rows, cols, list_ref,
                  pairs_ref, inter_ref, stage_ref, tallies, send, recv, local):
    r, c = lax.axis_index("row"), lax.axis_index("col")
    y, z = r // SIDE, lax.rem(r, SIDE)
    taken = [pltpu.make_async_copy(pairs.at[y], pairs_ref, local.at[0]),
             pltpu.make_async_copy(inter, inter_ref, local.at[1])]
    kept = [pltpu.make_async_copy(coords.at[y], rows.at[c, y], local.at[2]),
            pltpu.make_async_copy(counts.at[y], tallies.at[c, y], local.at[3])]
    for copy in kept + taken:
        copy.start()
    greet(r, c)

    def push(source, target, n, peer):
        return pltpu.make_async_remote_copy(source, target, send.at[n], recv.at[n],
                                            device_id=peer, device_id_type=MESH)

    early = []
    for d in (1, 3, 2):
        to = lax.rem(y + d, SIDE)
        peer = (to * SIDE + z, c)
        early.append(push(coords.at[to], rows.at[c, y], d, peer))
        early.append(push(counts.at[to], tallies.at[c, y], SIDE + d, peer))
    for copy in early:
        copy.start()
    for copy in kept:
        copy.wait()
    for copy in early:
        copy.wait_recv()
    same = pltpu.make_async_copy(rows.at[c], cols.at[z], local.at[4])
    same.start()
    late = []
    for d in (1, 3, 2):
        late.append(push(rows.at[c], cols.at[z], 2 * SIDE + d, (y * SIDE + lax.rem(z + d, SIDE), c)))
    for d in (4, 2, 6, 1, 3, 5, 7):
        late.append(push(rows.at[c], rows.at[c], 3 * SIDE + d, (r, lax.rem(c + d, COLS))))
    talk = []
    for d in range(1, COLS):
        talk.append(push(tallies.at[c], tallies.at[c], 3 * SIDE + COLS + d, (r, lax.rem(c + d, COLS))))
    for copy in late + talk:
        copy.start()
    for copy in taken:
        copy.wait()
    make_list(y, z, c, lens_ref, pairs_ref, inter_ref, stage_ref, list_ref)
    for copy in talk:
        copy.wait_recv()
    for k in range(COLS):
        for yy in range(SIDE):
            for u in range(U):
                at = TALLY + k * 8 + yy * 2 + u // 4
                list_ref[at:at + 1, (u % 4) * 32:(u % 4) * 32 + 32] = tallies[k, yy, u]
    for copy in early + talk:
        copy.wait_send()
    for copy in late:
        copy.wait()
    same.wait()


def scatter_kernel(rows, cols, out, land, own, total, last, send, recv, local):
    r, c = lax.axis_index("row"), lax.axis_index("col")
    y, z = r // SIDE, lax.rem(r, SIDE)
    kept = [pltpu.make_async_copy(rows.at[c], own.at[0], local.at[0]),
            pltpu.make_async_copy(cols.at[z], own.at[1], local.at[1])]
    for copy in kept:
        copy.start()
    greet(r, c)
    copies = []

    def push(source, target, n, peer):
        return pltpu.make_async_remote_copy(source, target, send.at[n], recv.at[n],
                                            device_id=peer, device_id_type=MESH)

    for d in (1, 3, 2):
        to = lax.rem(z + d, SIDE)
        copies.append(push(cols.at[to], land.at[d - 1], d, (y * SIDE + to, c)))
    for d in (4, 2, 6, 1, 3, 5, 7):
        to = lax.rem(c + d, COLS)
        copies.append(push(rows.at[to], land.at[SIDE - 2 + d], SIDE + d, (r, to)))
    for copy in copies:
        copy.start()
    for copy in kept:
        copy.wait()
    for copy in copies:
        copy.wait_recv()
    for i in range(SIDE):
        sums = own[0, i] + own[1, i]
        for d in range(SIDE + COLS - 2):
            sums = sums + land[d, i]
        total[i] = sums
    second = []
    for d in (1, 3, 2):
        to = lax.rem(y + d, SIDE)
        second.append(push(total.at[to], last.at[d - 1], SIDE + COLS + d, (to * SIDE + z, c)))
    for copy in second:
        copy.start()
    out[y] = total[y]
    for d, copy in zip((1, 3, 2), second):
        copy.wait_recv()
        out[lax.rem(y + SIDE - d, SIDE)] = last[d - 1]
    for copy in copies + second:
        copy.wait_send()


def split3(x):
    a = x.astype(BF16).astype(F32)
    b = (x - a).astype(BF16).astype(F32)
    return a, b, (x - a) - b


def points_of(x, y, z):
    c = 0.75 - 0.25 * (x * x + y * y + z * z)
    return split3(x), split3(y), split3(z), split3(c)


def pair_kernel(list_ref, lens_ref, rows_ref, cols_ref, prow_ref, pcol_ref,
                tile_ref, left_ref, lrow_ref, same_ref, differ_ref, arow_ref, acol_ref):
    z, c = list_ref[PLACE, 0], list_ref[PLACE, 1]
    starts, ends = chrom_bounds(lens_ref)
    starts = jnp.broadcast_to(starts, (LABELS, BEADS))
    ends = jnp.broadcast_to(ends, (LABELS, BEADS))
    lanes = iota((LABELS, BEADS), 1)
    eye = flag(iota((128, 128), 0) == iota((128, 128), 1))
    one = jnp.ones((8, 128), F32)
    nil = jnp.zeros((8, 128), F32)

    def hot_of(block):
        bead = lanes + block * BEADS
        return (bead >= starts) & (bead < ends)

    for v in range(SIDE):
        for u in range(U):
            for q in range(3):
                tile_ref[v, u, 8 * q:8 * q + 8] = nil
    for v in range(SIDE):
        tile_ref[v, :, 4, :] = one

    @pl.loop(0, COLS)
    def _(k):
        for yy in range(SIDE):
            parts = points_of(rows_ref[k, yy, 0], rows_ref[k, yy, 1], rows_ref[k, yy, 2])
            for q in range(3):
                for w in range(4):
                    value = parts[w][q]
                    tile_ref[yy, :, 8 * q + w, :] = 0.5 * value if w < 3 else value
        for yy in range(SIDE):
            for u in range(0, U, 2):
                fulls = []
                for i in range(2):
                    at = (k * SIDE + yy) * U + u + i
                    tiles = [tile_ref[yy, u + i, 8 * q:8 * q + 8] for q in range(3)]
                    full = jnp.concatenate([tiles[j] for j in (0, 0, 1, 0, 2, 1)], axis=0).astype(BF16)
                    hot = hot_of((u + i) * 128 + (4 * yy + z) * 8 + k)
                    fulls += [full, jnp.where(hot, 1.0, 0.0).astype(BF16), jnp.zeros((32, 128), BF16)]
                    lrow_ref[at] = jnp.concatenate(tiles[:2], axis=0).astype(BF16)
                flipped = lax.dot_general(eye, jnp.concatenate(fulls, axis=0), NT, preferred_element_type=F32)
                for i in range(2):
                    left_ref[(k * SIDE + yy) * U + u + i] = flipped[:, i * 128:i * 128 + 128].astype(BF16)

    for v in range(SIDE):
        tile_ref[v, :, 3, :] = one
        tile_ref[v, :, 11, :] = nil
        tile_ref[v, :, 19, :] = nil

    @pl.loop(0, SIDE)
    def _(zz):
        for yy in range(SIDE):
            parts = points_of(cols_ref[zz, yy, 0], cols_ref[zz, yy, 1], cols_ref[zz, yy, 2])
            for q in range(3):
                for w in range(4):
                    tile_ref[yy, :, 8 * q + (w if w < 3 else 4), :] = parts[w][q]
        for yy in range(SIDE):
            for u in range(U):
                at = u * ROWS + 4 * yy + zz
                tiles = [tile_ref[yy, u, 8 * q:8 * q + 8] for q in range(3)]
                full = jnp.concatenate([tiles[i] for i in (0, 1, 0, 2, 0, 1)], axis=0).astype(BF16)
                hot = hot_of(at * 8 + c)
                same_ref[at, 0:LABELS] = full
                differ_ref[at, 0:LABELS] = full
                same_ref[at, LABELS:] = jnp.where(hot, 0.0, -BIG).astype(BF16)
                differ_ref[at, LABELS:] = jnp.where(hot, -BIG, 0.0).astype(BF16)

    apart = jnp.concatenate([jnp.zeros((LABELS, BEADS), BF16), jnp.full((LABELS, BEADS), -BIG, BF16)], axis=0)
    for p in range(PAD):
        same_ref[NC + p] = apart
    differ_ref[NC] = apart

    @pl.loop(0, (NC + PAD) // 4)
    def _(i):
        for j in range(4):
            acol_ref[i * 4 + j] = nil

    @pl.loop(0, NR // 8)
    def _(i):
        for j in range(8):
            arow_ref[i * 8 + j] = nil

    triangle = iota((128, 128), 0) < iota((128, 128), 1)
    empty = jnp.zeros((16, 128), BF16)

    def finish(z, diagonal=False):
        t = jnp.tanh(z)
        if diagonal:
            t = jnp.concatenate([jnp.where(triangle, t[:, :128], -1.0), t[:, 128:]], axis=1)
        return jnp.sum(t, axis=0, keepdims=True), (1.0 - t * t).astype(BF16)

    def weigh(sums, n):
        expect = 0.5 + (0.5 * (16384.0 + jnp.sum(sums, axis=1, keepdims=True))) / 128.0
        n = jnp.full((1, 128), n, I32).astype(F32)
        return jnp.broadcast_to(1.0 - n / jnp.broadcast_to(expect, (1, 128)), (8, 128))

    def unit_drain(g, sums, at, start, counts):
        far = [same_ref[start + m, 0:16] for m in range(2)]
        o = jnp.dot(lrow_ref[at], g, preferred_element_type=F32)
        spread = jnp.concatenate([jnp.concatenate([far[0], empty], axis=1),
                                  jnp.concatenate([empty, far[1]], axis=1)], axis=0)
        p = lax.dot_general(spread, g, NT, preferred_element_type=F32)
        w = [weigh(sums[:, m * 128:m * 128 + 128], counts[m]) for m in range(2)]
        arow_ref[at] += w[0] * (p[0:8] + p[8:16]) + w[1] * (p[16:24] + p[24:32])
        for m in range(2):
            lane = slice(m * 128, m * 128 + 128)
            acol_ref[start + m] += w[m] * (o[0:8, lane] + o[8:16, lane])

    def run(unit_at, trips, diagonal):
        def body(it, held):
            for q in range(2):
                zs, now = [], []
                for i in range(WIDE):
                    entry = unit_at(it * 2 * WIDE + q * WIDE + i)
                    at, half = entry & (NR - 1), entry >> 8
                    k, u = at >> 5, at & 7
                    start = u * ROWS + 4 * ((at >> 3) & 3) + z + jnp.where(k > c, 1, 0) + 2 * half
                    start = jnp.where(entry < UNITS, start, NC)
                    lane = (at & 3) * 32 + ((c - k) & 7) + 16 * half
                    counts = [list_ref[TALLY + (at >> 2), lane + 8 * m] for m in range(2)]
                    right = jnp.concatenate([same_ref[start], same_ref[start + 1]], axis=1)
                    zs.append(jnp.dot(left_ref[at, :, 0:2 * LABELS], right, preferred_element_type=F32))
                    now.append((at, start, counts))
                for entry in held:
                    unit_drain(*entry)
                done = [finish(v, diagonal) for v in zs]
                held = [(done[i][1], done[i][0]) + now[i] for i in range(WIDE)]
            return held

        zero = jnp.int32(0)
        first = [(jnp.zeros((128, 256), BF16), jnp.zeros((1, 256), F32), zero, zero, [zero, zero])
                 for _ in range(WIDE)]
        for entry in lax.fori_loop(0, trips, body, first):
            unit_drain(*entry)

    run(lambda i: c * (SIDE * U) + i, SIDE * U // (2 * WIDE), True)
    run(lambda i: list_ref[UNIT + (i >> 7), i & 127], (list_ref[TOTALS, 1] + 2 * WIDE - 1) // (2 * WIDE), False)

    def listed_drain(held):
        for lo in range(0, WIDE, 2):
            pair = held[lo:lo + 2]
            near = jnp.concatenate([lrow_ref[p[2]] for p in pair], axis=0)
            far = jnp.concatenate([differ_ref[p[3], 0:16] for p in pair], axis=0)
            o = jnp.dot(near, jnp.concatenate([p[0] for p in pair], axis=1), preferred_element_type=F32)
            v = lax.dot_general(far, jnp.concatenate([p[0] for p in pair], axis=0), NT,
                                preferred_element_type=F32)
            for m, p in enumerate(pair):
                lane, at = slice(m * 128, m * 128 + 128), m * 16
                w = weigh(p[1], p[4])
                arow_ref[p[2]] += w * (v[at:at + 8, lane] + v[at + 8:at + 16, lane])
                acol_ref[p[3]] += w * (o[at:at + 8, lane] + o[at + 8:at + 16, lane])

    def listed_body(it, held):
        for q in range(2):
            zs, now = [], []
            for i in range(WIDE):
                slot = it * 2 * WIDE + q * WIDE + i
                line, lane = LISTED + (slot >> 7) * 8, slot & 127
                at, to, n = [list_ref[line + f, lane] for f in range(3)]
                zs.append(jnp.dot(left_ref[at, :, 0:2 * LABELS], differ_ref[to], preferred_element_type=F32))
                now.append((at, to, n))
            listed_drain(held)
            done = [finish(v) for v in zs]
            held = [(done[i][1], done[i][0]) + now[i] for i in range(WIDE)]
        return held

    zero = jnp.int32(0)
    first = [(jnp.zeros((128, 128), BF16), jnp.zeros((1, 128), F32), zero, zero, zero) for _ in range(WIDE)]
    listed_drain(lax.fori_loop(0, (list_ref[TOTALS, 0] + 2 * WIDE - 1) // (2 * WIDE), listed_body, first))

    @pl.loop(0, COLS)
    def _(k):
        for yy in range(SIDE):
            here = pl.ds((k * SIDE + yy) * U, U)
            mass = arow_ref[here, 3, :]
            for w in range(3):
                pulled = rows_ref[k, yy, w] * mass - arow_ref[here, w, :]
                prow_ref[k, yy, w] = pulled * (-1.0 / 512.0)

    @pl.loop(0, SIDE)
    def _(zz):
        for yy in range(SIDE):
            here = pl.ds(4 * yy + zz, U, stride=ROWS)
            mass = acol_ref[here, 4, :]
            for w in range(3):
                pulled = cols_ref[zz, yy, w] * mass - 2.0 * acol_ref[here, w, :]
                pcol_ref[zz, yy, w] = pulled * (-1.0 / 512.0)


def pairs_call(listing, lens, rows, cols):
    return pl.pallas_call(
        pair_kernel,
        out_shape=[jax.ShapeDtypeStruct(rows.shape, F32), jax.ShapeDtypeStruct(cols.shape, F32)],
        in_specs=[SMEM] + [VMEM] * 3, out_specs=[VMEM] * 2,
        scratch_shapes=[
            pltpu.VMEM((SIDE, U, 24, BEADS), F32),
            pltpu.VMEM((NR, BEADS, 128), BF16),
            pltpu.VMEM((NR, 16, BEADS), BF16),
            pltpu.VMEM((NC + PAD + 2, 2 * LABELS, BEADS), BF16),
            pltpu.VMEM((NC + 1, 2 * LABELS, BEADS), BF16),
            pltpu.VMEM((NR, 8, BEADS), F32),
            pltpu.VMEM((NC + PAD + 2, 8, BEADS), F32),
        ],
        compiler_params=pltpu.CompilerParams(vmem_limit_bytes=60 << 20),
        name="pairs",
    )(listing, lens, rows, cols)


def on_device(coords, chrom_lengths, band_counts, inter_pairs, inter_counts):
    part = coords.shape[1:]
    lens = chrom_lengths.reshape(1, -1)
    flipped = jnp.transpose(inter_pairs, (0, 2, 1))
    sems = 3 * SIDE + 2 * COLS
    rows, cols, listing = pl.pallas_call(
        gather_kernel,
        out_shape=[jax.ShapeDtypeStruct((COLS, SIDE) + part, F32), jax.ShapeDtypeStruct((SIDE, SIDE) + part, F32),
                   jax.ShapeDtypeStruct((LINES, 128), I32)],
        in_specs=[ANY] * 2 + [VMEM] + [ANY] * 2, out_specs=[ANY] * 2 + [VMEM],
        scratch_shapes=[
            pltpu.VMEM(flipped.shape[1:], I32),
            pltpu.VMEM(inter_counts.shape, I32),
            pltpu.VMEM((3, 32, 128), I32),
            pltpu.VMEM((COLS,) + band_counts.shape, I32),
            pltpu.SemaphoreType.DMA((sems,)),
            pltpu.SemaphoreType.DMA((sems,)),
            pltpu.SemaphoreType.DMA((5,)),
        ],
        compiler_params=pltpu.CompilerParams(collective_id=0, has_side_effects=True),
        name="gather",
    )(coords, band_counts, lens, flipped, inter_counts)
    prow, pcol = pairs_call(listing, lens, rows, cols)
    return pl.pallas_call(
        scatter_kernel,
        out_shape=jax.ShapeDtypeStruct(coords.shape, F32),
        in_specs=[ANY] * 2, out_specs=VMEM,
        scratch_shapes=[
            pltpu.VMEM((SIDE + COLS - 2, SIDE) + part, F32),
            pltpu.VMEM((2, SIDE) + part, F32),
            pltpu.VMEM((SIDE,) + part, F32),
            pltpu.VMEM((SIDE - 1,) + part, F32),
            pltpu.SemaphoreType.DMA((2 * SIDE + COLS,)),
            pltpu.SemaphoreType.DMA((2 * SIDE + COLS,)),
            pltpu.SemaphoreType.DMA((2,)),
        ],
        compiler_params=pltpu.CompilerParams(collective_id=1, has_side_effects=True),
        name="scatter",
    )(prow, pcol)


def solution(mesh):
    placed = (P(None, None, None, ("row", "col")), P(), P(None, None, ("row", "col"), None), P(), P())
    return jax.shard_map(on_device, mesh=mesh, in_specs=placed,
                         out_specs=P(None, None, None, ("row", "col")), check_vma=False)
```

```python
import jax
import jax.numpy as jnp
from jax import lax
from jax.experimental import pallas as pl
from jax.experimental.pallas import tpu as pltpu
from jax.sharding import PartitionSpec as P

MESH = pl.DeviceIdType.MESH
ROWS, COLS, SIDE = 16, 8, 4
U, BEADS = 8, 128
CAP = 256
LABELS = 48
NR, NC = SIDE * COLS * U, ROWS * U
UNITS = 2 * NR
PAD = 4
WIDE = 4
BIG = 64.0
F32, BF16, I32 = jnp.float32, jnp.bfloat16, jnp.int32
HBM = pl.BlockSpec(memory_space=pltpu.HBM)
VMEM = pl.BlockSpec(memory_space=pltpu.VMEM)
SMEM = pl.BlockSpec(memory_space=pltpu.SMEM)
NT = (((1,), (1,)), ((), ()))
LISTED, TOTALS, WIDTHS, PLACE, TALLY, UNIT, LINES = 0, 16, 17, 19, 24, 88, 96


def iota(shape, axis):
    return lax.broadcasted_iota(I32, shape, axis)


def flag(x):
    return x.astype(F32).astype(BF16)


def chrom_bounds(lens_ref):
    lens = jnp.broadcast_to(lens_ref[...], (LABELS, lens_ref.shape[1]))
    sub, lane = iota(lens.shape, 0), iota(lens.shape, 1)
    ends = jnp.sum(jnp.where(lane <= sub, lens, 0), axis=1, keepdims=True)
    starts = jnp.sum(jnp.where(lane < sub, lens, 0), axis=1, keepdims=True)
    return starts, ends


def compact(mine, values, slots):
    count = mine.shape[0]
    a, b = iota((128, 128), 0), iota((128, 128), 1)
    within = jnp.dot(flag(mine), flag(a <= b), preferred_element_type=F32)
    total = jnp.dot(flag(mine), jnp.ones((128, 128), BF16), preferred_element_type=F32)
    lower = flag(iota((count, count), 1) < iota((count, count), 0))
    offset = jnp.dot(lower, total.astype(BF16), preferred_element_type=F32)
    place = jnp.where(mine, (offset + within).astype(I32) - 1, -1)
    values = [v.astype(F32) for v in values] + [mine.astype(F32)]
    slot = iota((slots, 128), 0)
    pad = jnp.zeros((16 - len(values), 128), F32)
    acc = jnp.zeros((16, slots), F32)
    for lo in range(0, count, 8):
        span = range(lo, min(lo + 8, count))
        hot = jnp.concatenate([flag(place[e:e + 1] == slot) for e in span], axis=1)
        rows = [jnp.concatenate([v[e:e + 1] for v in values] + [pad], axis=0) for e in span]
        acc = acc + lax.dot_general(jnp.concatenate(rows, axis=1).astype(BF16), hot, NT,
                                    preferred_element_type=F32)
    return acc[0:8]


def make_list(y, z, c, lens_ref, pairs_ref, count_ref, stage_ref, out_ref, bounds_ref):
    for t in range(32):
        lane = slice(t * 128, t * 128 + 128)
        stage_ref[0, t:t + 1, :] = pairs_ref[0:1, lane]
        stage_ref[1, t:t + 1, :] = pairs_ref[1:2, lane]
        block = count_ref[:, lane]
        stage_ref[2, t:t + 1, :] = jnp.sum(jnp.where(iota(block.shape, 0) == y, block, 0), axis=0, keepdims=True)
    first, second, counts = stage_ref[0], stage_ref[1], stage_ref[2]
    mine = (((first >> 3) & 3) == z) & ((second & 7) == c)
    at = (first & 7) * 32 + ((first >> 5) & 3) * 8 + (first >> 7)
    acc = compact(mine, [at, second >> 3, counts], CAP)
    spare = jnp.where(iota((8, CAP), 0) == 1, NC * (1.0 - acc[3:4]), 0.0)
    found = (acc + spare).astype(I32)
    out_ref[LISTED:LISTED + 8, :] = found[:, 0:128]
    out_ref[LISTED + 8:LISTED + 16, :] = found[:, 128:256]

    starts, ends = chrom_bounds(lens_ref)
    bounds_ref[0] = jnp.broadcast_to(starts, (LABELS, BEADS))
    bounds_ref[1] = jnp.broadcast_to(ends, (LABELS, BEADS))
    widths = []
    for i in range(2):
        at = iota((1, 128), 1) + i * 128
        k = at >> 5
        block = (at & 7) * 128 + (((at >> 3) & 3) * 4 + z) * 8 + k
        last = jnp.broadcast_to(block * 128 + 127, (LABELS, 128))
        stop = jnp.min(jnp.where(ends > last, ends, 1 << 20), axis=0, keepdims=True)
        far = jnp.minimum(jnp.minimum((stop - 1) >> 7, block + 31), 1023)
        widths.append(((far - block - ((c - k) & 7)) >> 3) + 1)
    width = jnp.concatenate(widths + widths, axis=0)
    entry = iota((4, 128), 0) * 128 + iota((4, 128), 1)
    near = (entry < NR) & (width > 0) & (((entry >> 5) & 7) != c)
    live = near | ((entry >= NR) & (width > 2))
    acc = compact(live, [entry >> 2, entry & 3], UNITS)
    units = acc[0:1] * 4.0 + acc[1:2] + UNITS * (1.0 - acc[2:3])
    for i in range(4):
        out_ref[UNIT + i:UNIT + i + 1, :] = units[:, i * 128:i * 128 + 128].astype(I32)
    out_ref[UNIT + 4:UNIT + 8, :] = jnp.zeros((4, 128), I32)
    listed = jnp.sum(found[3:4].astype(F32), axis=1, keepdims=True).astype(I32)
    active = jnp.sum(acc[2:3], axis=1, keepdims=True).astype(I32)
    lane = iota((1, 128), 1)
    out_ref[TOTALS:TOTALS + 1, :] = jnp.where(lane == 0, listed, active)
    out_ref[WIDTHS:WIDTHS + 2, :] = jnp.zeros((2, 128), I32)
    out_ref[PLACE:PLACE + 1, :] = jnp.where(lane == 0, z, c)
    out_ref[PLACE + 1:TALLY, :] = jnp.zeros((4, 128), I32)


def greet(r, c):
    y, z = r // SIDE, lax.rem(r, SIDE)
    peers = [(r, lax.rem(c + d, COLS)) for d in range(1, COLS)]
    peers += [(lax.rem(y + d, SIDE) * SIDE + z, c) for d in range(1, SIDE)]
    peers += [(y * SIDE + lax.rem(z + d, SIDE), c) for d in range(1, SIDE)]
    barrier = pltpu.get_barrier_semaphore()
    for peer in peers:
        pl.semaphore_signal(barrier, 1, device_id=peer, device_id_type=MESH)
    pl.semaphore_wait(barrier, len(peers))


def gather_kernel(coords, counts, lens, pairs, inter, rows, cols, list_ref, bounds_ref,
                  lens_ref, pairs_ref, inter_ref, stage_ref, tallies, send, recv, local):
    r, c = lax.axis_index("row"), lax.axis_index("col")
    y, z = r // SIDE, lax.rem(r, SIDE)
    taken = [pltpu.make_async_copy(pairs.at[y], pairs_ref, local.at[0]),
             pltpu.make_async_copy(inter, inter_ref, local.at[1]),
             pltpu.make_async_copy(lens, lens_ref, local.at[5])]
    kept = [pltpu.make_async_copy(coords.at[y], rows.at[c, y], local.at[2]),
            pltpu.make_async_copy(counts.at[y], tallies.at[c, y], local.at[3])]
    for copy in kept + taken:
        copy.start()
    greet(r, c)

    def push(source, target, n, peer):
        return pltpu.make_async_remote_copy(source, target, send.at[n], recv.at[n],
                                            device_id=peer, device_id_type=MESH)

    early = []
    for d in (1, 3, 2):
        to = lax.rem(y + d, SIDE)
        peer = (to * SIDE + z, c)
        early.append(push(coords.at[to], rows.at[c, y], d, peer))
        early.append(push(counts.at[to], tallies.at[c, y], SIDE + d, peer))
    for copy in early:
        copy.start()
    for copy in kept:
        copy.wait()
    for copy in early:
        copy.wait_recv()
    same = pltpu.make_async_copy(rows.at[c], cols.at[z], local.at[4])
    same.start()
    late = []
    for d in (1, 3, 2):
        late.append(push(rows.at[c], cols.at[z], 2 * SIDE + d, (y * SIDE + lax.rem(z + d, SIDE), c)))
    for d in (4, 2, 6, 1, 3, 5, 7):
        late.append(push(rows.at[c], rows.at[c], 3 * SIDE + d, (r, lax.rem(c + d, COLS))))
    talk = []
    for d in range(1, COLS):
        talk.append(push(tallies.at[c], tallies.at[c], 3 * SIDE + COLS + d, (r, lax.rem(c + d, COLS))))
    for copy in late + talk:
        copy.start()
    for copy in taken:
        copy.wait()
    make_list(y, z, c, lens_ref, pairs_ref, inter_ref, stage_ref, list_ref, bounds_ref)
    for copy in talk:
        copy.wait_recv()
    for k in range(COLS):
        for yy in range(SIDE):
            for u in range(U):
                at = TALLY + k * 8 + yy * 2 + u // 4
                list_ref[at:at + 1, (u % 4) * 32:(u % 4) * 32 + 32] = tallies[k, yy, u]
    for copy in early + talk:
        copy.wait_send()
    for copy in late:
        copy.wait()
    same.wait()


def scatter_kernel(rows, cols, out, land, own, total, last, send, recv, local):
    r, c = lax.axis_index("row"), lax.axis_index("col")
    y, z = r // SIDE, lax.rem(r, SIDE)
    kept = [pltpu.make_async_copy(rows.at[c], own.at[0], local.at[0]),
            pltpu.make_async_copy(cols.at[z], own.at[1], local.at[1])]
    for copy in kept:
        copy.start()
    greet(r, c)
    copies = []

    def push(source, target, n, peer):
        return pltpu.make_async_remote_copy(source, target, send.at[n], recv.at[n],
                                            device_id=peer, device_id_type=MESH)

    for d in (1, 3, 2):
        to = lax.rem(z + d, SIDE)
        copies.append(push(cols.at[to], land.at[d - 1], d, (y * SIDE + to, c)))
    for d in (4, 2, 6, 1, 3, 5, 7):
        to = lax.rem(c + d, COLS)
        copies.append(push(rows.at[to], land.at[SIDE - 2 + d], SIDE + d, (r, to)))
    for copy in copies:
        copy.start()
    for copy in kept:
        copy.wait()
    for copy in copies:
        copy.wait_recv()
    for i in range(SIDE):
        sums = own[0, i] + own[1, i]
        for d in range(SIDE + COLS - 2):
            sums = sums + land[d, i]
        total[i] = sums
    second = []
    for d in (1, 3, 2):
        to = lax.rem(y + d, SIDE)
        second.append(push(total.at[to], last.at[d - 1], SIDE + COLS + d, (to * SIDE + z, c)))
    for copy in second:
        copy.start()
    out[y] = total[y]
    for d, copy in zip((1, 3, 2), second):
        copy.wait_recv()
        out[lax.rem(y + SIDE - d, SIDE)] = last[d - 1]
    for copy in copies + second:
        copy.wait_send()


def split3(x):
    a = x.astype(BF16).astype(F32)
    b = (x - a).astype(BF16).astype(F32)
    return a, b, (x - a) - b


def points_of(x, y, z):
    c = 0.75 - 0.25 * (x * x + y * y + z * z)
    return split3(x), split3(y), split3(z), split3(c)


def pair_kernel(list_ref, bounds_ref, rows_ref, cols_ref, prow_ref, pcol_ref,
                tile_ref, left_ref, lrow_ref, same_ref, differ_ref, arow_ref, acol_ref):
    z, c = list_ref[PLACE, 0], list_ref[PLACE, 1]
    starts, ends = bounds_ref[0], bounds_ref[1]
    lanes = iota((LABELS, BEADS), 1)
    eye = flag(iota((128, 128), 0) == iota((128, 128), 1))
    one = jnp.ones((8, 128), F32)
    nil = jnp.zeros((8, 128), F32)

    def hot_of(block):
        bead = lanes + block * BEADS
        return (bead >= starts) & (bead < ends)

    for v in range(SIDE):
        for u in range(U):
            for q in range(3):
                tile_ref[v, u, 8 * q:8 * q + 8] = nil
    for v in range(SIDE):
        tile_ref[v, :, 4, :] = one

    @pl.loop(0, COLS)
    def _(k):
        for yy in range(SIDE):
            parts = points_of(rows_ref[k, yy, 0], rows_ref[k, yy, 1], rows_ref[k, yy, 2])
            for q in range(3):
                for w in range(4):
                    value = parts[w][q]
                    tile_ref[yy, :, 8 * q + w, :] = 0.5 * value if w < 3 else value
        for yy in range(SIDE):
            for u in range(0, U, 2):
                fulls = []
                for i in range(2):
                    at = (k * SIDE + yy) * U + u + i
                    tiles = [tile_ref[yy, u + i, 8 * q:8 * q + 8] for q in range(3)]
                    full = jnp.concatenate([tiles[j] for j in (0, 0, 1, 0, 2, 1)], axis=0).astype(BF16)
                    hot = hot_of((u + i) * 128 + (4 * yy + z) * 8 + k)
                    fulls += [full, jnp.where(hot, 1.0, 0.0).astype(BF16), jnp.zeros((32, 128), BF16)]
                    lrow_ref[at] = jnp.concatenate(tiles[:2], axis=0).astype(BF16)
                flipped = lax.dot_general(eye, jnp.concatenate(fulls, axis=0), NT, preferred_element_type=F32)
                for i in range(2):
                    left_ref[(k * SIDE + yy) * U + u + i] = flipped[:, i * 128:i * 128 + 128].astype(BF16)

    for v in range(SIDE):
        tile_ref[v, :, 3, :] = one
        tile_ref[v, :, 11, :] = nil
        tile_ref[v, :, 19, :] = nil

    @pl.loop(0, SIDE)
    def _(zz):
        for yy in range(SIDE):
            parts = points_of(cols_ref[zz, yy, 0], cols_ref[zz, yy, 1], cols_ref[zz, yy, 2])
            for q in range(3):
                for w in range(4):
                    tile_ref[yy, :, 8 * q + (w if w < 3 else 4), :] = parts[w][q]
        for yy in range(SIDE):
            for u in range(U):
                at = u * ROWS + 4 * yy + zz
                tiles = [tile_ref[yy, u, 8 * q:8 * q + 8] for q in range(3)]
                full = jnp.concatenate([tiles[i] for i in (0, 1, 0, 2, 0, 1)], axis=0).astype(BF16)
                hot = hot_of(at * 8 + c)
                same_ref[at, 0:LABELS] = full
                differ_ref[at, 0:LABELS] = full
                same_ref[at, LABELS:] = jnp.where(hot, 0.0, -BIG).astype(BF16)
                differ_ref[at, LABELS:] = jnp.where(hot, -BIG, 0.0).astype(BF16)

    apart = jnp.concatenate([jnp.zeros((LABELS, BEADS), BF16), jnp.full((LABELS, BEADS), -BIG, BF16)], axis=0)
    for p in range(PAD):
        same_ref[NC + p] = apart
    differ_ref[NC] = apart

    @pl.loop(0, (NC + PAD) // 4)
    def _(i):
        for j in range(4):
            acol_ref[i * 4 + j] = nil

    @pl.loop(0, NR // 8)
    def _(i):
        for j in range(8):
            arow_ref[i * 8 + j] = nil

    triangle = iota((128, 128), 0) < iota((128, 128), 1)
    empty = jnp.zeros((16, 128), BF16)

    def finish(z, diagonal=False):
        t = jnp.tanh(z)
        if diagonal:
            t = jnp.concatenate([jnp.where(triangle, t[:, :128], -1.0), t[:, 128:]], axis=1)
        return jnp.sum(t, axis=0, keepdims=True), (1.0 - t * t).astype(BF16)

    def weigh(sums, n):
        expect = 0.5 + (0.5 * (16384.0 + jnp.sum(sums, axis=1, keepdims=True))) / 128.0
        n = jnp.full((1, 128), n, I32).astype(F32)
        return jnp.broadcast_to(1.0 - n / jnp.broadcast_to(expect, (1, 128)), (8, 128))

    def unit_drain(g, sums, at, start, counts):
        far = [same_ref[start + m, 0:16] for m in range(2)]
        o = jnp.dot(lrow_ref[at], g, preferred_element_type=F32)
        spread = jnp.concatenate([jnp.concatenate([far[0], empty], axis=1),
                                  jnp.concatenate([empty, far[1]], axis=1)], axis=0)
        p = lax.dot_general(spread, g, NT, preferred_element_type=F32)
        w = [weigh(sums[:, m * 128:m * 128 + 128], counts[m]) for m in range(2)]
        arow_ref[at] += w[0] * (p[0:8] + p[8:16]) + w[1] * (p[16:24] + p[24:32])
        for m in range(2):
            lane = slice(m * 128, m * 128 + 128)
            acol_ref[start + m] += w[m] * (o[0:8, lane] + o[8:16, lane])

    def run(unit_at, trips, diagonal):
        def body(it, held):
            for q in range(2):
                zs, now = [], []
                for i in range(WIDE):
                    entry = unit_at(it * 2 * WIDE + q * WIDE + i)
                    at, half = entry & (NR - 1), entry >> 8
                    k, u = at >> 5, at & 7
                    start = u * ROWS + 4 * ((at >> 3) & 3) + z + jnp.where(k > c, 1, 0) + 2 * half
                    start = jnp.where(entry < UNITS, start, NC)
                    lane = (at & 3) * 32 + ((c - k) & 7) + 16 * half
                    counts = [list_ref[TALLY + (at >> 2), lane + 8 * m] for m in range(2)]
                    right = jnp.concatenate([same_ref[start], same_ref[start + 1]], axis=1)
                    zs.append(jnp.dot(left_ref[at, :, 0:2 * LABELS], right, preferred_element_type=F32))
                    now.append((at, start, counts))
                for entry in held:
                    unit_drain(*entry)
                done = [finish(v, diagonal) for v in zs]
                held = [(done[i][1], done[i][0]) + now[i] for i in range(WIDE)]
            return held

        zero = jnp.int32(0)
        first = [(jnp.zeros((128, 256), BF16), jnp.zeros((1, 256), F32), zero, zero, [zero, zero])
                 for _ in range(WIDE)]
        for entry in lax.fori_loop(0, trips, body, first):
            unit_drain(*entry)

    run(lambda i: c * (SIDE * U) + i, SIDE * U // (2 * WIDE), True)
    run(lambda i: list_ref[UNIT + (i >> 7), i & 127], (list_ref[TOTALS, 1] + 2 * WIDE - 1) // (2 * WIDE), False)

    def listed_drain(held):
        for lo in range(0, WIDE, 2):
            pair = held[lo:lo + 2]
            near = jnp.concatenate([lrow_ref[p[2]] for p in pair], axis=0)
            far = jnp.concatenate([differ_ref[p[3], 0:16] for p in pair], axis=0)
            o = jnp.dot(near, jnp.concatenate([p[0] for p in pair], axis=1), preferred_element_type=F32)
            v = lax.dot_general(far, jnp.concatenate([p[0] for p in pair], axis=0), NT,
                                preferred_element_type=F32)
            for m, p in enumerate(pair):
                lane, at = slice(m * 128, m * 128 + 128), m * 16
                w = weigh(p[1], p[4])
                arow_ref[p[2]] += w * (v[at:at + 8, lane] + v[at + 8:at + 16, lane])
                acol_ref[p[3]] += w * (o[at:at + 8, lane] + o[at + 8:at + 16, lane])

    def listed_body(it, held):
        for q in range(2):
            zs, now = [], []
            for i in range(WIDE):
                slot = it * 2 * WIDE + q * WIDE + i
                line, lane = LISTED + (slot >> 7) * 8, slot & 127
                at, to, n = [list_ref[line + f, lane] for f in range(3)]
                zs.append(jnp.dot(left_ref[at, :, 0:2 * LABELS], differ_ref[to], preferred_element_type=F32))
                now.append((at, to, n))
            listed_drain(held)
            done = [finish(v) for v in zs]
            held = [(done[i][1], done[i][0]) + now[i] for i in range(WIDE)]
        return held

    zero = jnp.int32(0)
    first = [(jnp.zeros((128, 128), BF16), jnp.zeros((1, 128), F32), zero, zero, zero) for _ in range(WIDE)]
    listed_drain(lax.fori_loop(0, (list_ref[TOTALS, 0] + 2 * WIDE - 1) // (2 * WIDE), listed_body, first))

    @pl.loop(0, COLS)
    def _(k):
        for yy in range(SIDE):
            here = pl.ds((k * SIDE + yy) * U, U)
            mass = arow_ref[here, 3, :]
            for w in range(3):
                pulled = rows_ref[k, yy, w] * mass - arow_ref[here, w, :]
                prow_ref[k, yy, w] = pulled * (-1.0 / 512.0)

    @pl.loop(0, SIDE)
    def _(zz):
        for yy in range(SIDE):
            here = pl.ds(4 * yy + zz, U, stride=ROWS)
            mass = acol_ref[here, 4, :]
            for w in range(3):
                pulled = cols_ref[zz, yy, w] * mass - 2.0 * acol_ref[here, w, :]
                pcol_ref[zz, yy, w] = pulled * (-1.0 / 512.0)


def pairs_call(listing, bounds, rows, cols):
    return pl.pallas_call(
        pair_kernel,
        out_shape=[jax.ShapeDtypeStruct(rows.shape, F32), jax.ShapeDtypeStruct(cols.shape, F32)],
        in_specs=[SMEM] + [VMEM] * 3, out_specs=[VMEM] * 2,
        scratch_shapes=[
            pltpu.VMEM((SIDE, U, 24, BEADS), F32),
            pltpu.VMEM((NR, BEADS, 128), BF16),
            pltpu.VMEM((NR, 16, BEADS), BF16),
            pltpu.VMEM((NC + PAD + 2, 2 * LABELS, BEADS), BF16),
            pltpu.VMEM((NC + 1, 2 * LABELS, BEADS), BF16),
            pltpu.VMEM((NR, 8, BEADS), F32),
            pltpu.VMEM((NC + PAD + 2, 8, BEADS), F32),
        ],
        compiler_params=pltpu.CompilerParams(vmem_limit_bytes=32 << 20),
        name="pairs",
    )(listing, bounds, rows, cols)


def on_device(coords, chrom_lengths, band_counts, inter_pairs, inter_counts):
    part = coords.shape[1:]
    lens = chrom_lengths.reshape(1, -1)
    flipped = jnp.transpose(inter_pairs, (0, 2, 1))
    sems = 3 * SIDE + 2 * COLS
    rows, cols, listing, bounds = pl.pallas_call(
        gather_kernel,
        out_shape=[jax.ShapeDtypeStruct((COLS, SIDE) + part, F32), jax.ShapeDtypeStruct((SIDE, SIDE) + part, F32),
                   jax.ShapeDtypeStruct((LINES, 128), I32), jax.ShapeDtypeStruct((2, LABELS, BEADS), I32)],
        in_specs=[HBM] * 5, out_specs=[VMEM] * 4,
        scratch_shapes=[
            pltpu.VMEM(lens.shape, I32),
            pltpu.VMEM(flipped.shape[1:], I32),
            pltpu.VMEM(inter_counts.shape, I32),
            pltpu.VMEM((3, 32, 128), I32),
            pltpu.VMEM((COLS,) + band_counts.shape, I32),
            pltpu.SemaphoreType.DMA((sems,)),
            pltpu.SemaphoreType.DMA((sems,)),
            pltpu.SemaphoreType.DMA((6,)),
        ],
        compiler_params=pltpu.CompilerParams(collective_id=0, has_side_effects=True, vmem_limit_bytes=24 << 20),
        name="gather",
    )(*[pltpu.with_memory_space_constraint(v, pltpu.HBM)
        for v in (coords, band_counts, lens, flipped, inter_counts)])
    prow, pcol = pairs_call(listing, bounds, rows, cols)
    return pl.pallas_call(
        scatter_kernel,
        out_shape=jax.ShapeDtypeStruct(coords.shape, F32),
        in_specs=[VMEM] * 2, out_specs=VMEM,
        scratch_shapes=[
            pltpu.VMEM((SIDE + COLS - 2, SIDE) + part, F32),
            pltpu.VMEM((2, SIDE) + part, F32),
            pltpu.VMEM((SIDE,) + part, F32),
            pltpu.VMEM((SIDE - 1,) + part, F32),
            pltpu.SemaphoreType.DMA((2 * SIDE + COLS,)),
            pltpu.SemaphoreType.DMA((2 * SIDE + COLS,)),
            pltpu.SemaphoreType.DMA((2,)),
        ],
        compiler_params=pltpu.CompilerParams(collective_id=1, has_side_effects=True, vmem_limit_bytes=24 << 20),
        name="scatter",
    )(prow, pcol)


def solution(mesh):
    placed = (P(None, None, None, ("row", "col")), P(), P(None, None, ("row", "col"), None), P(), P())
    return jax.shard_map(on_device, mesh=mesh, in_specs=placed,
                         out_specs=P(None, None, None, ("row", "col")), check_vma=False)
```

```python
import jax
import jax.numpy as jnp
from jax import lax
from jax.experimental import pallas as pl
from jax.experimental.pallas import tpu as pltpu
from jax.sharding import PartitionSpec as P

MESH = pl.DeviceIdType.MESH
ROWS, COLS, SIDE = 16, 8, 4
U, BEADS = 8, 128
CAP = 256
LABELS = 48
NR, NC = SIDE * COLS * U, ROWS * U
UNITS = 2 * NR
PAD = 4
WIDE = 4
LONG, SHORT = 12, 2
BIG = 64.0
F32, BF16, I32 = jnp.float32, jnp.bfloat16, jnp.int32
HBM = pl.BlockSpec(memory_space=pltpu.HBM)
VMEM = pl.BlockSpec(memory_space=pltpu.VMEM)
SMEM = pl.BlockSpec(memory_space=pltpu.SMEM)
NT = (((1,), (1,)), ((), ()))
LISTED, TOTALS, WIDTHS, PLACE, TALLY, UNIT, LINES = 0, 16, 17, 19, 24, 88, 96


def iota(shape, axis):
    return lax.broadcasted_iota(I32, shape, axis)


def flag(x):
    return x.astype(F32).astype(BF16)


def chrom_bounds(lens_ref):
    lens = jnp.broadcast_to(lens_ref[...], (LABELS, lens_ref.shape[1]))
    sub, lane = iota(lens.shape, 0), iota(lens.shape, 1)
    ends = jnp.sum(jnp.where(lane <= sub, lens, 0), axis=1, keepdims=True)
    starts = jnp.sum(jnp.where(lane < sub, lens, 0), axis=1, keepdims=True)
    return starts, ends


def compact(mine, values, slots):
    count = mine.shape[0]
    a, b = iota((128, 128), 0), iota((128, 128), 1)
    within = jnp.dot(flag(mine), flag(a <= b), preferred_element_type=F32)
    total = jnp.dot(flag(mine), jnp.ones((128, 128), BF16), preferred_element_type=F32)
    lower = flag(iota((count, count), 1) < iota((count, count), 0))
    offset = jnp.dot(lower, total.astype(BF16), preferred_element_type=F32)
    place = jnp.where(mine, (offset + within).astype(I32) - 1, -1)
    values = [v.astype(F32) for v in values] + [mine.astype(F32)]
    slot = iota((slots, 128), 0)
    pad = jnp.zeros((16 - len(values), 128), F32)
    acc = jnp.zeros((16, slots), F32)
    for lo in range(0, count, 8):
        span = range(lo, min(lo + 8, count))
        hot = jnp.concatenate([flag(place[e:e + 1] == slot) for e in span], axis=1)
        rows = [jnp.concatenate([v[e:e + 1] for v in values] + [pad], axis=0) for e in span]
        acc = acc + lax.dot_general(jnp.concatenate(rows, axis=1).astype(BF16), hot, NT,
                                    preferred_element_type=F32)
    return acc[0:8]


def make_list(y, z, c, lens_ref, pairs_ref, count_ref, stage_ref, out_ref, bounds_ref):
    for t in range(32):
        lane = slice(t * 128, t * 128 + 128)
        stage_ref[0, t:t + 1, :] = pairs_ref[0:1, lane]
        stage_ref[1, t:t + 1, :] = pairs_ref[1:2, lane]
        block = count_ref[:, lane]
        stage_ref[2, t:t + 1, :] = jnp.sum(jnp.where(iota(block.shape, 0) == y, block, 0), axis=0, keepdims=True)
    first, second, counts = stage_ref[0], stage_ref[1], stage_ref[2]
    mine = (((first >> 3) & 3) == z) & ((second & 7) == c)
    at = (first & 7) * 32 + ((first >> 5) & 3) * 8 + (first >> 7)
    acc = compact(mine, [at, second >> 3, counts], CAP)
    spare = jnp.where(iota((8, CAP), 0) == 1, NC * (1.0 - acc[3:4]), 0.0)
    found = (acc + spare).astype(I32)
    out_ref[LISTED:LISTED + 8, :] = found[:, 0:128]
    out_ref[LISTED + 8:LISTED + 16, :] = found[:, 128:256]

    starts, ends = chrom_bounds(lens_ref)
    bounds_ref[0] = jnp.broadcast_to(starts, (LABELS, BEADS))
    bounds_ref[1] = jnp.broadcast_to(ends, (LABELS, BEADS))
    widths = []
    for i in range(2):
        at = iota((1, 128), 1) + i * 128
        k = at >> 5
        block = (at & 7) * 128 + (((at >> 3) & 3) * 4 + z) * 8 + k
        last = jnp.broadcast_to(block * 128 + 127, (LABELS, 128))
        stop = jnp.min(jnp.where(ends > last, ends, 1 << 20), axis=0, keepdims=True)
        far = jnp.minimum(jnp.minimum((stop - 1) >> 7, block + 31), 1023)
        widths.append(((far - block - ((c - k) & 7)) >> 3) + 1)
    width = jnp.concatenate(widths + widths, axis=0)
    entry = iota((4, 128), 0) * 128 + iota((4, 128), 1)
    near = (entry < NR) & (width > 0) & (((entry >> 5) & 7) != c)
    live = near | ((entry >= NR) & (width > 2))
    acc = compact(live, [entry >> 2, entry & 3], UNITS)
    units = acc[0:1] * 4.0 + acc[1:2] + UNITS * (1.0 - acc[2:3])
    for i in range(4):
        out_ref[UNIT + i:UNIT + i + 1, :] = units[:, i * 128:i * 128 + 128].astype(I32)
    out_ref[UNIT + 4:UNIT + 8, :] = jnp.zeros((4, 128), I32)
    listed = jnp.sum(found[3:4].astype(F32), axis=1, keepdims=True).astype(I32)
    active = jnp.sum(acc[2:3], axis=1, keepdims=True).astype(I32)
    lane = iota((1, 128), 1)
    out_ref[TOTALS:TOTALS + 1, :] = jnp.where(lane == 0, listed, active)
    out_ref[WIDTHS:WIDTHS + 2, :] = jnp.zeros((2, 128), I32)
    out_ref[PLACE:PLACE + 1, :] = jnp.where(lane == 0, z, c)
    out_ref[PLACE + 1:TALLY, :] = jnp.zeros((4, 128), I32)


def greet(r, c):
    y, z = r // SIDE, lax.rem(r, SIDE)
    peers = [(r, lax.rem(c + d, COLS)) for d in range(1, COLS)]
    peers += [(lax.rem(y + d, SIDE) * SIDE + z, c) for d in range(1, SIDE)]
    peers += [(y * SIDE + lax.rem(z + d, SIDE), c) for d in range(1, SIDE)]
    barrier = pltpu.get_barrier_semaphore()
    for peer in peers:
        pl.semaphore_signal(barrier, 1, device_id=peer, device_id_type=MESH)
    pl.semaphore_wait(barrier, len(peers))


def gather_kernel(coords, counts, lens, pairs, inter, rows, cols, list_ref, bounds_ref,
                  lens_ref, pairs_ref, inter_ref, stage_ref, tallies, send, recv, local):
    r, c = lax.axis_index("row"), lax.axis_index("col")
    y, z = r // SIDE, lax.rem(r, SIDE)
    taken = [pltpu.make_async_copy(pairs.at[y], pairs_ref, local.at[0]),
             pltpu.make_async_copy(inter, inter_ref, local.at[1]),
             pltpu.make_async_copy(lens, lens_ref, local.at[5])]
    kept = [pltpu.make_async_copy(coords.at[y], rows.at[c, y], local.at[2]),
            pltpu.make_async_copy(counts.at[y], tallies.at[c, y], local.at[3])]
    for copy in kept + taken:
        copy.start()
    greet(r, c)

    def push(source, target, n, peer):
        return pltpu.make_async_remote_copy(source, target, send.at[n], recv.at[n],
                                            device_id=peer, device_id_type=MESH)

    early = []
    for d in (1, 3, 2):
        to = lax.rem(y + d, SIDE)
        peer = (to * SIDE + z, c)
        early.append(push(coords.at[to], rows.at[c, y], d, peer))
        early.append(push(counts.at[to], tallies.at[c, y], SIDE + d, peer))
    for copy in early:
        copy.start()
    for copy in kept:
        copy.wait()
    for copy in early:
        copy.wait_recv()
    same = pltpu.make_async_copy(rows.at[c], cols.at[z], local.at[4])
    same.start()
    late = []
    for d in (1, 3, 2):
        late.append(push(rows.at[c], cols.at[z], 2 * SIDE + d, (y * SIDE + lax.rem(z + d, SIDE), c)))
    for d in (4, 2, 6, 1, 3, 5, 7):
        late.append(push(rows.at[c], rows.at[c], 3 * SIDE + d, (r, lax.rem(c + d, COLS))))
    talk = []
    for d in range(1, COLS):
        talk.append(push(tallies.at[c], tallies.at[c], 3 * SIDE + COLS + d, (r, lax.rem(c + d, COLS))))
    for copy in late + talk:
        copy.start()
    for copy in taken:
        copy.wait()
    make_list(y, z, c, lens_ref, pairs_ref, inter_ref, stage_ref, list_ref, bounds_ref)
    for copy in talk:
        copy.wait_recv()
    for k in range(COLS):
        for yy in range(SIDE):
            for u in range(U):
                at = TALLY + k * 8 + yy * 2 + u // 4
                list_ref[at:at + 1, (u % 4) * 32:(u % 4) * 32 + 32] = tallies[k, yy, u]
    for copy in early + talk:
        copy.wait_send()
    for copy in late:
        copy.wait()
    same.wait()


def scatter_kernel(rows, cols, out, land, own, total, last, send, recv, local):
    r, c = lax.axis_index("row"), lax.axis_index("col")
    y, z = r // SIDE, lax.rem(r, SIDE)
    kept = [pltpu.make_async_copy(rows.at[c], own.at[0], local.at[0]),
            pltpu.make_async_copy(cols.at[z], own.at[1], local.at[1])]
    for copy in kept:
        copy.start()
    greet(r, c)
    copies = []

    def push(source, target, n, peer):
        return pltpu.make_async_remote_copy(source, target, send.at[n], recv.at[n],
                                            device_id=peer, device_id_type=MESH)

    for d in (1, 3, 2):
        to = lax.rem(z + d, SIDE)
        copies.append(push(cols.at[to], land.at[d - 1], d, (y * SIDE + to, c)))
    for d in (4, 2, 6, 1, 3, 5, 7):
        to = lax.rem(c + d, COLS)
        copies.append(push(rows.at[to], land.at[SIDE - 2 + d], SIDE + d, (r, to)))
    for copy in copies:
        copy.start()
    for copy in kept:
        copy.wait()
    for copy in copies:
        copy.wait_recv()
    for i in range(SIDE):
        sums = own[0, i] + own[1, i]
        for d in range(SIDE + COLS - 2):
            sums = sums + land[d, i]
        total[i] = sums
    second = []
    for d in (1, 3, 2):
        to = lax.rem(y + d, SIDE)
        second.append(push(total.at[to], last.at[d - 1], SIDE + COLS + d, (to * SIDE + z, c)))
    for copy in second:
        copy.start()
    out[y] = total[y]
    for d, copy in zip((1, 3, 2), second):
        copy.wait_recv()
        out[lax.rem(y + SIDE - d, SIDE)] = last[d - 1]
    for copy in copies + second:
        copy.wait_send()


def split3(x):
    a = x.astype(BF16).astype(F32)
    b = (x - a).astype(BF16).astype(F32)
    return a, b, (x - a) - b


def points_of(x, y, z):
    c = 0.75 - 0.25 * (x * x + y * y + z * z)
    return split3(x), split3(y), split3(z), split3(c)


def pair_kernel(list_ref, bounds_ref, rows_ref, cols_ref, prow_ref, pcol_ref,
                tile_ref, left_ref, lrow_ref, same_ref, differ_ref, arow_ref, acol_ref):
    z, c = list_ref[PLACE, 0], list_ref[PLACE, 1]
    starts, ends = bounds_ref[0], bounds_ref[1]
    lanes = iota((LABELS, BEADS), 1)
    eye = flag(iota((128, 128), 0) == iota((128, 128), 1))
    one = jnp.ones((8, 128), F32)
    nil = jnp.zeros((8, 128), F32)

    def hot_of(block):
        bead = lanes + block * BEADS
        return (bead >= starts) & (bead < ends)

    for v in range(SIDE):
        for u in range(U):
            for q in range(3):
                tile_ref[v, u, 8 * q:8 * q + 8] = nil
    for v in range(SIDE):
        tile_ref[v, :, 4, :] = one

    @pl.loop(0, COLS)
    def _(k):
        for yy in range(SIDE):
            parts = points_of(rows_ref[k, yy, 0], rows_ref[k, yy, 1], rows_ref[k, yy, 2])
            for q in range(3):
                for w in range(4):
                    value = parts[w][q]
                    tile_ref[yy, :, 8 * q + w, :] = 0.5 * value if w < 3 else value
        for yy in range(SIDE):
            for u in range(0, U, 2):
                fulls = []
                for i in range(2):
                    at = (k * SIDE + yy) * U + u + i
                    tiles = [tile_ref[yy, u + i, 8 * q:8 * q + 8] for q in range(3)]
                    full = jnp.concatenate([tiles[j] for j in (0, 0, 1, 0, 2, 1)], axis=0).astype(BF16)
                    hot = hot_of((u + i) * 128 + (4 * yy + z) * 8 + k)
                    fulls += [full, jnp.where(hot, 1.0, 0.0).astype(BF16), jnp.zeros((32, 128), BF16)]
                    lrow_ref[at] = jnp.concatenate(tiles[:2], axis=0).astype(BF16)
                flipped = [jnp.concatenate(fulls[i * 3:i * 3 + 3], axis=0).T for i in range(2)]
                for i in range(2):
                    left_ref[(k * SIDE + yy) * U + u + i] = flipped[i]

    for v in range(SIDE):
        tile_ref[v, :, 3, :] = one
        tile_ref[v, :, 11, :] = nil
        tile_ref[v, :, 19, :] = nil

    @pl.loop(0, SIDE)
    def _(zz):
        for yy in range(SIDE):
            parts = points_of(cols_ref[zz, yy, 0], cols_ref[zz, yy, 1], cols_ref[zz, yy, 2])
            for q in range(3):
                for w in range(4):
                    tile_ref[yy, :, 8 * q + (w if w < 3 else 4), :] = parts[w][q]
        for yy in range(SIDE):
            for u in range(U):
                at = u * ROWS + 4 * yy + zz
                tiles = [tile_ref[yy, u, 8 * q:8 * q + 8] for q in range(3)]
                full = jnp.concatenate([tiles[i] for i in (0, 1, 0, 2, 0, 1)], axis=0).astype(BF16)
                hot = hot_of(at * 8 + c)
                same_ref[at, 0:LABELS] = full
                differ_ref[at, 0:LABELS] = full
                same_ref[at, LABELS:] = jnp.where(hot, 0.0, -BIG).astype(BF16)
                differ_ref[at, LABELS:] = jnp.where(hot, -BIG, 0.0).astype(BF16)

    apart = jnp.concatenate([jnp.zeros((LABELS, BEADS), BF16), jnp.full((LABELS, BEADS), -BIG, BF16)], axis=0)
    for p in range(PAD):
        same_ref[NC + p] = apart
    differ_ref[NC] = apart

    @pl.loop(0, (NC + PAD) // 4)
    def _(i):
        for j in range(4):
            acol_ref[i * 4 + j] = nil

    @pl.loop(0, NR // 8)
    def _(i):
        for j in range(8):
            arow_ref[i * 8 + j] = nil

    triangle = iota((128, 128), 0) < iota((128, 128), 1)
    empty = jnp.zeros((16, 128), BF16)

    def finish(z, diagonal=False):
        t = jnp.tanh(z)
        if diagonal:
            t = jnp.concatenate([jnp.where(triangle, t[:, :128], -1.0), t[:, 128:]], axis=1)
        return jnp.sum(t, axis=0, keepdims=True), (1.0 - t * t).astype(BF16)

    def weigh(sums, n):
        expect = 0.5 + (0.5 * (16384.0 + jnp.sum(sums, axis=1, keepdims=True))) / 128.0
        n = jnp.full((1, 128), n, I32).astype(F32)
        return jnp.broadcast_to(1.0 - n / jnp.broadcast_to(expect, (1, 128)), (8, 128))

    def unit_drain(g, sums, at, start, counts):
        far = [same_ref[start + m, 0:16] for m in range(2)]
        o = jnp.dot(lrow_ref[at], g, preferred_element_type=F32)
        spread = jnp.concatenate([jnp.concatenate([far[0], empty], axis=1),
                                  jnp.concatenate([empty, far[1]], axis=1)], axis=0)
        p = lax.dot_general(spread, g, NT, preferred_element_type=F32)
        w = [weigh(sums[:, m * 128:m * 128 + 128], counts[m]) for m in range(2)]
        arow_ref[at] += w[0] * (p[0:8] + p[8:16]) + w[1] * (p[16:24] + p[24:32])
        for m in range(2):
            lane = slice(m * 128, m * 128 + 128)
            acol_ref[start + m] += w[m] * (o[0:8, lane] + o[8:16, lane])

    def run(held, unit_at, trips, turns, diagonal):
        def body(it, held):
            for q in range(turns):
                zs, now = [], []
                for i in range(WIDE):
                    entry = unit_at((it * turns + q) * WIDE + i)
                    at, half = entry & (NR - 1), entry >> 8
                    k, u = at >> 5, at & 7
                    start = u * ROWS + 4 * ((at >> 3) & 3) + z + jnp.where(k > c, 1, 0) + 2 * half
                    start = jnp.where(entry < UNITS, start, NC)
                    lane = (at & 3) * 32 + ((c - k) & 7) + 16 * half
                    counts = [list_ref[TALLY + (at >> 2), lane + 8 * m] for m in range(2)]
                    right = jnp.concatenate([same_ref[start], same_ref[start + 1]], axis=1)
                    zs.append(jnp.dot(left_ref[at, :, 0:2 * LABELS], right, preferred_element_type=F32))
                    now.append((at, start, counts))
                for entry in held:
                    unit_drain(*entry)
                done = [finish(v, diagonal) for v in zs]
                held = [(done[i][1], done[i][0]) + now[i] for i in range(WIDE)]
            return held

        return lax.fori_loop(0, trips, body, held)

    def split(count):
        whole = count // (WIDE * LONG)
        done = whole * (WIDE * LONG)
        return whole, done, (count - done + WIDE * SHORT - 1) // (WIDE * SHORT)

    zero = jnp.int32(0)
    held = [(jnp.zeros((128, 256), BF16), jnp.zeros((1, 256), F32), zero, zero, [zero, zero])
            for _ in range(WIDE)]
    held = run(held, lambda i: c * (SIDE * U) + i, 1, SIDE * U // WIDE, True)
    whole, done, rest = split(list_ref[TOTALS, 1])
    held = run(held, lambda i: list_ref[UNIT + (i >> 7), i & 127], whole, LONG, False)
    held = run(held, lambda i: list_ref[UNIT + ((i + done) >> 7), (i + done) & 127], rest, SHORT, False)
    for entry in held:
        unit_drain(*entry)

    def listed_drain(held):
        for lo in range(0, WIDE, 2):
            pair = held[lo:lo + 2]
            near = jnp.concatenate([lrow_ref[p[2]] for p in pair], axis=0)
            far = jnp.concatenate([differ_ref[p[3], 0:16] for p in pair], axis=0)
            o = jnp.dot(near, jnp.concatenate([p[0] for p in pair], axis=1), preferred_element_type=F32)
            v = lax.dot_general(far, jnp.concatenate([p[0] for p in pair], axis=0), NT,
                                preferred_element_type=F32)
            for m, p in enumerate(pair):
                lane, at = slice(m * 128, m * 128 + 128), m * 16
                w = weigh(p[1], p[4])
                arow_ref[p[2]] += w * (v[at:at + 8, lane] + v[at + 8:at + 16, lane])
                acol_ref[p[3]] += w * (o[at:at + 8, lane] + o[at + 8:at + 16, lane])

    def listed_run(held, offset, trips, laps):
        def body(it, held):
            for q in range(laps):
                zs, now = [], []
                for i in range(WIDE):
                    slot = offset + (it * laps + q) * WIDE + i
                    line, lane = LISTED + (slot >> 7) * 8, slot & 127
                    at, to, n = [list_ref[line + f, lane] for f in range(3)]
                    zs.append(jnp.dot(left_ref[at, :, 0:2 * LABELS], differ_ref[to], preferred_element_type=F32))
                    now.append((at, to, n))
                listed_drain(held)
                done = [finish(v) for v in zs]
                held = [(done[i][1], done[i][0]) + now[i] for i in range(WIDE)]
            return held

        return lax.fori_loop(0, trips, body, held)

    held = [(jnp.zeros((128, 128), BF16), jnp.zeros((1, 128), F32), zero, zero, zero) for _ in range(WIDE)]
    whole, done, rest = split(list_ref[TOTALS, 0])
    held = listed_run(held, 0, whole, LONG)
    listed_drain(listed_run(held, done, rest, SHORT))

    @pl.loop(0, COLS)
    def _(k):
        for yy in range(SIDE):
            here = pl.ds((k * SIDE + yy) * U, U)
            mass = arow_ref[here, 3, :]
            for w in range(3):
                pulled = rows_ref[k, yy, w] * mass - arow_ref[here, w, :]
                prow_ref[k, yy, w] = pulled * (-1.0 / 512.0)

    @pl.loop(0, SIDE)
    def _(zz):
        for yy in range(SIDE):
            here = pl.ds(4 * yy + zz, U, stride=ROWS)
            mass = acol_ref[here, 4, :]
            for w in range(3):
                pulled = cols_ref[zz, yy, w] * mass - 2.0 * acol_ref[here, w, :]
                pcol_ref[zz, yy, w] = pulled * (-1.0 / 512.0)


def pairs_call(listing, bounds, rows, cols):
    return pl.pallas_call(
        pair_kernel,
        out_shape=[jax.ShapeDtypeStruct(rows.shape, F32), jax.ShapeDtypeStruct(cols.shape, F32)],
        in_specs=[SMEM] + [VMEM] * 3, out_specs=[VMEM] * 2,
        scratch_shapes=[
            pltpu.VMEM((SIDE, U, 24, BEADS), F32),
            pltpu.VMEM((NR, BEADS, 128), BF16),
            pltpu.VMEM((NR, 16, BEADS), BF16),
            pltpu.VMEM((NC + PAD + 2, 2 * LABELS, BEADS), BF16),
            pltpu.VMEM((NC + 1, 2 * LABELS, BEADS), BF16),
            pltpu.VMEM((NR, 8, BEADS), F32),
            pltpu.VMEM((NC + PAD + 2, 8, BEADS), F32),
        ],
        compiler_params=pltpu.CompilerParams(vmem_limit_bytes=32 << 20),
        name="pairs",
    )(listing, bounds, rows, cols)


def on_device(coords, chrom_lengths, band_counts, inter_pairs, inter_counts):
    part = coords.shape[1:]
    lens = chrom_lengths.reshape(1, -1)
    flipped = jnp.transpose(inter_pairs, (0, 2, 1))
    sems = 3 * SIDE + 2 * COLS
    rows, cols, listing, bounds = pl.pallas_call(
        gather_kernel,
        out_shape=[jax.ShapeDtypeStruct((COLS, SIDE) + part, F32), jax.ShapeDtypeStruct((SIDE, SIDE) + part, F32),
                   jax.ShapeDtypeStruct((LINES, 128), I32), jax.ShapeDtypeStruct((2, LABELS, BEADS), I32)],
        in_specs=[HBM] * 5, out_specs=[VMEM] * 4,
        scratch_shapes=[
            pltpu.VMEM(lens.shape, I32),
            pltpu.VMEM(flipped.shape[1:], I32),
            pltpu.VMEM(inter_counts.shape, I32),
            pltpu.VMEM((3, 32, 128), I32),
            pltpu.VMEM((COLS,) + band_counts.shape, I32),
            pltpu.SemaphoreType.DMA((sems,)),
            pltpu.SemaphoreType.DMA((sems,)),
            pltpu.SemaphoreType.DMA((6,)),
        ],
        compiler_params=pltpu.CompilerParams(collective_id=0, has_side_effects=True, vmem_limit_bytes=24 << 20),
        name="gather",
    )(*[pltpu.with_memory_space_constraint(v, pltpu.HBM)
        for v in (coords, band_counts, lens, flipped, inter_counts)])
    prow, pcol = pairs_call(listing, bounds, rows, cols)
    return pl.pallas_call(
        scatter_kernel,
        out_shape=jax.ShapeDtypeStruct(coords.shape, F32),
        in_specs=[VMEM] * 2, out_specs=VMEM,
        scratch_shapes=[
            pltpu.VMEM((SIDE + COLS - 2, SIDE) + part, F32),
            pltpu.VMEM((2, SIDE) + part, F32),
            pltpu.VMEM((SIDE,) + part, F32),
            pltpu.VMEM((SIDE - 1,) + part, F32),
            pltpu.SemaphoreType.DMA((2 * SIDE + COLS,)),
            pltpu.SemaphoreType.DMA((2 * SIDE + COLS,)),
            pltpu.SemaphoreType.DMA((2,)),
        ],
        compiler_params=pltpu.CompilerParams(collective_id=1, has_side_effects=True, vmem_limit_bytes=24 << 20),
        name="scatter",
    )(prow, pcol)


def solution(mesh):
    placed = (P(None, None, None, ("row", "col")), P(), P(None, None, ("row", "col"), None), P(), P())
    return jax.shard_map(on_device, mesh=mesh, in_specs=placed,
                         out_specs=P(None, None, None, ("row", "col")), check_vma=False)
```

```python
import jax
import jax.numpy as jnp
from jax import lax
from jax.experimental import pallas as pl
from jax.experimental.pallas import tpu as pltpu
from jax.sharding import PartitionSpec as P

MESH = pl.DeviceIdType.MESH
ROWS, COLS, SIDE = 16, 8, 4
U, BEADS = 8, 128
CAP = 256
LABELS = 48
NR, NC = SIDE * COLS * U, ROWS * U
UNITS = 2 * NR
PAD = 4
WIDE = 4
LONG, SHORT = 12, 2
BIG = 64.0
F32, BF16, I32 = jnp.float32, jnp.bfloat16, jnp.int32
HBM = pl.BlockSpec(memory_space=pltpu.HBM)
VMEM = pl.BlockSpec(memory_space=pltpu.VMEM)
SMEM = pl.BlockSpec(memory_space=pltpu.SMEM)
NT = (((1,), (1,)), ((), ()))
LISTED, TOTALS, WIDTHS, PLACE, TALLY, UNIT, LINES = 0, 16, 17, 19, 24, 88, 96


def iota(shape, axis):
    return lax.broadcasted_iota(I32, shape, axis)


def flag(x):
    return x.astype(F32).astype(BF16)


def chrom_bounds(lens_ref):
    lens = jnp.broadcast_to(lens_ref[...], (LABELS, lens_ref.shape[1]))
    sub, lane = iota(lens.shape, 0), iota(lens.shape, 1)
    ends = jnp.sum(jnp.where(lane <= sub, lens, 0), axis=1, keepdims=True)
    starts = jnp.sum(jnp.where(lane < sub, lens, 0), axis=1, keepdims=True)
    return starts, ends


def compact(mine, values, slots):
    count = mine.shape[0]
    a, b = iota((128, 128), 0), iota((128, 128), 1)
    within = jnp.dot(flag(mine), flag(a <= b), preferred_element_type=F32)
    total = jnp.dot(flag(mine), jnp.ones((128, 128), BF16), preferred_element_type=F32)
    lower = flag(iota((count, count), 1) < iota((count, count), 0))
    offset = jnp.dot(lower, total.astype(BF16), preferred_element_type=F32)
    place = jnp.where(mine, (offset + within).astype(I32) - 1, -1)
    values = [v.astype(F32) for v in values] + [mine.astype(F32)]
    slot = iota((slots, 128), 0)
    pad = jnp.zeros((16 - len(values), 128), F32)
    acc = jnp.zeros((16, slots), F32)
    for lo in range(0, count, 8):
        span = range(lo, min(lo + 8, count))
        hot = jnp.concatenate([flag(place[e:e + 1] == slot) for e in span], axis=1)
        rows = [jnp.concatenate([v[e:e + 1] for v in values] + [pad], axis=0) for e in span]
        acc = acc + lax.dot_general(jnp.concatenate(rows, axis=1).astype(BF16), hot, NT,
                                    preferred_element_type=F32)
    return acc[0:8]


def make_list(y, z, c, lens_ref, pairs_ref, count_ref, stage_ref, out_ref, bounds_ref):
    for t in range(32):
        lane = slice(t * 128, t * 128 + 128)
        stage_ref[0, t:t + 1, :] = pairs_ref[0:1, lane]
        stage_ref[1, t:t + 1, :] = pairs_ref[1:2, lane]
        block = count_ref[:, lane]
        stage_ref[2, t:t + 1, :] = jnp.sum(jnp.where(iota(block.shape, 0) == y, block, 0), axis=0, keepdims=True)
    first, second, counts = stage_ref[0], stage_ref[1], stage_ref[2]
    mine = (((first >> 3) & 3) == z) & ((second & 7) == c)
    at = (first & 7) * 32 + ((first >> 5) & 3) * 8 + (first >> 7)
    acc = compact(mine, [at, second >> 3, counts], CAP)
    spare = jnp.where(iota((8, CAP), 0) == 1, NC * (1.0 - acc[3:4]), 0.0)
    found = (acc + spare).astype(I32)
    out_ref[LISTED:LISTED + 8, :] = found[:, 0:128]
    out_ref[LISTED + 8:LISTED + 16, :] = found[:, 128:256]

    starts, ends = chrom_bounds(lens_ref)
    bounds_ref[0] = jnp.broadcast_to(starts, (LABELS, BEADS))
    bounds_ref[1] = jnp.broadcast_to(ends, (LABELS, BEADS))
    widths = []
    for i in range(2):
        at = iota((1, 128), 1) + i * 128
        k = at >> 5
        block = (at & 7) * 128 + (((at >> 3) & 3) * 4 + z) * 8 + k
        last = jnp.broadcast_to(block * 128 + 127, (LABELS, 128))
        stop = jnp.min(jnp.where(ends > last, ends, 1 << 20), axis=0, keepdims=True)
        far = jnp.minimum(jnp.minimum((stop - 1) >> 7, block + 31), 1023)
        widths.append(((far - block - ((c - k) & 7)) >> 3) + 1)
    width = jnp.concatenate(widths + widths, axis=0)
    entry = iota((4, 128), 0) * 128 + iota((4, 128), 1)
    near = (entry < NR) & (width > 0) & (((entry >> 5) & 7) != c)
    live = near | ((entry >= NR) & (width > 2))
    acc = compact(live, [entry >> 2, entry & 3], UNITS)
    units = acc[0:1] * 4.0 + acc[1:2] + UNITS * (1.0 - acc[2:3])
    for i in range(4):
        out_ref[UNIT + i:UNIT + i + 1, :] = units[:, i * 128:i * 128 + 128].astype(I32)
    out_ref[UNIT + 4:UNIT + 8, :] = jnp.zeros((4, 128), I32)
    listed = jnp.sum(found[3:4].astype(F32), axis=1, keepdims=True).astype(I32)
    active = jnp.sum(acc[2:3], axis=1, keepdims=True).astype(I32)
    lane = iota((1, 128), 1)
    out_ref[TOTALS:TOTALS + 1, :] = jnp.where(lane == 0, listed, active)
    out_ref[WIDTHS:WIDTHS + 2, :] = jnp.zeros((2, 128), I32)
    out_ref[PLACE:PLACE + 1, :] = jnp.where(lane == 0, z, c)
    out_ref[PLACE + 1:TALLY, :] = jnp.zeros((4, 128), I32)


def greet(r, c):
    y, z = r // SIDE, lax.rem(r, SIDE)
    peers = [(r, lax.rem(c + d, COLS)) for d in range(1, COLS)]
    peers += [(lax.rem(y + d, SIDE) * SIDE + z, c) for d in range(1, SIDE)]
    peers += [(y * SIDE + lax.rem(z + d, SIDE), c) for d in range(1, SIDE)]
    barrier = pltpu.get_barrier_semaphore()
    for peer in peers:
        pl.semaphore_signal(barrier, 1, device_id=peer, device_id_type=MESH)
    pl.semaphore_wait(barrier, len(peers))


def gather_kernel(coords, counts, lens, pairs, inter, rows, cols, list_ref, bounds_ref,
                  lens_ref, pairs_ref, inter_ref, stage_ref, tallies, send, recv, local):
    r, c = lax.axis_index("row"), lax.axis_index("col")
    y, z = r // SIDE, lax.rem(r, SIDE)
    taken = [pltpu.make_async_copy(pairs.at[y], pairs_ref, local.at[0]),
             pltpu.make_async_copy(inter, inter_ref, local.at[1]),
             pltpu.make_async_copy(lens, lens_ref, local.at[5])]
    kept = [pltpu.make_async_copy(coords.at[y], rows.at[c, y], local.at[2]),
            pltpu.make_async_copy(counts.at[y], tallies.at[c, y], local.at[3])]
    for copy in kept + taken:
        copy.start()
    greet(r, c)

    def push(source, target, n, peer):
        return pltpu.make_async_remote_copy(source, target, send.at[n], recv.at[n],
                                            device_id=peer, device_id_type=MESH)

    early, talks = [], []
    for d in (1, 3, 2):
        to = lax.rem(y + d, SIDE)
        peer = (to * SIDE + z, c)
        early.append(push(coords.at[to], rows.at[c, y], d, peer))
        talks.append(push(counts.at[to], tallies.at[c, y], SIDE + d, peer))
    for copy in early:
        copy.start()
    late = []

    def spread(step):
        part = lax.rem(y + SIDE - step, SIDE)
        source = rows.at[c, part] if step else coords.at[y]
        base = 2 * SIDE + COLS + step * (SIDE + COLS)
        copies = [push(source, rows.at[c, part], base + SIDE + d, (r, lax.rem(c + d, COLS)))
                  for d in (4, 2, 6, 1, 3, 5, 7)]
        copies += [push(source, cols.at[z, part], base + d, (y * SIDE + lax.rem(z + d, SIDE), c))
                   for d in (1, 3, 2)]
        for copy in copies:
            copy.start()
        late.extend(copies)

    spread(0)
    for copy in talks:
        copy.start()
    for step, copy in zip((1, 3, 2), early):
        copy.wait_recv()
        spread(step)
    for copy in kept:
        copy.wait()
    same = pltpu.make_async_copy(rows.at[c], cols.at[z], local.at[4])
    same.start()
    for copy in talks:
        copy.wait_recv()
    talk = [push(tallies.at[c], tallies.at[c], 2 * SIDE + d, (r, lax.rem(c + d, COLS))) for d in range(1, COLS)]
    for copy in talk:
        copy.start()
    for copy in taken:
        copy.wait()
    make_list(y, z, c, lens_ref, pairs_ref, inter_ref, stage_ref, list_ref, bounds_ref)
    for copy in talk:
        copy.wait_recv()
    for k in range(COLS):
        for yy in range(SIDE):
            for u in range(U):
                at = TALLY + k * 8 + yy * 2 + u // 4
                list_ref[at:at + 1, (u % 4) * 32:(u % 4) * 32 + 32] = tallies[k, yy, u]
    for copy in early + talks + talk:
        copy.wait_send()
    for copy in late:
        copy.wait()
    same.wait()


def scatter_kernel(rows, cols, out, land, own, total, last, send, recv, local):
    r, c = lax.axis_index("row"), lax.axis_index("col")
    y, z = r // SIDE, lax.rem(r, SIDE)
    kept = [pltpu.make_async_copy(rows.at[c], own.at[0], local.at[0]),
            pltpu.make_async_copy(cols.at[z], own.at[1], local.at[1])]
    for copy in kept:
        copy.start()
    greet(r, c)
    copies = []

    def push(source, target, n, peer):
        return pltpu.make_async_remote_copy(source, target, send.at[n], recv.at[n],
                                            device_id=peer, device_id_type=MESH)

    order = (2, 1, 3, 0)
    for turn in order:
        part, base = lax.rem(y + turn, SIDE), turn * (SIDE + COLS)
        group = []
        for d in (4, 2, 6, 1, 3, 5, 7):
            to = lax.rem(c + d, COLS)
            group.append(push(rows.at[to, part], land.at[SIDE - 2 + d, part], base + SIDE + d, (r, to)))
        for d in (1, 3, 2):
            to = lax.rem(z + d, SIDE)
            group.append(push(cols.at[to, part], land.at[d - 1, part], base + d, (y * SIDE + to, c)))
        for copy in group:
            copy.start()
        copies.append(group)
    for copy in kept:
        copy.wait()
    second = []
    for turn, group in zip(order, copies):
        part = lax.rem(y + turn, SIDE)
        for copy in group:
            copy.wait_recv()
        sums = [own[0, part] + own[1, part]] + [land[d, part] for d in range(SIDE + COLS - 2)]
        while len(sums) > 1:
            sums = [a + b for a, b in zip(sums[::2], sums[1::2])] + sums[len(sums) - len(sums) % 2:]
        if turn == 0:
            out[y] = sums[0]
        else:
            total[turn - 1] = sums[0]
            copy = push(total.at[turn - 1], last.at[turn - 1], SIDE * (SIDE + COLS) + turn, (part * SIDE + z, c))
            copy.start()
            second.append((turn, copy))
    for turn, copy in second:
        copy.wait_recv()
        out[lax.rem(y + SIDE - turn, SIDE)] = last[turn - 1]
    for copy in [copy for group in copies for copy in group] + [copy for _, copy in second]:
        copy.wait_send()


def split3(x):
    a = x.astype(BF16).astype(F32)
    b = (x - a).astype(BF16).astype(F32)
    return a, b, (x - a) - b


def points_of(x, y, z):
    c = 0.75 - 0.25 * (x * x + y * y + z * z)
    return split3(x), split3(y), split3(z), split3(c)


def pair_kernel(list_ref, bounds_ref, rows_ref, cols_ref, prow_ref, pcol_ref,
                tile_ref, left_ref, lrow_ref, same_ref, differ_ref, arow_ref, acol_ref):
    z, c = list_ref[PLACE, 0], list_ref[PLACE, 1]
    starts, ends = bounds_ref[0], bounds_ref[1]
    lanes = iota((LABELS, BEADS), 1)
    eye = flag(iota((128, 128), 0) == iota((128, 128), 1))
    one = jnp.ones((8, 128), F32)
    nil = jnp.zeros((8, 128), F32)

    def hot_of(block):
        bead = lanes + block * BEADS
        return (bead >= starts) & (bead < ends)

    for v in range(SIDE):
        for u in range(U):
            for q in range(3):
                tile_ref[v, u, 8 * q:8 * q + 8] = nil
    for v in range(SIDE):
        tile_ref[v, :, 4, :] = one

    @pl.loop(0, COLS)
    def _(k):
        for yy in range(SIDE):
            parts = points_of(rows_ref[k, yy, 0], rows_ref[k, yy, 1], rows_ref[k, yy, 2])
            for q in range(3):
                for w in range(4):
                    value = parts[w][q]
                    tile_ref[yy, :, 8 * q + w, :] = 0.5 * value if w < 3 else value
        for yy in range(SIDE):
            for u in range(0, U, 2):
                fulls = []
                for i in range(2):
                    at = (k * SIDE + yy) * U + u + i
                    tiles = [tile_ref[yy, u + i, 8 * q:8 * q + 8] for q in range(3)]
                    full = jnp.concatenate([tiles[j] for j in (0, 0, 1, 0, 2, 1)], axis=0).astype(BF16)
                    hot = hot_of((u + i) * 128 + (4 * yy + z) * 8 + k)
                    fulls += [full, jnp.where(hot, 1.0, 0.0).astype(BF16), jnp.zeros((32, 128), BF16)]
                    lrow_ref[at] = jnp.concatenate(tiles[:2], axis=0).astype(BF16)
                flipped = [jnp.concatenate(fulls[i * 3:i * 3 + 3], axis=0).T for i in range(2)]
                for i in range(2):
                    left_ref[(k * SIDE + yy) * U + u + i] = flipped[i]

    for v in range(SIDE):
        tile_ref[v, :, 3, :] = one
        tile_ref[v, :, 11, :] = nil
        tile_ref[v, :, 19, :] = nil

    @pl.loop(0, SIDE)
    def _(zz):
        for yy in range(SIDE):
            parts = points_of(cols_ref[zz, yy, 0], cols_ref[zz, yy, 1], cols_ref[zz, yy, 2])
            for q in range(3):
                for w in range(4):
                    tile_ref[yy, :, 8 * q + (w if w < 3 else 4), :] = parts[w][q]
        for yy in range(SIDE):
            for u in range(U):
                at = u * ROWS + 4 * yy + zz
                tiles = [tile_ref[yy, u, 8 * q:8 * q + 8] for q in range(3)]
                full = jnp.concatenate([tiles[i] for i in (0, 1, 0, 2, 0, 1)], axis=0).astype(BF16)
                hot = hot_of(at * 8 + c)
                same_ref[at, 0:LABELS] = full
                differ_ref[at, 0:LABELS] = full
                same_ref[at, LABELS:] = jnp.where(hot, 0.0, -BIG).astype(BF16)
                differ_ref[at, LABELS:] = jnp.where(hot, -BIG, 0.0).astype(BF16)

    apart = jnp.concatenate([jnp.zeros((LABELS, BEADS), BF16), jnp.full((LABELS, BEADS), -BIG, BF16)], axis=0)
    for p in range(PAD):
        same_ref[NC + p] = apart
    differ_ref[NC] = apart

    @pl.loop(0, (NC + PAD) // 4)
    def _(i):
        for j in range(4):
            acol_ref[i * 4 + j] = nil

    @pl.loop(0, NR // 8)
    def _(i):
        for j in range(8):
            arow_ref[i * 8 + j] = nil

    triangle = iota((128, 128), 0) < iota((128, 128), 1)
    empty = jnp.zeros((16, 128), BF16)

    def finish(z, diagonal=False):
        t = jnp.tanh(z)
        if diagonal:
            t = jnp.concatenate([jnp.where(triangle, t[:, :128], -1.0), t[:, 128:]], axis=1)
        return jnp.sum(t, axis=0, keepdims=True), (1.0 - t * t).astype(BF16)

    def weigh(sums, n):
        expect = 0.5 + (0.5 * (16384.0 + jnp.sum(sums, axis=1, keepdims=True))) / 128.0
        n = jnp.full((1, 128), n, I32).astype(F32)
        return jnp.broadcast_to(1.0 - n / jnp.broadcast_to(expect, (1, 128)), (8, 128))

    def unit_drain(g, sums, at, start, counts):
        far = [same_ref[start + m, 0:16] for m in range(2)]
        o = jnp.dot(lrow_ref[at], g, preferred_element_type=F32)
        spread = jnp.concatenate([jnp.concatenate([far[0], empty], axis=1),
                                  jnp.concatenate([empty, far[1]], axis=1)], axis=0)
        p = lax.dot_general(spread, g, NT, preferred_element_type=F32)
        w = [weigh(sums[:, m * 128:m * 128 + 128], counts[m]) for m in range(2)]
        arow_ref[at] += w[0] * (p[0:8] + p[8:16]) + w[1] * (p[16:24] + p[24:32])
        for m in range(2):
            lane = slice(m * 128, m * 128 + 128)
            acol_ref[start + m] += w[m] * (o[0:8, lane] + o[8:16, lane])

    def run(held, unit_at, trips, turns, diagonal):
        def body(it, held):
            for q in range(turns):
                zs, now = [], []
                for i in range(WIDE):
                    entry = unit_at((it * turns + q) * WIDE + i)
                    at, half = entry & (NR - 1), entry >> 8
                    k, u = at >> 5, at & 7
                    start = u * ROWS + 4 * ((at >> 3) & 3) + z + jnp.where(k > c, 1, 0) + 2 * half
                    start = jnp.where(entry < UNITS, start, NC)
                    lane = (at & 3) * 32 + ((c - k) & 7) + 16 * half
                    counts = [list_ref[TALLY + (at >> 2), lane + 8 * m] for m in range(2)]
                    right = jnp.concatenate([same_ref[start], same_ref[start + 1]], axis=1)
                    zs.append(jnp.dot(left_ref[at, :, 0:2 * LABELS], right, preferred_element_type=F32))
                    now.append((at, start, counts))
                for entry in held:
                    unit_drain(*entry)
                done = [finish(v, diagonal) for v in zs]
                held = [(done[i][1], done[i][0]) + now[i] for i in range(WIDE)]
            return held

        return lax.fori_loop(0, trips, body, held)

    def split(count):
        whole = count // (WIDE * LONG)
        done = whole * (WIDE * LONG)
        return whole, done, (count - done + WIDE * SHORT - 1) // (WIDE * SHORT)

    zero = jnp.int32(0)
    held = [(jnp.zeros((128, 256), BF16), jnp.zeros((1, 256), F32), zero, zero, [zero, zero])
            for _ in range(WIDE)]
    held = run(held, lambda i: c * (SIDE * U) + i, 1, SIDE * U // WIDE, True)
    whole, done, rest = split(list_ref[TOTALS, 1])
    held = run(held, lambda i: list_ref[UNIT + (i >> 7), i & 127], whole, LONG, False)
    held = run(held, lambda i: list_ref[UNIT + ((i + done) >> 7), (i + done) & 127], rest, SHORT, False)
    for entry in held:
        unit_drain(*entry)

    def listed_drain(held):
        for lo in range(0, WIDE, 2):
            pair = held[lo:lo + 2]
            near = jnp.concatenate([lrow_ref[p[2]] for p in pair], axis=0)
            far = jnp.concatenate([differ_ref[p[3], 0:16] for p in pair], axis=0)
            o = jnp.dot(near, jnp.concatenate([p[0] for p in pair], axis=1), preferred_element_type=F32)
            v = lax.dot_general(far, jnp.concatenate([p[0] for p in pair], axis=0), NT,
                                preferred_element_type=F32)
            for m, p in enumerate(pair):
                lane, at = slice(m * 128, m * 128 + 128), m * 16
                w = weigh(p[1], p[4])
                arow_ref[p[2]] += w * (v[at:at + 8, lane] + v[at + 8:at + 16, lane])
                acol_ref[p[3]] += w * (o[at:at + 8, lane] + o[at + 8:at + 16, lane])

    def listed_run(held, offset, trips, laps):
        def body(it, held):
            for q in range(laps):
                zs, now = [], []
                for i in range(WIDE):
                    slot = offset + (it * laps + q) * WIDE + i
                    line, lane = LISTED + (slot >> 7) * 8, slot & 127
                    at, to, n = [list_ref[line + f, lane] for f in range(3)]
                    zs.append(jnp.dot(left_ref[at, :, 0:2 * LABELS], differ_ref[to], preferred_element_type=F32))
                    now.append((at, to, n))
                listed_drain(held)
                done = [finish(v) for v in zs]
                held = [(done[i][1], done[i][0]) + now[i] for i in range(WIDE)]
            return held

        return lax.fori_loop(0, trips, body, held)

    held = [(jnp.zeros((128, 128), BF16), jnp.zeros((1, 128), F32), zero, zero, zero) for _ in range(WIDE)]
    whole, done, rest = split(list_ref[TOTALS, 0])
    held = listed_run(held, 0, whole, LONG)
    listed_drain(listed_run(held, done, rest, SHORT))

    @pl.loop(0, COLS)
    def _(k):
        for yy in range(SIDE):
            here = pl.ds((k * SIDE + yy) * U, U)
            mass = arow_ref[here, 3, :]
            for w in range(3):
                pulled = rows_ref[k, yy, w] * mass - arow_ref[here, w, :]
                prow_ref[k, yy, w] = pulled * (-1.0 / 512.0)

    @pl.loop(0, SIDE)
    def _(zz):
        for yy in range(SIDE):
            here = pl.ds(4 * yy + zz, U, stride=ROWS)
            mass = acol_ref[here, 4, :]
            for w in range(3):
                pulled = cols_ref[zz, yy, w] * mass - 2.0 * acol_ref[here, w, :]
                pcol_ref[zz, yy, w] = pulled * (-1.0 / 512.0)


def pairs_call(listing, bounds, rows, cols):
    return pl.pallas_call(
        pair_kernel,
        out_shape=[jax.ShapeDtypeStruct(rows.shape, F32), jax.ShapeDtypeStruct(cols.shape, F32)],
        in_specs=[SMEM] + [VMEM] * 3, out_specs=[VMEM] * 2,
        scratch_shapes=[
            pltpu.VMEM((SIDE, U, 24, BEADS), F32),
            pltpu.VMEM((NR, BEADS, 128), BF16),
            pltpu.VMEM((NR, 16, BEADS), BF16),
            pltpu.VMEM((NC + PAD + 2, 2 * LABELS, BEADS), BF16),
            pltpu.VMEM((NC + 1, 2 * LABELS, BEADS), BF16),
            pltpu.VMEM((NR, 8, BEADS), F32),
            pltpu.VMEM((NC + PAD + 2, 8, BEADS), F32),
        ],
        compiler_params=pltpu.CompilerParams(vmem_limit_bytes=32 << 20),
        name="pairs",
    )(listing, bounds, rows, cols)


def on_device(coords, chrom_lengths, band_counts, inter_pairs, inter_counts):
    part = coords.shape[1:]
    lens = chrom_lengths.reshape(1, -1)
    flipped = jnp.transpose(inter_pairs, (0, 2, 1))
    sems = 2 * SIDE + COLS + SIDE * (SIDE + COLS)
    rows, cols, listing, bounds = pl.pallas_call(
        gather_kernel,
        out_shape=[jax.ShapeDtypeStruct((COLS, SIDE) + part, F32), jax.ShapeDtypeStruct((SIDE, SIDE) + part, F32),
                   jax.ShapeDtypeStruct((LINES, 128), I32), jax.ShapeDtypeStruct((2, LABELS, BEADS), I32)],
        in_specs=[HBM] * 5, out_specs=[VMEM] * 4,
        scratch_shapes=[
            pltpu.VMEM(lens.shape, I32),
            pltpu.VMEM(flipped.shape[1:], I32),
            pltpu.VMEM(inter_counts.shape, I32),
            pltpu.VMEM((3, 32, 128), I32),
            pltpu.VMEM((COLS,) + band_counts.shape, I32),
            pltpu.SemaphoreType.DMA((sems,)),
            pltpu.SemaphoreType.DMA((sems,)),
            pltpu.SemaphoreType.DMA((6,)),
        ],
        compiler_params=pltpu.CompilerParams(collective_id=0, has_side_effects=True, vmem_limit_bytes=24 << 20),
        name="gather",
    )(*[pltpu.with_memory_space_constraint(v, pltpu.HBM)
        for v in (coords, band_counts, lens, flipped, inter_counts)])
    prow, pcol = pairs_call(listing, bounds, rows, cols)
    return pl.pallas_call(
        scatter_kernel,
        out_shape=jax.ShapeDtypeStruct(coords.shape, F32),
        in_specs=[VMEM] * 2, out_specs=VMEM,
        scratch_shapes=[
            pltpu.VMEM((SIDE + COLS - 2, SIDE) + part, F32),
            pltpu.VMEM((2, SIDE) + part, F32),
            pltpu.VMEM((SIDE - 1,) + part, F32),
            pltpu.VMEM((SIDE - 1,) + part, F32),
            pltpu.SemaphoreType.DMA((SIDE * (SIDE + COLS) + SIDE,)),
            pltpu.SemaphoreType.DMA((SIDE * (SIDE + COLS) + SIDE,)),
            pltpu.SemaphoreType.DMA((2,)),
        ],
        compiler_params=pltpu.CompilerParams(collective_id=1, has_side_effects=True, vmem_limit_bytes=24 << 20),
        name="scatter",
    )(prow, pcol)


def solution(mesh):
    placed = (P(None, None, None, ("row", "col")), P(), P(None, None, ("row", "col"), None), P(), P())
    return jax.shard_map(on_device, mesh=mesh, in_specs=placed,
                         out_specs=P(None, None, None, ("row", "col")), check_vma=False)
```

```python
import jax
import jax.numpy as jnp
from jax import lax
from jax.experimental import pallas as pl
from jax.experimental.pallas import tpu as pltpu
from jax.sharding import PartitionSpec as P

MESH = pl.DeviceIdType.MESH
ROWS, COLS, SIDE = 16, 8, 4
U, BEADS = 8, 128
CAP = 256
LABELS = 48
NR, NC = SIDE * COLS * U, ROWS * U
UNITS = 2 * NR
PAD = 4
WIDE = 4
LONG, SHORT = 12, 2
BIG = 64.0
F32, BF16, I32 = jnp.float32, jnp.bfloat16, jnp.int32
HBM = pl.BlockSpec(memory_space=pltpu.HBM)
VMEM = pl.BlockSpec(memory_space=pltpu.VMEM)
SMEM = pl.BlockSpec(memory_space=pltpu.SMEM)
NT = (((1,), (1,)), ((), ()))
LISTED, TOTALS, WIDTHS, PLACE, TALLY, UNIT, LINES = 0, 16, 17, 19, 24, 88, 96


def iota(shape, axis):
    return lax.broadcasted_iota(I32, shape, axis)


def flag(x):
    return x.astype(F32).astype(BF16)


def chrom_bounds(lens_ref):
    lens = jnp.broadcast_to(lens_ref[...], (LABELS, lens_ref.shape[1]))
    sub, lane = iota(lens.shape, 0), iota(lens.shape, 1)
    ends = jnp.sum(jnp.where(lane <= sub, lens, 0), axis=1, keepdims=True)
    starts = jnp.sum(jnp.where(lane < sub, lens, 0), axis=1, keepdims=True)
    return starts, ends


def compact(mine, values, slots):
    count = mine.shape[0]
    a, b = iota((128, 128), 0), iota((128, 128), 1)
    within = jnp.dot(flag(mine), flag(a <= b), preferred_element_type=F32)
    total = jnp.dot(flag(mine), jnp.ones((128, 128), BF16), preferred_element_type=F32)
    lower = flag(iota((count, count), 1) < iota((count, count), 0))
    offset = jnp.dot(lower, total.astype(BF16), preferred_element_type=F32)
    place = jnp.where(mine, (offset + within).astype(I32) - 1, -1)
    values = [v.astype(F32) for v in values] + [mine.astype(F32)]
    slot = iota((slots, 128), 0)
    pad = jnp.zeros((16 - len(values), 128), F32)
    acc = jnp.zeros((16, slots), F32)
    for lo in range(0, count, 8):
        span = range(lo, min(lo + 8, count))
        hot = jnp.concatenate([flag(place[e:e + 1] == slot) for e in span], axis=1)
        rows = [jnp.concatenate([v[e:e + 1] for v in values] + [pad], axis=0) for e in span]
        acc = acc + lax.dot_general(jnp.concatenate(rows, axis=1).astype(BF16), hot, NT,
                                    preferred_element_type=F32)
    return acc[0:8]


def make_list(y, z, c, lens_ref, pairs_ref, count_ref, stage_ref, out_ref, bounds_ref):
    for t in range(32):
        lane = slice(t * 128, t * 128 + 128)
        stage_ref[0, t:t + 1, :] = pairs_ref[0:1, lane]
        stage_ref[1, t:t + 1, :] = pairs_ref[1:2, lane]
        block = count_ref[:, lane]
        stage_ref[2, t:t + 1, :] = jnp.sum(jnp.where(iota(block.shape, 0) == y, block, 0), axis=0, keepdims=True)
    first, second, counts = stage_ref[0], stage_ref[1], stage_ref[2]
    mine = (((first >> 3) & 3) == z) & ((second & 7) == c)
    at = (first & 7) * 32 + ((first >> 5) & 3) * 8 + (first >> 7)
    acc = compact(mine, [at, second >> 3, counts], CAP)
    spare = jnp.where(iota((8, CAP), 0) == 1, NC * (1.0 - acc[3:4]), 0.0)
    found = (acc + spare).astype(I32)
    out_ref[LISTED:LISTED + 8, :] = found[:, 0:128]
    out_ref[LISTED + 8:LISTED + 16, :] = found[:, 128:256]

    starts, ends = chrom_bounds(lens_ref)
    bounds_ref[0] = jnp.broadcast_to(starts, (LABELS, BEADS))
    bounds_ref[1] = jnp.broadcast_to(ends, (LABELS, BEADS))
    widths = []
    for i in range(2):
        at = iota((1, 128), 1) + i * 128
        k = at >> 5
        block = (at & 7) * 128 + (((at >> 3) & 3) * 4 + z) * 8 + k
        last = jnp.broadcast_to(block * 128 + 127, (LABELS, 128))
        stop = jnp.min(jnp.where(ends > last, ends, 1 << 20), axis=0, keepdims=True)
        far = jnp.minimum(jnp.minimum((stop - 1) >> 7, block + 31), 1023)
        widths.append(((far - block - ((c - k) & 7)) >> 3) + 1)
    width = jnp.concatenate(widths + widths, axis=0)
    entry = iota((4, 128), 0) * 128 + iota((4, 128), 1)
    near = (entry < NR) & (width > 0) & (((entry >> 5) & 7) != c)
    live = near | ((entry >= NR) & (width > 2))
    acc = compact(live, [entry >> 2, entry & 3], UNITS)
    units = acc[0:1] * 4.0 + acc[1:2] + UNITS * (1.0 - acc[2:3])
    for i in range(4):
        out_ref[UNIT + i:UNIT + i + 1, :] = units[:, i * 128:i * 128 + 128].astype(I32)
    out_ref[UNIT + 4:UNIT + 8, :] = jnp.zeros((4, 128), I32)
    listed = jnp.sum(found[3:4].astype(F32), axis=1, keepdims=True).astype(I32)
    active = jnp.sum(acc[2:3], axis=1, keepdims=True).astype(I32)
    lane = iota((1, 128), 1)
    out_ref[TOTALS:TOTALS + 1, :] = jnp.where(lane == 0, listed, active)
    out_ref[WIDTHS:WIDTHS + 2, :] = jnp.zeros((2, 128), I32)
    out_ref[PLACE:PLACE + 1, :] = jnp.where(lane == 0, z, c)
    out_ref[PLACE + 1:TALLY, :] = jnp.zeros((4, 128), I32)


def greet(r, c):
    y, z = r // SIDE, lax.rem(r, SIDE)
    peers = [(r, lax.rem(c + d, COLS)) for d in range(1, COLS)]
    peers += [(lax.rem(y + d, SIDE) * SIDE + z, c) for d in range(1, SIDE)]
    peers += [(y * SIDE + lax.rem(z + d, SIDE), c) for d in range(1, SIDE)]
    barrier = pltpu.get_barrier_semaphore()
    for peer in peers:
        pl.semaphore_signal(barrier, 1, device_id=peer, device_id_type=MESH)
    pl.semaphore_wait(barrier, len(peers))


def split3(x):
    a = x.astype(BF16).astype(F32)
    b = (x - a).astype(BF16).astype(F32)
    return a, b, (x - a) - b


def points_of(x, y, z):
    c = 0.75 - 0.25 * (x * x + y * y + z * z)
    return split3(x), split3(y), split3(z), split3(c)


def turn_rows(k, z, rows_ref, bounds_ref, tile_ref, left_ref, lrow_ref):
    starts, ends = bounds_ref[0], bounds_ref[1]
    lanes = iota((LABELS, BEADS), 1)
    for yy in range(SIDE):
        parts = points_of(rows_ref[k, yy, 0], rows_ref[k, yy, 1], rows_ref[k, yy, 2])
        for q in range(3):
            for w in range(4):
                value = parts[w][q]
                tile_ref[yy, :, 8 * q + w, :] = 0.5 * value if w < 3 else value
    for yy in range(SIDE):
        for u in range(U):
            at = (k * SIDE + yy) * U + u
            tiles = [tile_ref[yy, u, 8 * q:8 * q + 8] for q in range(3)]
            full = jnp.concatenate([tiles[j] for j in (0, 0, 1, 0, 2, 1)], axis=0).astype(BF16)
            bead = lanes + (u * 128 + (4 * yy + z) * 8 + k) * BEADS
            hot = jnp.where((bead >= starts) & (bead < ends), 1.0, 0.0).astype(BF16)
            lrow_ref[at] = jnp.concatenate(tiles[:2], axis=0).astype(BF16)
            left_ref[at] = jnp.concatenate([full, hot, jnp.zeros((32, 128), BF16)], axis=0).T


def gather_kernel(coords, counts, lens, pairs, inter, rows, cols, list_ref, bounds_ref, left_ref, lrow_ref,
                  lens_ref, pairs_ref, inter_ref, stage_ref, tile_ref, tallies, send, recv, local):
    r, c = lax.axis_index("row"), lax.axis_index("col")
    y, z = r // SIDE, lax.rem(r, SIDE)
    taken = [pltpu.make_async_copy(pairs.at[y], pairs_ref, local.at[0]),
             pltpu.make_async_copy(inter, inter_ref, local.at[1]),
             pltpu.make_async_copy(lens, lens_ref, local.at[5])]
    kept = [pltpu.make_async_copy(coords.at[y], rows.at[c, y], local.at[2]),
            pltpu.make_async_copy(counts.at[y], tallies.at[c, y], local.at[3])]
    for copy in kept + taken:
        copy.start()
    greet(r, c)

    def push(source, target, n, peer):
        return pltpu.make_async_remote_copy(source, target, send.at[n], recv.at[n],
                                            device_id=peer, device_id_type=MESH)

    early, talks = [], []
    for d in (1, 3, 2):
        to = lax.rem(y + d, SIDE)
        peer = (to * SIDE + z, c)
        early.append(push(coords.at[to], rows.at[c, y], d, peer))
        talks.append(push(counts.at[to], tallies.at[c, y], SIDE + d, peer))
    for copy in early:
        copy.start()
    late, across = [], []

    def spread(step):
        part = lax.rem(y + SIDE - step, SIDE)
        source = rows.at[c, part] if step else coords.at[y]
        base = 2 * SIDE + COLS + step * (SIDE + COLS)
        copies = [push(source, rows.at[c, part], base + SIDE + d, (r, lax.rem(c + d, COLS)))
                  for d in (4, 2, 6, 1, 3, 5, 7)]
        copies += [push(source, cols.at[z, part], base + d, (y * SIDE + lax.rem(z + d, SIDE), c))
                   for d in (1, 3, 2)]
        for copy in copies:
            copy.start()
        across.extend(copies[:COLS - 1])
        late.extend(copies[COLS - 1:])

    spread(0)
    for copy in talks:
        copy.start()
    for step, copy in zip((1, 3, 2), early):
        copy.wait_recv()
        spread(step)
    for copy in kept:
        copy.wait()
    same = pltpu.make_async_copy(rows.at[c], cols.at[z], local.at[4])
    same.start()
    for copy in talks:
        copy.wait_recv()
    talk = [push(tallies.at[c], tallies.at[c], 2 * SIDE + d, (r, lax.rem(c + d, COLS))) for d in range(1, COLS)]
    for copy in talk:
        copy.start()
    for copy in taken:
        copy.wait()
    make_list(y, z, c, lens_ref, pairs_ref, inter_ref, stage_ref, list_ref, bounds_ref)
    for copy in talk:
        copy.wait_recv()
    for k in range(COLS):
        for yy in range(SIDE):
            for u in range(U):
                at = TALLY + k * 8 + yy * 2 + u // 4
                list_ref[at:at + 1, (u % 4) * 32:(u % 4) * 32 + 32] = tallies[k, yy, u]
    for v in range(SIDE):
        for u in range(U):
            for q in range(3):
                tile_ref[v, u, 8 * q:8 * q + 8] = jnp.zeros((8, 128), F32)
    for v in range(SIDE):
        tile_ref[v, :, 4, :] = jnp.ones((8, 128), F32)
    turn_rows(c, z, rows, bounds_ref, tile_ref, left_ref, lrow_ref)

    def land(d, carry):
        k = lax.rem(c + COLS - d, COLS)
        for step in range(SIDE):
            n = 2 * SIDE + COLS + step * (SIDE + COLS) + SIDE + d
            push(coords.at[0], rows.at[k, lax.rem(y + SIDE - step, SIDE)], n, (r, lax.rem(c + d, COLS))).wait_recv()
        turn_rows(k, z, rows, bounds_ref, tile_ref, left_ref, lrow_ref)
        return carry

    lax.fori_loop(1, COLS, land, 0)
    for copy in early + talks + talk + across:
        copy.wait_send()
    for copy in late:
        copy.wait()
    same.wait()


def scatter_kernel(rows, cols, out, land, own, total, last, send, recv, local):
    r, c = lax.axis_index("row"), lax.axis_index("col")
    y, z = r // SIDE, lax.rem(r, SIDE)
    kept = [pltpu.make_async_copy(rows.at[c], own.at[0], local.at[0]),
            pltpu.make_async_copy(cols.at[z], own.at[1], local.at[1])]
    for copy in kept:
        copy.start()
    greet(r, c)
    copies = []

    def push(source, target, n, peer):
        return pltpu.make_async_remote_copy(source, target, send.at[n], recv.at[n],
                                            device_id=peer, device_id_type=MESH)

    order = (2, 1, 3, 0)
    for turn in order:
        part, base = lax.rem(y + turn, SIDE), turn * (SIDE + COLS)
        group = []
        for d in (4, 2, 6, 1, 3, 5, 7):
            to = lax.rem(c + d, COLS)
            group.append(push(rows.at[to, part], land.at[SIDE - 2 + d, part], base + SIDE + d, (r, to)))
        for d in (1, 3, 2):
            to = lax.rem(z + d, SIDE)
            group.append(push(cols.at[to, part], land.at[d - 1, part], base + d, (y * SIDE + to, c)))
        for copy in group:
            copy.start()
        copies.append(group)
    for copy in kept:
        copy.wait()
    second = []
    for turn, group in zip(order, copies):
        part = lax.rem(y + turn, SIDE)
        for copy in group:
            copy.wait_recv()
        sums = [own[0, part] + own[1, part]] + [land[d, part] for d in range(SIDE + COLS - 2)]
        while len(sums) > 1:
            sums = [a + b for a, b in zip(sums[::2], sums[1::2])] + sums[len(sums) - len(sums) % 2:]
        if turn == 0:
            out[y] = sums[0]
        else:
            total[turn - 1] = sums[0]
            copy = push(total.at[turn - 1], last.at[turn - 1], SIDE * (SIDE + COLS) + turn, (part * SIDE + z, c))
            copy.start()
            second.append((turn, copy))
    for turn, copy in second:
        copy.wait_recv()
        out[lax.rem(y + SIDE - turn, SIDE)] = last[turn - 1]
    for copy in [copy for group in copies for copy in group] + [copy for _, copy in second]:
        copy.wait_send()


def pair_kernel(list_ref, bounds_ref, rows_ref, cols_ref, left_ref, lrow_ref, prow_ref, pcol_ref,
                tile_ref, same_ref, differ_ref, arow_ref, acol_ref):
    z, c = list_ref[PLACE, 0], list_ref[PLACE, 1]
    starts, ends = bounds_ref[0], bounds_ref[1]
    lanes = iota((LABELS, BEADS), 1)
    one = jnp.ones((8, 128), F32)
    nil = jnp.zeros((8, 128), F32)

    def hot_of(block):
        bead = lanes + block * BEADS
        return (bead >= starts) & (bead < ends)

    for v in range(SIDE):
        for u in range(U):
            for q in range(3):
                tile_ref[v, u, 8 * q:8 * q + 8] = nil

    for v in range(SIDE):
        tile_ref[v, :, 3, :] = one

    @pl.loop(0, SIDE)
    def _(zz):
        for yy in range(SIDE):
            parts = points_of(cols_ref[zz, yy, 0], cols_ref[zz, yy, 1], cols_ref[zz, yy, 2])
            for q in range(3):
                for w in range(4):
                    tile_ref[yy, :, 8 * q + (w if w < 3 else 4), :] = parts[w][q]
        for yy in range(SIDE):
            for u in range(U):
                at = u * ROWS + 4 * yy + zz
                tiles = [tile_ref[yy, u, 8 * q:8 * q + 8] for q in range(3)]
                full = jnp.concatenate([tiles[i] for i in (0, 1, 0, 2, 0, 1)], axis=0).astype(BF16)
                hot = hot_of(at * 8 + c)
                same_ref[at, 0:LABELS] = full
                differ_ref[at, 0:LABELS] = full
                same_ref[at, LABELS:] = jnp.where(hot, 0.0, -BIG).astype(BF16)
                differ_ref[at, LABELS:] = jnp.where(hot, -BIG, 0.0).astype(BF16)

    apart = jnp.concatenate([jnp.zeros((LABELS, BEADS), BF16), jnp.full((LABELS, BEADS), -BIG, BF16)], axis=0)
    for p in range(PAD):
        same_ref[NC + p] = apart
    differ_ref[NC] = apart

    @pl.loop(0, (NC + PAD) // 4)
    def _(i):
        for j in range(4):
            acol_ref[i * 4 + j] = nil

    @pl.loop(0, NR // 8)
    def _(i):
        for j in range(8):
            arow_ref[i * 8 + j] = nil

    triangle = iota((128, 128), 0) < iota((128, 128), 1)
    empty = jnp.zeros((16, 128), BF16)

    def finish(z, diagonal=False):
        t = jnp.tanh(z)
        if diagonal:
            t = jnp.concatenate([jnp.where(triangle, t[:, :128], -1.0), t[:, 128:]], axis=1)
        return jnp.sum(t, axis=0, keepdims=True), (1.0 - t * t).astype(BF16)

    def weigh(sums, n):
        expect = 0.5 + (0.5 * (16384.0 + jnp.sum(sums, axis=1, keepdims=True))) / 128.0
        n = jnp.full((1, 128), n, I32).astype(F32)
        return jnp.broadcast_to(1.0 - n / jnp.broadcast_to(expect, (1, 128)), (8, 128))

    def unit_drain(g, sums, at, start, counts):
        far = [same_ref[start + m, 0:16] for m in range(2)]
        o = jnp.dot(lrow_ref[at], g, preferred_element_type=F32)
        spread = jnp.concatenate([jnp.concatenate([far[0], empty], axis=1),
                                  jnp.concatenate([empty, far[1]], axis=1)], axis=0)
        p = lax.dot_general(spread, g, NT, preferred_element_type=F32)
        w = [weigh(sums[:, m * 128:m * 128 + 128], counts[m]) for m in range(2)]
        arow_ref[at] += w[0] * (p[0:8] + p[8:16]) + w[1] * (p[16:24] + p[24:32])
        for m in range(2):
            lane = slice(m * 128, m * 128 + 128)
            acol_ref[start + m] += w[m] * (o[0:8, lane] + o[8:16, lane])

    def run(held, unit_at, trips, turns, diagonal):
        def body(it, held):
            for q in range(turns):
                zs, now = [], []
                for i in range(WIDE):
                    entry = unit_at((it * turns + q) * WIDE + i)
                    at, half = entry & (NR - 1), entry >> 8
                    k, u = at >> 5, at & 7
                    start = u * ROWS + 4 * ((at >> 3) & 3) + z + jnp.where(k > c, 1, 0) + 2 * half
                    start = jnp.where(entry < UNITS, start, NC)
                    lane = (at & 3) * 32 + ((c - k) & 7) + 16 * half
                    counts = [list_ref[TALLY + (at >> 2), lane + 8 * m] for m in range(2)]
                    right = jnp.concatenate([same_ref[start], same_ref[start + 1]], axis=1)
                    zs.append(jnp.dot(left_ref[at, :, 0:2 * LABELS], right, preferred_element_type=F32))
                    now.append((at, start, counts))
                for entry in held:
                    unit_drain(*entry)
                done = [finish(v, diagonal) for v in zs]
                held = [(done[i][1], done[i][0]) + now[i] for i in range(WIDE)]
            return held

        return lax.fori_loop(0, trips, body, held)

    def split(count):
        whole = count // (WIDE * LONG)
        done = whole * (WIDE * LONG)
        return whole, done, (count - done + WIDE * SHORT - 1) // (WIDE * SHORT)

    zero = jnp.int32(0)
    held = [(jnp.zeros((128, 256), BF16), jnp.zeros((1, 256), F32), zero, zero, [zero, zero])
            for _ in range(WIDE)]
    held = run(held, lambda i: c * (SIDE * U) + i, 1, SIDE * U // WIDE, True)
    whole, done, rest = split(list_ref[TOTALS, 1])
    held = run(held, lambda i: list_ref[UNIT + (i >> 7), i & 127], whole, LONG, False)
    held = run(held, lambda i: list_ref[UNIT + ((i + done) >> 7), (i + done) & 127], rest, SHORT, False)
    for entry in held:
        unit_drain(*entry)

    def listed_drain(held):
        for lo in range(0, WIDE, 2):
            pair = held[lo:lo + 2]
            near = jnp.concatenate([lrow_ref[p[2]] for p in pair], axis=0)
            far = jnp.concatenate([differ_ref[p[3], 0:16] for p in pair], axis=0)
            o = jnp.dot(near, jnp.concatenate([p[0] for p in pair], axis=1), preferred_element_type=F32)
            v = lax.dot_general(far, jnp.concatenate([p[0] for p in pair], axis=0), NT,
                                preferred_element_type=F32)
            for m, p in enumerate(pair):
                lane, at = slice(m * 128, m * 128 + 128), m * 16
                w = weigh(p[1], p[4])
                arow_ref[p[2]] += w * (v[at:at + 8, lane] + v[at + 8:at + 16, lane])
                acol_ref[p[3]] += w * (o[at:at + 8, lane] + o[at + 8:at + 16, lane])

    def listed_run(held, offset, trips, laps):
        def body(it, held):
            for q in range(laps):
                zs, now = [], []
                for i in range(WIDE):
                    slot = offset + (it * laps + q) * WIDE + i
                    line, lane = LISTED + (slot >> 7) * 8, slot & 127
                    at, to, n = [list_ref[line + f, lane] for f in range(3)]
                    zs.append(jnp.dot(left_ref[at, :, 0:2 * LABELS], differ_ref[to], preferred_element_type=F32))
                    now.append((at, to, n))
                listed_drain(held)
                done = [finish(v) for v in zs]
                held = [(done[i][1], done[i][0]) + now[i] for i in range(WIDE)]
            return held

        return lax.fori_loop(0, trips, body, held)

    held = [(jnp.zeros((128, 128), BF16), jnp.zeros((1, 128), F32), zero, zero, zero) for _ in range(WIDE)]
    whole, done, rest = split(list_ref[TOTALS, 0])
    held = listed_run(held, 0, whole, LONG)
    listed_drain(listed_run(held, done, rest, SHORT))

    @pl.loop(0, COLS)
    def _(k):
        for yy in range(SIDE):
            here = pl.ds((k * SIDE + yy) * U, U)
            mass = arow_ref[here, 3, :]
            for w in range(3):
                pulled = rows_ref[k, yy, w] * mass - arow_ref[here, w, :]
                prow_ref[k, yy, w] = pulled * (-1.0 / 512.0)

    @pl.loop(0, SIDE)
    def _(zz):
        for yy in range(SIDE):
            here = pl.ds(4 * yy + zz, U, stride=ROWS)
            mass = acol_ref[here, 4, :]
            for w in range(3):
                pulled = cols_ref[zz, yy, w] * mass - 2.0 * acol_ref[here, w, :]
                pcol_ref[zz, yy, w] = pulled * (-1.0 / 512.0)


def pairs_call(listing, bounds, rows, cols, left, lrow):
    return pl.pallas_call(
        pair_kernel,
        out_shape=[jax.ShapeDtypeStruct(rows.shape, F32), jax.ShapeDtypeStruct(cols.shape, F32)],
        in_specs=[SMEM] + [VMEM] * 5, out_specs=[VMEM] * 2,
        scratch_shapes=[
            pltpu.VMEM((SIDE, U, 24, BEADS), F32),
            pltpu.VMEM((NC + PAD + 2, 2 * LABELS, BEADS), BF16),
            pltpu.VMEM((NC + 1, 2 * LABELS, BEADS), BF16),
            pltpu.VMEM((NR, 8, BEADS), F32),
            pltpu.VMEM((NC + PAD + 2, 8, BEADS), F32),
        ],
        compiler_params=pltpu.CompilerParams(vmem_limit_bytes=32 << 20),
        name="pairs",
    )(listing, bounds, rows, cols, left, lrow)


def on_device(coords, chrom_lengths, band_counts, inter_pairs, inter_counts):
    part = coords.shape[1:]
    lens = chrom_lengths.reshape(1, -1)
    flipped = jnp.transpose(inter_pairs, (0, 2, 1))
    sems = 2 * SIDE + COLS + SIDE * (SIDE + COLS)
    rows, cols, listing, bounds, left, lrow = pl.pallas_call(
        gather_kernel,
        out_shape=[jax.ShapeDtypeStruct((COLS, SIDE) + part, F32), jax.ShapeDtypeStruct((SIDE, SIDE) + part, F32),
                   jax.ShapeDtypeStruct((LINES, 128), I32), jax.ShapeDtypeStruct((2, LABELS, BEADS), I32),
                   jax.ShapeDtypeStruct((NR, BEADS, 128), BF16), jax.ShapeDtypeStruct((NR, 16, BEADS), BF16)],
        in_specs=[HBM] * 5, out_specs=[VMEM] * 6,
        scratch_shapes=[
            pltpu.VMEM(lens.shape, I32),
            pltpu.VMEM(flipped.shape[1:], I32),
            pltpu.VMEM(inter_counts.shape, I32),
            pltpu.VMEM((3, 32, 128), I32),
            pltpu.VMEM((SIDE, U, 24, BEADS), F32),
            pltpu.VMEM((COLS,) + band_counts.shape, I32),
            pltpu.SemaphoreType.DMA((sems,)),
            pltpu.SemaphoreType.DMA((sems,)),
            pltpu.SemaphoreType.DMA((6,)),
        ],
        compiler_params=pltpu.CompilerParams(collective_id=0, has_side_effects=True, vmem_limit_bytes=24 << 20),
        name="gather",
    )(*[pltpu.with_memory_space_constraint(v, pltpu.HBM)
        for v in (coords, band_counts, lens, flipped, inter_counts)])
    prow, pcol = pairs_call(listing, bounds, rows, cols, left, lrow)
    return pl.pallas_call(
        scatter_kernel,
        out_shape=jax.ShapeDtypeStruct(coords.shape, F32),
        in_specs=[VMEM] * 2, out_specs=VMEM,
        scratch_shapes=[
            pltpu.VMEM((SIDE + COLS - 2, SIDE) + part, F32),
            pltpu.VMEM((2, SIDE) + part, F32),
            pltpu.VMEM((SIDE - 1,) + part, F32),
            pltpu.VMEM((SIDE - 1,) + part, F32),
            pltpu.SemaphoreType.DMA((SIDE * (SIDE + COLS) + SIDE,)),
            pltpu.SemaphoreType.DMA((SIDE * (SIDE + COLS) + SIDE,)),
            pltpu.SemaphoreType.DMA((2,)),
        ],
        compiler_params=pltpu.CompilerParams(collective_id=1, has_side_effects=True, vmem_limit_bytes=24 << 20),
        name="scatter",
    )(prow, pcol)


def solution(mesh):
    placed = (P(None, None, None, ("row", "col")), P(), P(None, None, ("row", "col"), None), P(), P())
    return jax.shard_map(on_device, mesh=mesh, in_specs=placed,
                         out_specs=P(None, None, None, ("row", "col")), check_vma=False)
```

```python
import jax
import jax.numpy as jnp
from jax import lax
from jax.experimental import pallas as pl
from jax.experimental.pallas import tpu as pltpu
from jax.sharding import PartitionSpec as P

MESH = pl.DeviceIdType.MESH
ROWS, COLS, SIDE = 16, 8, 4
U, BEADS = 8, 128
CAP = 256
LABELS = 48
NR, NC = SIDE * COLS * U, ROWS * U
UNITS = 2 * NR
PAD = 4
WIDE = 4
LONG, SHORT = 12, 2
BIG = 64.0
F32, BF16, I32 = jnp.float32, jnp.bfloat16, jnp.int32
HBM = pl.BlockSpec(memory_space=pltpu.HBM)
VMEM = pl.BlockSpec(memory_space=pltpu.VMEM)
SMEM = pl.BlockSpec(memory_space=pltpu.SMEM)
NT = (((1,), (1,)), ((), ()))
LISTED, TOTALS, WIDTHS, PLACE, TALLY, UNIT, LINES = 0, 16, 17, 19, 24, 88, 96


def iota(shape, axis):
    return lax.broadcasted_iota(I32, shape, axis)


def flag(x):
    return x.astype(F32).astype(BF16)


def chrom_bounds(lens_ref):
    lens = jnp.broadcast_to(lens_ref[...], (LABELS, lens_ref.shape[1]))
    sub, lane = iota(lens.shape, 0), iota(lens.shape, 1)
    ends = jnp.sum(jnp.where(lane <= sub, lens, 0), axis=1, keepdims=True)
    starts = jnp.sum(jnp.where(lane < sub, lens, 0), axis=1, keepdims=True)
    return starts, ends


def compact(mine, values, slots):
    count = mine.shape[0]
    a, b = iota((128, 128), 0), iota((128, 128), 1)
    within = jnp.dot(flag(mine), flag(a <= b), preferred_element_type=F32)
    total = jnp.dot(flag(mine), jnp.ones((128, 128), BF16), preferred_element_type=F32)
    lower = flag(iota((count, count), 1) < iota((count, count), 0))
    offset = jnp.dot(lower, total.astype(BF16), preferred_element_type=F32)
    place = jnp.where(mine, (offset + within).astype(I32) - 1, -1)
    values = [v.astype(F32) for v in values] + [mine.astype(F32)]
    slot = iota((slots, 128), 0)
    pad = jnp.zeros((16 - len(values), 128), F32)
    acc = jnp.zeros((16, slots), F32)
    for lo in range(0, count, 8):
        span = range(lo, min(lo + 8, count))
        hot = jnp.concatenate([flag(place[e:e + 1] == slot) for e in span], axis=1)
        rows = [jnp.concatenate([v[e:e + 1] for v in values] + [pad], axis=0) for e in span]
        acc = acc + lax.dot_general(jnp.concatenate(rows, axis=1).astype(BF16), hot, NT,
                                    preferred_element_type=F32)
    return acc[0:8]


def make_list(y, z, c, pairs_ref, count_ref, stage_ref, out_ref):
    for t in range(32):
        lane = slice(t * 128, t * 128 + 128)
        stage_ref[0, t:t + 1, :] = pairs_ref[0:1, lane]
        stage_ref[1, t:t + 1, :] = pairs_ref[1:2, lane]
        block = count_ref[:, lane]
        stage_ref[2, t:t + 1, :] = jnp.sum(jnp.where(iota(block.shape, 0) == y, block, 0), axis=0, keepdims=True)
    first, second, counts = stage_ref[0], stage_ref[1], stage_ref[2]
    mine = (((first >> 3) & 3) == z) & ((second & 7) == c)
    at = (first & 7) * 32 + ((first >> 5) & 3) * 8 + (first >> 7)
    acc = compact(mine, [at, second >> 3, counts], CAP)
    spare = jnp.where(iota((8, CAP), 0) == 1, NC * (1.0 - acc[3:4]), 0.0)
    found = (acc + spare).astype(I32)
    out_ref[LISTED:LISTED + 8, :] = found[:, 0:128]
    out_ref[LISTED + 8:LISTED + 16, :] = found[:, 128:256]
    listed = jnp.sum(found[3:4].astype(F32), axis=1, keepdims=True).astype(I32)
    out_ref[TOTALS:TOTALS + 1, :] = jnp.where(iota((1, 128), 1) == 0, listed, out_ref[TOTALS:TOTALS + 1, :])


def make_units(z, c, lens_ref, out_ref, bounds_ref):
    starts, ends = chrom_bounds(lens_ref)
    bounds_ref[0] = jnp.broadcast_to(starts, (LABELS, BEADS))
    bounds_ref[1] = jnp.broadcast_to(ends, (LABELS, BEADS))
    widths = []
    for i in range(2):
        at = iota((1, 128), 1) + i * 128
        k = at >> 5
        block = (at & 7) * 128 + (((at >> 3) & 3) * 4 + z) * 8 + k
        last = jnp.broadcast_to(block * 128 + 127, (LABELS, 128))
        stop = jnp.min(jnp.where(ends > last, ends, 1 << 20), axis=0, keepdims=True)
        far = jnp.minimum(jnp.minimum((stop - 1) >> 7, block + 31), 1023)
        widths.append(((far - block - ((c - k) & 7)) >> 3) + 1)
    width = jnp.concatenate(widths + widths, axis=0)
    entry = iota((4, 128), 0) * 128 + iota((4, 128), 1)
    near = (entry < NR) & (width > 0) & (((entry >> 5) & 7) != c)
    live = near | ((entry >= NR) & (width > 2))
    acc = compact(live, [entry >> 2, entry & 3], UNITS)
    units = acc[0:1] * 4.0 + acc[1:2] + UNITS * (1.0 - acc[2:3])
    for i in range(4):
        out_ref[UNIT + i:UNIT + i + 1, :] = units[:, i * 128:i * 128 + 128].astype(I32)
    out_ref[UNIT + 4:UNIT + 8, :] = jnp.zeros((4, 128), I32)
    active = jnp.sum(acc[2:3], axis=1, keepdims=True).astype(I32)
    lane = iota((1, 128), 1)
    out_ref[TOTALS:TOTALS + 1, :] = jnp.broadcast_to(active, (1, 128))
    out_ref[WIDTHS:WIDTHS + 2, :] = jnp.zeros((2, 128), I32)
    out_ref[PLACE:PLACE + 1, :] = jnp.where(lane == 0, z, c)
    out_ref[PLACE + 1:TALLY, :] = jnp.zeros((4, 128), I32)


def greet(r, c):
    y, z = r // SIDE, lax.rem(r, SIDE)
    peers = [(r, lax.rem(c + d, COLS)) for d in range(1, COLS)]
    peers += [(lax.rem(y + d, SIDE) * SIDE + z, c) for d in range(1, SIDE)]
    peers += [(y * SIDE + lax.rem(z + d, SIDE), c) for d in range(1, SIDE)]
    barrier = pltpu.get_barrier_semaphore()
    for peer in peers:
        pl.semaphore_signal(barrier, 1, device_id=peer, device_id_type=MESH)
    pl.semaphore_wait(barrier, len(peers))


def split3(x):
    a = x.astype(BF16).astype(F32)
    b = (x - a).astype(BF16).astype(F32)
    return a, b, (x - a) - b


def points_of(x, y, z):
    c = 0.75 - 0.25 * (x * x + y * y + z * z)
    return split3(x), split3(y), split3(z), split3(c)


def turn_rows(k, z, rows_ref, bounds_ref, tile_ref, left_ref, lrow_ref):
    starts, ends = bounds_ref[0], bounds_ref[1]
    lanes = iota((LABELS, BEADS), 1)
    for yy in range(SIDE):
        parts = points_of(rows_ref[k, yy, 0], rows_ref[k, yy, 1], rows_ref[k, yy, 2])
        for q in range(3):
            for w in range(4):
                value = parts[w][q]
                tile_ref[yy, :, 8 * q + w, :] = 0.5 * value if w < 3 else value
    for yy in range(SIDE):
        for u in range(U):
            at = (k * SIDE + yy) * U + u
            tiles = [tile_ref[yy, u, 8 * q:8 * q + 8] for q in range(3)]
            full = jnp.concatenate([tiles[j] for j in (0, 0, 1, 0, 2, 1)], axis=0).astype(BF16)
            bead = lanes + (u * 128 + (4 * yy + z) * 8 + k) * BEADS
            hot = jnp.where((bead >= starts) & (bead < ends), 1.0, 0.0).astype(BF16)
            lrow_ref[at] = jnp.concatenate(tiles[:2], axis=0).astype(BF16)
            left_ref[at] = jnp.concatenate([full, hot, jnp.zeros((32, 128), BF16)], axis=0).T


def gather_kernel(coords, counts, lens, pairs, inter, rows, cols, list_ref, bounds_ref, left_ref, lrow_ref,
                  lens_ref, pairs_ref, inter_ref, stage_ref, tile_ref, tallies, send, recv, local):
    r, c = lax.axis_index("row"), lax.axis_index("col")
    y, z = r // SIDE, lax.rem(r, SIDE)
    taken = [pltpu.make_async_copy(pairs.at[y], pairs_ref, local.at[0]),
             pltpu.make_async_copy(inter, inter_ref, local.at[1]),
             pltpu.make_async_copy(lens, lens_ref, local.at[5])]
    kept = [pltpu.make_async_copy(coords.at[y], rows.at[c, y], local.at[2]),
            pltpu.make_async_copy(counts.at[y], tallies.at[c, y], local.at[3])]
    for copy in kept + taken:
        copy.start()
    greet(r, c)

    def push(source, target, n, peer):
        return pltpu.make_async_remote_copy(source, target, send.at[n], recv.at[n],
                                            device_id=peer, device_id_type=MESH)

    early, talks = [], []
    for d in (1, 3, 2):
        to = lax.rem(y + d, SIDE)
        peer = (to * SIDE + z, c)
        early.append(push(coords.at[to], rows.at[c, y], d, peer))
        talks.append(push(counts.at[to], tallies.at[c, y], SIDE + d, peer))
    for copy in early:
        copy.start()
    late, across = [], []

    def spread(step):
        part = lax.rem(y + SIDE - step, SIDE)
        source = rows.at[c, part] if step else coords.at[y]
        base = 2 * SIDE + COLS + step * (SIDE + COLS)
        copies = [push(source, rows.at[c, part], base + SIDE + d, (r, lax.rem(c + d, COLS)))
                  for d in (4, 2, 6, 1, 3, 5, 7)]
        copies += [push(source, cols.at[z, part], base + d, (y * SIDE + lax.rem(z + d, SIDE), c))
                   for d in (1, 3, 2)]
        for copy in copies:
            copy.start()
        across.extend(copies[:COLS - 1])
        late.extend(copies[COLS - 1:])

    spread(0)
    for copy in talks:
        copy.start()
    taken[2].wait()
    make_units(z, c, lens_ref, list_ref, bounds_ref)
    for v in range(SIDE):
        for u in range(U):
            for q in range(3):
                tile_ref[v, u, 8 * q:8 * q + 8] = jnp.zeros((8, 128), F32)
    for v in range(SIDE):
        tile_ref[v, :, 4, :] = jnp.ones((8, 128), F32)
    for step, copy in zip((1, 3, 2), early):
        copy.wait_recv()
        spread(step)
    for copy in kept:
        copy.wait()
    same = pltpu.make_async_copy(rows.at[c], cols.at[z], local.at[4])
    same.start()
    for copy in talks:
        copy.wait_recv()
    talk = [push(tallies.at[c], tallies.at[c], 2 * SIDE + d, (r, lax.rem(c + d, COLS))) for d in range(1, COLS)]
    for copy in talk:
        copy.start()
    for copy in taken[:2]:
        copy.wait()
    make_list(y, z, c, pairs_ref, inter_ref, stage_ref, list_ref)
    turn_rows(c, z, rows, bounds_ref, tile_ref, left_ref, lrow_ref)

    def land(d, carry):
        k = lax.rem(c + COLS - d, COLS)
        for step in range(SIDE):
            n = 2 * SIDE + COLS + step * (SIDE + COLS) + SIDE + d
            push(coords.at[0], rows.at[k, lax.rem(y + SIDE - step, SIDE)], n, (r, lax.rem(c + d, COLS))).wait_recv()
        turn_rows(k, z, rows, bounds_ref, tile_ref, left_ref, lrow_ref)
        return carry

    lax.fori_loop(1, COLS, land, 0)
    for copy in talk:
        copy.wait_recv()
    for k in range(COLS):
        for yy in range(SIDE):
            for u in range(U):
                at = TALLY + k * 8 + yy * 2 + u // 4
                list_ref[at:at + 1, (u % 4) * 32:(u % 4) * 32 + 32] = tallies[k, yy, u]
    for copy in early + talks + talk + across:
        copy.wait_send()
    for copy in late:
        copy.wait()
    same.wait()


def scatter_kernel(rows, cols, out, land, own, total, last, send, recv, local):
    r, c = lax.axis_index("row"), lax.axis_index("col")
    y, z = r // SIDE, lax.rem(r, SIDE)
    kept = [pltpu.make_async_copy(rows.at[c], own.at[0], local.at[0]),
            pltpu.make_async_copy(cols.at[z], own.at[1], local.at[1])]
    for copy in kept:
        copy.start()
    greet(r, c)
    copies = []

    def push(source, target, n, peer):
        return pltpu.make_async_remote_copy(source, target, send.at[n], recv.at[n],
                                            device_id=peer, device_id_type=MESH)

    order = (2, 1, 3, 0)
    for turn in order:
        part, base = lax.rem(y + turn, SIDE), turn * (SIDE + COLS)
        group = []
        for d in (4, 2, 6, 1, 3, 5, 7):
            to = lax.rem(c + d, COLS)
            group.append(push(rows.at[to, part], land.at[SIDE - 2 + d, part], base + SIDE + d, (r, to)))
        for d in (1, 3, 2):
            to = lax.rem(z + d, SIDE)
            group.append(push(cols.at[to, part], land.at[d - 1, part], base + d, (y * SIDE + to, c)))
        for copy in group:
            copy.start()
        copies.append(group)
    for copy in kept:
        copy.wait()
    second = []
    for turn, group in zip(order, copies):
        part = lax.rem(y + turn, SIDE)
        for copy in group:
            copy.wait_recv()
        sums = [own[0, part] + own[1, part]] + [land[d, part] for d in range(SIDE + COLS - 2)]
        while len(sums) > 1:
            sums = [a + b for a, b in zip(sums[::2], sums[1::2])] + sums[len(sums) - len(sums) % 2:]
        if turn == 0:
            out[y] = sums[0]
        else:
            total[turn - 1] = sums[0]
            copy = push(total.at[turn - 1], last.at[turn - 1], SIDE * (SIDE + COLS) + turn, (part * SIDE + z, c))
            copy.start()
            second.append((turn, copy))
    for turn, copy in second:
        copy.wait_recv()
        out[lax.rem(y + SIDE - turn, SIDE)] = last[turn - 1]
    for copy in [copy for group in copies for copy in group] + [copy for _, copy in second]:
        copy.wait_send()


def pair_kernel(list_ref, bounds_ref, rows_ref, cols_ref, left_ref, lrow_ref, prow_ref, pcol_ref,
                tile_ref, same_ref, differ_ref, arow_ref, acol_ref):
    z, c = list_ref[PLACE, 0], list_ref[PLACE, 1]
    starts, ends = bounds_ref[0], bounds_ref[1]
    lanes = iota((LABELS, BEADS), 1)
    one = jnp.ones((8, 128), F32)
    nil = jnp.zeros((8, 128), F32)

    def hot_of(block):
        bead = lanes + block * BEADS
        return (bead >= starts) & (bead < ends)

    for v in range(SIDE):
        for u in range(U):
            for q in range(3):
                tile_ref[v, u, 8 * q:8 * q + 8] = nil

    for v in range(SIDE):
        tile_ref[v, :, 3, :] = one

    @pl.loop(0, SIDE)
    def _(zz):
        for yy in range(SIDE):
            parts = points_of(cols_ref[zz, yy, 0], cols_ref[zz, yy, 1], cols_ref[zz, yy, 2])
            for q in range(3):
                for w in range(4):
                    tile_ref[yy, :, 8 * q + (w if w < 3 else 4), :] = parts[w][q]
        for yy in range(SIDE):
            for u in range(U):
                at = u * ROWS + 4 * yy + zz
                tiles = [tile_ref[yy, u, 8 * q:8 * q + 8] for q in range(3)]
                full = jnp.concatenate([tiles[i] for i in (0, 1, 0, 2, 0, 1)], axis=0).astype(BF16)
                hot = hot_of(at * 8 + c)
                same_ref[at, 0:LABELS] = full
                differ_ref[at, 0:LABELS] = full
                same_ref[at, LABELS:] = jnp.where(hot, 0.0, -BIG).astype(BF16)
                differ_ref[at, LABELS:] = jnp.where(hot, -BIG, 0.0).astype(BF16)

    apart = jnp.concatenate([jnp.zeros((LABELS, BEADS), BF16), jnp.full((LABELS, BEADS), -BIG, BF16)], axis=0)
    for p in range(PAD):
        same_ref[NC + p] = apart
    differ_ref[NC] = apart

    @pl.loop(0, (NC + PAD) // 4)
    def _(i):
        for j in range(4):
            acol_ref[i * 4 + j] = nil

    @pl.loop(0, NR // 8)
    def _(i):
        for j in range(8):
            arow_ref[i * 8 + j] = nil

    triangle = iota((128, 128), 0) < iota((128, 128), 1)
    empty = jnp.zeros((16, 128), BF16)

    def finish(z, diagonal=False):
        t = jnp.tanh(z)
        if diagonal:
            t = jnp.concatenate([jnp.where(triangle, t[:, :128], -1.0), t[:, 128:]], axis=1)
        return jnp.sum(t, axis=0, keepdims=True), (1.0 - t * t).astype(BF16)

    def weigh(sums, n):
        expect = 0.5 + (0.5 * (16384.0 + jnp.sum(sums, axis=1, keepdims=True))) / 128.0
        n = jnp.full((1, 128), n, I32).astype(F32)
        return jnp.broadcast_to(1.0 - n / jnp.broadcast_to(expect, (1, 128)), (8, 128))

    def unit_drain(g, sums, at, start, counts):
        far = [same_ref[start + m, 0:16] for m in range(2)]
        o = jnp.dot(lrow_ref[at], g, preferred_element_type=F32)
        spread = jnp.concatenate([jnp.concatenate([far[0], empty], axis=1),
                                  jnp.concatenate([empty, far[1]], axis=1)], axis=0)
        p = lax.dot_general(spread, g, NT, preferred_element_type=F32)
        w = [weigh(sums[:, m * 128:m * 128 + 128], counts[m]) for m in range(2)]
        arow_ref[at] += w[0] * (p[0:8] + p[8:16]) + w[1] * (p[16:24] + p[24:32])
        for m in range(2):
            lane = slice(m * 128, m * 128 + 128)
            acol_ref[start + m] += w[m] * (o[0:8, lane] + o[8:16, lane])

    def run(held, unit_at, trips, turns, diagonal):
        def body(it, held):
            for q in range(turns):
                zs, now = [], []
                for i in range(WIDE):
                    entry = unit_at((it * turns + q) * WIDE + i)
                    at, half = entry & (NR - 1), entry >> 8
                    k, u = at >> 5, at & 7
                    start = u * ROWS + 4 * ((at >> 3) & 3) + z + jnp.where(k > c, 1, 0) + 2 * half
                    start = jnp.where(entry < UNITS, start, NC)
                    lane = (at & 3) * 32 + ((c - k) & 7) + 16 * half
                    counts = [list_ref[TALLY + (at >> 2), lane + 8 * m] for m in range(2)]
                    right = jnp.concatenate([same_ref[start], same_ref[start + 1]], axis=1)
                    zs.append(jnp.dot(left_ref[at, :, 0:2 * LABELS], right, preferred_element_type=F32))
                    now.append((at, start, counts))
                for entry in held:
                    unit_drain(*entry)
                done = [finish(v, diagonal) for v in zs]
                held = [(done[i][1], done[i][0]) + now[i] for i in range(WIDE)]
            return held

        return lax.fori_loop(0, trips, body, held)

    def split(count):
        whole = count // (WIDE * LONG)
        done = whole * (WIDE * LONG)
        return whole, done, (count - done + WIDE * SHORT - 1) // (WIDE * SHORT)

    zero = jnp.int32(0)
    held = [(jnp.zeros((128, 256), BF16), jnp.zeros((1, 256), F32), zero, zero, [zero, zero])
            for _ in range(WIDE)]
    held = run(held, lambda i: c * (SIDE * U) + i, 1, SIDE * U // WIDE, True)
    whole, done, rest = split(list_ref[TOTALS, 1])
    held = run(held, lambda i: list_ref[UNIT + (i >> 7), i & 127], whole, LONG, False)
    held = run(held, lambda i: list_ref[UNIT + ((i + done) >> 7), (i + done) & 127], rest, SHORT, False)
    for entry in held:
        unit_drain(*entry)

    def listed_drain(held):
        for lo in range(0, WIDE, 2):
            pair = held[lo:lo + 2]
            near = jnp.concatenate([lrow_ref[p[2]] for p in pair], axis=0)
            far = jnp.concatenate([differ_ref[p[3], 0:16] for p in pair], axis=0)
            o = jnp.dot(near, jnp.concatenate([p[0] for p in pair], axis=1), preferred_element_type=F32)
            v = lax.dot_general(far, jnp.concatenate([p[0] for p in pair], axis=0), NT,
                                preferred_element_type=F32)
            for m, p in enumerate(pair):
                lane, at = slice(m * 128, m * 128 + 128), m * 16
                w = weigh(p[1], p[4])
                arow_ref[p[2]] += w * (v[at:at + 8, lane] + v[at + 8:at + 16, lane])
                acol_ref[p[3]] += w * (o[at:at + 8, lane] + o[at + 8:at + 16, lane])

    def listed_run(held, offset, trips, laps):
        def body(it, held):
            for q in range(laps):
                zs, now = [], []
                for i in range(WIDE):
                    slot = offset + (it * laps + q) * WIDE + i
                    line, lane = LISTED + (slot >> 7) * 8, slot & 127
                    at, to, n = [list_ref[line + f, lane] for f in range(3)]
                    zs.append(jnp.dot(left_ref[at, :, 0:2 * LABELS], differ_ref[to], preferred_element_type=F32))
                    now.append((at, to, n))
                listed_drain(held)
                done = [finish(v) for v in zs]
                held = [(done[i][1], done[i][0]) + now[i] for i in range(WIDE)]
            return held

        return lax.fori_loop(0, trips, body, held)

    held = [(jnp.zeros((128, 128), BF16), jnp.zeros((1, 128), F32), zero, zero, zero) for _ in range(WIDE)]
    whole, done, rest = split(list_ref[TOTALS, 0])
    held = listed_run(held, 0, whole, LONG)
    listed_drain(listed_run(held, done, rest, SHORT))

    @pl.loop(0, COLS)
    def _(k):
        for yy in range(SIDE):
            here = pl.ds((k * SIDE + yy) * U, U)
            mass = arow_ref[here, 3, :]
            for w in range(3):
                pulled = rows_ref[k, yy, w] * mass - arow_ref[here, w, :]
                prow_ref[k, yy, w] = pulled * (-1.0 / 512.0)

    @pl.loop(0, SIDE)
    def _(zz):
        for yy in range(SIDE):
            here = pl.ds(4 * yy + zz, U, stride=ROWS)
            mass = acol_ref[here, 4, :]
            for w in range(3):
                pulled = cols_ref[zz, yy, w] * mass - 2.0 * acol_ref[here, w, :]
                pcol_ref[zz, yy, w] = pulled * (-1.0 / 512.0)


def pairs_call(listing, bounds, rows, cols, left, lrow):
    return pl.pallas_call(
        pair_kernel,
        out_shape=[jax.ShapeDtypeStruct(rows.shape, F32), jax.ShapeDtypeStruct(cols.shape, F32)],
        in_specs=[SMEM] + [VMEM] * 5, out_specs=[VMEM] * 2,
        scratch_shapes=[
            pltpu.VMEM((SIDE, U, 24, BEADS), F32),
            pltpu.VMEM((NC + PAD + 2, 2 * LABELS, BEADS), BF16),
            pltpu.VMEM((NC + 1, 2 * LABELS, BEADS), BF16),
            pltpu.VMEM((NR, 8, BEADS), F32),
            pltpu.VMEM((NC + PAD + 2, 8, BEADS), F32),
        ],
        compiler_params=pltpu.CompilerParams(vmem_limit_bytes=32 << 20),
        name="pairs",
    )(listing, bounds, rows, cols, left, lrow)


def on_device(coords, chrom_lengths, band_counts, inter_pairs, inter_counts):
    part = coords.shape[1:]
    lens = chrom_lengths.reshape(1, -1)
    flipped = jnp.transpose(inter_pairs, (0, 2, 1))
    sems = 2 * SIDE + COLS + SIDE * (SIDE + COLS)
    rows, cols, listing, bounds, left, lrow = pl.pallas_call(
        gather_kernel,
        out_shape=[jax.ShapeDtypeStruct((COLS, SIDE) + part, F32), jax.ShapeDtypeStruct((SIDE, SIDE) + part, F32),
                   jax.ShapeDtypeStruct((LINES, 128), I32), jax.ShapeDtypeStruct((2, LABELS, BEADS), I32),
                   jax.ShapeDtypeStruct((NR, BEADS, 128), BF16), jax.ShapeDtypeStruct((NR, 16, BEADS), BF16)],
        in_specs=[HBM] * 5, out_specs=[VMEM] * 6,
        scratch_shapes=[
            pltpu.VMEM(lens.shape, I32),
            pltpu.VMEM(flipped.shape[1:], I32),
            pltpu.VMEM(inter_counts.shape, I32),
            pltpu.VMEM((3, 32, 128), I32),
            pltpu.VMEM((SIDE, U, 24, BEADS), F32),
            pltpu.VMEM((COLS,) + band_counts.shape, I32),
            pltpu.SemaphoreType.DMA((sems,)),
            pltpu.SemaphoreType.DMA((sems,)),
            pltpu.SemaphoreType.DMA((6,)),
        ],
        compiler_params=pltpu.CompilerParams(collective_id=0, has_side_effects=True, vmem_limit_bytes=24 << 20),
        name="gather",
    )(*[pltpu.with_memory_space_constraint(v, pltpu.HBM)
        for v in (coords, band_counts, lens, flipped, inter_counts)])
    prow, pcol = pairs_call(listing, bounds, rows, cols, left, lrow)
    return pl.pallas_call(
        scatter_kernel,
        out_shape=jax.ShapeDtypeStruct(coords.shape, F32),
        in_specs=[VMEM] * 2, out_specs=VMEM,
        scratch_shapes=[
            pltpu.VMEM((SIDE + COLS - 2, SIDE) + part, F32),
            pltpu.VMEM((2, SIDE) + part, F32),
            pltpu.VMEM((SIDE - 1,) + part, F32),
            pltpu.VMEM((SIDE - 1,) + part, F32),
            pltpu.SemaphoreType.DMA((SIDE * (SIDE + COLS) + SIDE,)),
            pltpu.SemaphoreType.DMA((SIDE * (SIDE + COLS) + SIDE,)),
            pltpu.SemaphoreType.DMA((2,)),
        ],
        compiler_params=pltpu.CompilerParams(collective_id=1, has_side_effects=True, vmem_limit_bytes=24 << 20),
        name="scatter",
    )(prow, pcol)


def solution(mesh):
    placed = (P(None, None, None, ("row", "col")), P(), P(None, None, ("row", "col"), None), P(), P())
    return jax.shard_map(on_device, mesh=mesh, in_specs=placed,
                         out_specs=P(None, None, None, ("row", "col")), check_vma=False)
```

```python
import jax
import jax.numpy as jnp
from jax import lax
from jax.experimental import pallas as pl
from jax.experimental.pallas import tpu as pltpu
from jax.sharding import PartitionSpec as P

MESH = pl.DeviceIdType.MESH
ROWS, COLS, SIDE = 16, 8, 4
U, BEADS = 8, 128
CAP = 256
LABELS = 48
NR, NC = SIDE * COLS * U, ROWS * U
UNITS = 2 * NR
PAD = 4
WIDE = 4
LONG, SHORT = 16, 2
BIG = 64.0
F32, BF16, I32 = jnp.float32, jnp.bfloat16, jnp.int32
HBM = pl.BlockSpec(memory_space=pltpu.HBM)
VMEM = pl.BlockSpec(memory_space=pltpu.VMEM)
SMEM = pl.BlockSpec(memory_space=pltpu.SMEM)
NT = (((1,), (1,)), ((), ()))
LISTED, TOTALS, WIDTHS, PLACE, TALLY, UNIT, LINES = 0, 16, 17, 19, 24, 88, 96


def iota(shape, axis):
    return lax.broadcasted_iota(I32, shape, axis)


def flag(x):
    return x.astype(F32).astype(BF16)


def chrom_bounds(lens_ref):
    lens = jnp.broadcast_to(lens_ref[...], (LABELS, lens_ref.shape[1]))
    sub, lane = iota(lens.shape, 0), iota(lens.shape, 1)
    ends = jnp.sum(jnp.where(lane <= sub, lens, 0), axis=1, keepdims=True)
    starts = jnp.sum(jnp.where(lane < sub, lens, 0), axis=1, keepdims=True)
    return starts, ends


def compact(mine, values, slots):
    count = mine.shape[0]
    a, b = iota((128, 128), 0), iota((128, 128), 1)
    within = jnp.dot(flag(mine), flag(a <= b), preferred_element_type=F32)
    total = jnp.dot(flag(mine), jnp.ones((128, 128), BF16), preferred_element_type=F32)
    lower = flag(iota((count, count), 1) < iota((count, count), 0))
    offset = jnp.dot(lower, total.astype(BF16), preferred_element_type=F32)
    place = jnp.where(mine, (offset + within).astype(I32) - 1, -1)
    values = [v.astype(F32) for v in values] + [mine.astype(F32)]
    slot = iota((slots, 128), 0)
    pad = jnp.zeros((16 - len(values), 128), F32)
    acc = jnp.zeros((16, slots), F32)
    for lo in range(0, count, 8):
        span = range(lo, min(lo + 8, count))
        hot = jnp.concatenate([flag(place[e:e + 1] == slot) for e in span], axis=1)
        rows = [jnp.concatenate([v[e:e + 1] for v in values] + [pad], axis=0) for e in span]
        acc = acc + lax.dot_general(jnp.concatenate(rows, axis=1).astype(BF16), hot, NT,
                                    preferred_element_type=F32)
    return acc[0:8]


def make_list(y, z, c, pairs_ref, count_ref, stage_ref, out_ref):
    for t in range(32):
        lane = slice(t * 128, t * 128 + 128)
        stage_ref[0, t:t + 1, :] = pairs_ref[0:1, lane]
        stage_ref[1, t:t + 1, :] = pairs_ref[1:2, lane]
        block = count_ref[:, lane]
        stage_ref[2, t:t + 1, :] = jnp.sum(jnp.where(iota(block.shape, 0) == y, block, 0), axis=0, keepdims=True)
    first, second, counts = stage_ref[0], stage_ref[1], stage_ref[2]
    mine = (((first >> 3) & 3) == z) & ((second & 7) == c)
    at = (first & 7) * 32 + ((first >> 5) & 3) * 8 + (first >> 7)
    acc = compact(mine, [at, second >> 3, counts], CAP)
    spare = jnp.where(iota((8, CAP), 0) == 1, NC * (1.0 - acc[3:4]), 0.0)
    found = (acc + spare).astype(I32)
    out_ref[LISTED:LISTED + 8, :] = found[:, 0:128]
    out_ref[LISTED + 8:LISTED + 16, :] = found[:, 128:256]
    listed = jnp.sum(found[3:4].astype(F32), axis=1, keepdims=True).astype(I32)
    out_ref[TOTALS:TOTALS + 1, :] = jnp.where(iota((1, 128), 1) == 0, listed, out_ref[TOTALS:TOTALS + 1, :])


def make_units(z, c, lens_ref, out_ref, bounds_ref):
    starts, ends = chrom_bounds(lens_ref)
    bounds_ref[0] = jnp.broadcast_to(starts, (LABELS, BEADS))
    bounds_ref[1] = jnp.broadcast_to(ends, (LABELS, BEADS))
    widths = []
    for i in range(2):
        at = iota((1, 128), 1) + i * 128
        k = at >> 5
        block = (at & 7) * 128 + (((at >> 3) & 3) * 4 + z) * 8 + k
        last = jnp.broadcast_to(block * 128 + 127, (LABELS, 128))
        stop = jnp.min(jnp.where(ends > last, ends, 1 << 20), axis=0, keepdims=True)
        far = jnp.minimum(jnp.minimum((stop - 1) >> 7, block + 31), 1023)
        widths.append(((far - block - ((c - k) & 7)) >> 3) + 1)
    width = jnp.concatenate(widths + widths, axis=0)
    entry = iota((4, 128), 0) * 128 + iota((4, 128), 1)
    near = (entry < NR) & (width > 0) & (((entry >> 5) & 7) != c)
    live = near | ((entry >= NR) & (width > 2))
    acc = compact(live, [entry >> 2, entry & 3], UNITS)
    units = acc[0:1] * 4.0 + acc[1:2] + UNITS * (1.0 - acc[2:3])
    for i in range(4):
        out_ref[UNIT + i:UNIT + i + 1, :] = units[:, i * 128:i * 128 + 128].astype(I32)
    out_ref[UNIT + 4:UNIT + 8, :] = jnp.zeros((4, 128), I32)
    active = jnp.sum(acc[2:3], axis=1, keepdims=True).astype(I32)
    lane = iota((1, 128), 1)
    out_ref[TOTALS:TOTALS + 1, :] = jnp.broadcast_to(active, (1, 128))
    out_ref[WIDTHS:WIDTHS + 2, :] = jnp.zeros((2, 128), I32)
    out_ref[PLACE:PLACE + 1, :] = jnp.where(lane == 0, z, c)
    out_ref[PLACE + 1:TALLY, :] = jnp.zeros((4, 128), I32)


def greet(r, c):
    y, z = r // SIDE, lax.rem(r, SIDE)
    peers = [(r, lax.rem(c + d, COLS)) for d in range(1, COLS)]
    peers += [(lax.rem(y + d, SIDE) * SIDE + z, c) for d in range(1, SIDE)]
    peers += [(y * SIDE + lax.rem(z + d, SIDE), c) for d in range(1, SIDE)]
    barrier = pltpu.get_barrier_semaphore()
    for peer in peers:
        pl.semaphore_signal(barrier, 1, device_id=peer, device_id_type=MESH)
    pl.semaphore_wait(barrier, len(peers))


def split3(x):
    a = x.astype(BF16).astype(F32)
    b = (x - a).astype(BF16).astype(F32)
    return a, b, (x - a) - b


def points_of(x, y, z):
    c = 0.75 - 0.25 * (x * x + y * y + z * z)
    return split3(x), split3(y), split3(z), split3(c)


def turn_rows(k, z, rows_ref, bounds_ref, tile_ref, left_ref, lrow_ref):
    starts, ends = bounds_ref[0], bounds_ref[1]
    lanes = iota((LABELS, BEADS), 1)
    for yy in range(SIDE):
        parts = points_of(rows_ref[k, yy, 0], rows_ref[k, yy, 1], rows_ref[k, yy, 2])
        for q in range(3):
            for w in range(4):
                value = parts[w][q]
                tile_ref[yy, :, 8 * q + w, :] = 0.5 * value if w < 3 else value
    for yy in range(SIDE):
        for u in range(U):
            at = (k * SIDE + yy) * U + u
            tiles = [tile_ref[yy, u, 8 * q:8 * q + 8] for q in range(3)]
            full = jnp.concatenate([tiles[j] for j in (0, 0, 1, 0, 2, 1)], axis=0).astype(BF16)
            bead = lanes + (u * 128 + (4 * yy + z) * 8 + k) * BEADS
            hot = jnp.where((bead >= starts) & (bead < ends), 1.0, 0.0).astype(BF16)
            lrow_ref[at] = jnp.concatenate(tiles[:2], axis=0).astype(BF16)
            left_ref[at] = jnp.concatenate([full, hot, jnp.zeros((32, 128), BF16)], axis=0).T


def gather_kernel(coords, counts, lens, pairs, inter, rows, cols, list_ref, bounds_ref, left_ref, lrow_ref,
                  lens_ref, pairs_ref, inter_ref, stage_ref, tile_ref, tallies, send, recv, local):
    r, c = lax.axis_index("row"), lax.axis_index("col")
    y, z = r // SIDE, lax.rem(r, SIDE)
    taken = [pltpu.make_async_copy(pairs.at[y], pairs_ref, local.at[0]),
             pltpu.make_async_copy(inter, inter_ref, local.at[1]),
             pltpu.make_async_copy(lens, lens_ref, local.at[5])]
    kept = [pltpu.make_async_copy(coords.at[y], rows.at[c, y], local.at[2]),
            pltpu.make_async_copy(counts.at[y], tallies.at[c, y], local.at[3])]
    for copy in kept + taken:
        copy.start()
    greet(r, c)

    def push(source, target, n, peer):
        return pltpu.make_async_remote_copy(source, target, send.at[n], recv.at[n],
                                            device_id=peer, device_id_type=MESH)

    early, talks = [], []
    for d in (1, 3, 2):
        to = lax.rem(y + d, SIDE)
        peer = (to * SIDE + z, c)
        early.append(push(coords.at[to], rows.at[c, y], d, peer))
        talks.append(push(counts.at[to], tallies.at[c, y], SIDE + d, peer))
    for copy in early:
        copy.start()
    late, across = [], []

    def spread(step):
        part = lax.rem(y + SIDE - step, SIDE)
        source = rows.at[c, part] if step else coords.at[y]
        base = 2 * SIDE + COLS + step * (SIDE + COLS)
        copies = [push(source, rows.at[c, part], base + SIDE + d, (r, lax.rem(c + d, COLS)))
                  for d in (4, 2, 6, 1, 3, 5, 7)]
        copies += [push(source, cols.at[z, part], base + d, (y * SIDE + lax.rem(z + d, SIDE), c))
                   for d in (1, 3, 2)]
        for copy in copies:
            copy.start()
        across.extend(copies[:COLS - 1])
        late.extend(copies[COLS - 1:])

    spread(0)
    for copy in talks:
        copy.start()
    taken[2].wait()
    make_units(z, c, lens_ref, list_ref, bounds_ref)
    for v in range(SIDE):
        for u in range(U):
            for q in range(3):
                tile_ref[v, u, 8 * q:8 * q + 8] = jnp.zeros((8, 128), F32)
    for v in range(SIDE):
        tile_ref[v, :, 4, :] = jnp.ones((8, 128), F32)
    for step, copy in zip((1, 3, 2), early):
        copy.wait_recv()
        spread(step)
    for copy in kept:
        copy.wait()
    same = pltpu.make_async_copy(rows.at[c], cols.at[z], local.at[4])
    same.start()
    for copy in talks:
        copy.wait_recv()
    talk = [push(tallies.at[c], tallies.at[c], 2 * SIDE + d, (r, lax.rem(c + d, COLS))) for d in range(1, COLS)]
    for copy in talk:
        copy.start()
    for copy in taken[:2]:
        copy.wait()
    make_list(y, z, c, pairs_ref, inter_ref, stage_ref, list_ref)
    turn_rows(c, z, rows, bounds_ref, tile_ref, left_ref, lrow_ref)

    def land(d, carry):
        k = lax.rem(c + COLS - d, COLS)
        for step in range(SIDE):
            n = 2 * SIDE + COLS + step * (SIDE + COLS) + SIDE + d
            push(coords.at[0], rows.at[k, lax.rem(y + SIDE - step, SIDE)], n, (r, lax.rem(c + d, COLS))).wait_recv()
        turn_rows(k, z, rows, bounds_ref, tile_ref, left_ref, lrow_ref)
        return carry

    lax.fori_loop(1, COLS, land, 0)
    for copy in talk:
        copy.wait_recv()
    for k in range(COLS):
        for yy in range(SIDE):
            for u in range(U):
                at = TALLY + k * 8 + yy * 2 + u // 4
                list_ref[at:at + 1, (u % 4) * 32:(u % 4) * 32 + 32] = tallies[k, yy, u]
    for copy in early + talks + talk + across:
        copy.wait_send()
    for copy in late:
        copy.wait()
    same.wait()


def scatter_kernel(rows, cols, out, land, own, total, last, send, recv, local):
    r, c = lax.axis_index("row"), lax.axis_index("col")
    y, z = r // SIDE, lax.rem(r, SIDE)
    kept = [pltpu.make_async_copy(rows.at[c], own.at[0], local.at[0]),
            pltpu.make_async_copy(cols.at[z], own.at[1], local.at[1])]
    for copy in kept:
        copy.start()
    greet(r, c)
    copies = []

    def push(source, target, n, peer):
        return pltpu.make_async_remote_copy(source, target, send.at[n], recv.at[n],
                                            device_id=peer, device_id_type=MESH)

    order = (2, 1, 3, 0)
    for turn in order:
        part, base = lax.rem(y + turn, SIDE), turn * (SIDE + COLS)
        group = []
        for d in (4, 2, 6, 1, 3, 5, 7):
            to = lax.rem(c + d, COLS)
            group.append(push(rows.at[to, part], land.at[SIDE - 2 + d, part], base + SIDE + d, (r, to)))
        for d in (1, 3, 2):
            to = lax.rem(z + d, SIDE)
            group.append(push(cols.at[to, part], land.at[d - 1, part], base + d, (y * SIDE + to, c)))
        for copy in group:
            copy.start()
        copies.append(group)
    for copy in kept:
        copy.wait()
    second = []
    for turn, group in zip(order, copies):
        part = lax.rem(y + turn, SIDE)
        for copy in group:
            copy.wait_recv()
        sums = [own[0, part] + own[1, part]] + [land[d, part] for d in range(SIDE + COLS - 2)]
        while len(sums) > 1:
            sums = [a + b for a, b in zip(sums[::2], sums[1::2])] + sums[len(sums) - len(sums) % 2:]
        if turn == 0:
            out[y] = sums[0]
        else:
            total[turn - 1] = sums[0]
            copy = push(total.at[turn - 1], last.at[turn - 1], SIDE * (SIDE + COLS) + turn, (part * SIDE + z, c))
            copy.start()
            second.append((turn, copy))
    for turn, copy in second:
        copy.wait_recv()
        out[lax.rem(y + SIDE - turn, SIDE)] = last[turn - 1]
    for copy in [copy for group in copies for copy in group] + [copy for _, copy in second]:
        copy.wait_send()


def pair_kernel(list_ref, bounds_ref, rows_ref, cols_ref, left_ref, lrow_ref, prow_ref, pcol_ref,
                tile_ref, same_ref, differ_ref, arow_ref, acol_ref):
    z, c = list_ref[PLACE, 0], list_ref[PLACE, 1]
    starts, ends = bounds_ref[0], bounds_ref[1]
    lanes = iota((LABELS, BEADS), 1)
    one = jnp.ones((8, 128), F32)
    nil = jnp.zeros((8, 128), F32)

    def hot_of(block):
        bead = lanes + block * BEADS
        return (bead >= starts) & (bead < ends)

    for v in range(SIDE):
        for u in range(U):
            for q in range(3):
                tile_ref[v, u, 8 * q:8 * q + 8] = nil

    for v in range(SIDE):
        tile_ref[v, :, 3, :] = one

    @pl.loop(0, SIDE)
    def _(zz):
        for yy in range(SIDE):
            parts = points_of(cols_ref[zz, yy, 0], cols_ref[zz, yy, 1], cols_ref[zz, yy, 2])
            for q in range(3):
                for w in range(4):
                    tile_ref[yy, :, 8 * q + (w if w < 3 else 4), :] = parts[w][q]
        for yy in range(SIDE):
            for u in range(U):
                at = u * ROWS + 4 * yy + zz
                tiles = [tile_ref[yy, u, 8 * q:8 * q + 8] for q in range(3)]
                full = jnp.concatenate([tiles[i] for i in (0, 1, 0, 2, 0, 1)], axis=0).astype(BF16)
                hot = hot_of(at * 8 + c)
                same_ref[at, 0:LABELS] = full
                differ_ref[at, 0:LABELS] = full
                same_ref[at, LABELS:] = jnp.where(hot, 0.0, -BIG).astype(BF16)
                differ_ref[at, LABELS:] = jnp.where(hot, -BIG, 0.0).astype(BF16)

    apart = jnp.concatenate([jnp.zeros((LABELS, BEADS), BF16), jnp.full((LABELS, BEADS), -BIG, BF16)], axis=0)
    for p in range(PAD):
        same_ref[NC + p] = apart
    differ_ref[NC] = apart

    @pl.loop(0, (NC + PAD) // 4)
    def _(i):
        for j in range(4):
            acol_ref[i * 4 + j] = nil

    @pl.loop(0, NR // 8)
    def _(i):
        for j in range(8):
            arow_ref[i * 8 + j] = nil

    triangle = iota((128, 128), 0) < iota((128, 128), 1)
    empty = jnp.zeros((16, 128), BF16)

    def finish(z, diagonal=False):
        t = jnp.tanh(z)
        if diagonal:
            t = jnp.concatenate([jnp.where(triangle, t[:, :128], -1.0), t[:, 128:]], axis=1)
        return jnp.sum(t, axis=0, keepdims=True), (1.0 - t * t).astype(BF16)

    def weigh(sums, n):
        expect = 0.5 + (0.5 * (16384.0 + jnp.sum(sums, axis=1, keepdims=True))) / 128.0
        n = jnp.full((1, 128), n, I32).astype(F32)
        return jnp.broadcast_to(1.0 - n / jnp.broadcast_to(expect, (1, 128)), (8, 128))

    def unit_drain(g, sums, at, start, counts):
        far = [same_ref[start + m, 0:16] for m in range(2)]
        o = jnp.dot(lrow_ref[at], g, preferred_element_type=F32)
        spread = jnp.concatenate([jnp.concatenate([far[0], empty], axis=1),
                                  jnp.concatenate([empty, far[1]], axis=1)], axis=0)
        p = lax.dot_general(spread, g, NT, preferred_element_type=F32)
        w = [weigh(sums[:, m * 128:m * 128 + 128], counts[m]) for m in range(2)]
        arow_ref[at] += w[0] * (p[0:8] + p[8:16]) + w[1] * (p[16:24] + p[24:32])
        for m in range(2):
            lane = slice(m * 128, m * 128 + 128)
            acol_ref[start + m] += w[m] * (o[0:8, lane] + o[8:16, lane])

    def run(held, unit_at, trips, turns, diagonal):
        def body(it, held):
            for q in range(turns):
                zs, now = [], []
                for i in range(WIDE):
                    entry = unit_at((it * turns + q) * WIDE + i)
                    at, half = entry & (NR - 1), entry >> 8
                    k, u = at >> 5, at & 7
                    start = u * ROWS + 4 * ((at >> 3) & 3) + z + jnp.where(k > c, 1, 0) + 2 * half
                    start = jnp.where(entry < UNITS, start, NC)
                    lane = (at & 3) * 32 + ((c - k) & 7) + 16 * half
                    counts = [list_ref[TALLY + (at >> 2), lane + 8 * m] for m in range(2)]
                    right = jnp.concatenate([same_ref[start], same_ref[start + 1]], axis=1)
                    zs.append(jnp.dot(left_ref[at, :, 0:2 * LABELS], right, preferred_element_type=F32))
                    now.append((at, start, counts))
                for entry in held:
                    unit_drain(*entry)
                done = [finish(v, diagonal) for v in zs]
                held = [(done[i][1], done[i][0]) + now[i] for i in range(WIDE)]
            return held

        return lax.fori_loop(0, trips, body, held)

    def split(count):
        whole = count // (WIDE * LONG)
        done = whole * (WIDE * LONG)
        return whole, done, (count - done + WIDE * SHORT - 1) // (WIDE * SHORT)

    zero = jnp.int32(0)
    held = [(jnp.zeros((128, 256), BF16), jnp.zeros((1, 256), F32), zero, zero, [zero, zero])
            for _ in range(WIDE)]
    held = run(held, lambda i: c * (SIDE * U) + i, 1, SIDE * U // WIDE, True)
    whole, done, rest = split(list_ref[TOTALS, 1])
    held = run(held, lambda i: list_ref[UNIT + (i >> 7), i & 127], whole, LONG, False)
    held = run(held, lambda i: list_ref[UNIT + ((i + done) >> 7), (i + done) & 127], rest, SHORT, False)
    for entry in held:
        unit_drain(*entry)

    def listed_drain(held):
        for lo in range(0, WIDE, 2):
            pair = held[lo:lo + 2]
            near = jnp.concatenate([lrow_ref[p[2]] for p in pair], axis=0)
            far = jnp.concatenate([differ_ref[p[3], 0:16] for p in pair], axis=0)
            o = jnp.dot(near, jnp.concatenate([p[0] for p in pair], axis=1), preferred_element_type=F32)
            v = lax.dot_general(far, jnp.concatenate([p[0] for p in pair], axis=0), NT,
                                preferred_element_type=F32)
            for m, p in enumerate(pair):
                lane, at = slice(m * 128, m * 128 + 128), m * 16
                w = weigh(p[1], p[4])
                arow_ref[p[2]] += w * (v[at:at + 8, lane] + v[at + 8:at + 16, lane])
                acol_ref[p[3]] += w * (o[at:at + 8, lane] + o[at + 8:at + 16, lane])

    def listed_run(held, offset, trips, laps):
        def body(it, held):
            for q in range(laps):
                zs, now = [], []
                for i in range(WIDE):
                    slot = offset + (it * laps + q) * WIDE + i
                    line, lane = LISTED + (slot >> 7) * 8, slot & 127
                    at, to, n = [list_ref[line + f, lane] for f in range(3)]
                    zs.append(jnp.dot(left_ref[at, :, 0:2 * LABELS], differ_ref[to], preferred_element_type=F32))
                    now.append((at, to, n))
                listed_drain(held)
                done = [finish(v) for v in zs]
                held = [(done[i][1], done[i][0]) + now[i] for i in range(WIDE)]
            return held

        return lax.fori_loop(0, trips, body, held)

    held = [(jnp.zeros((128, 128), BF16), jnp.zeros((1, 128), F32), zero, zero, zero) for _ in range(WIDE)]
    whole, done, rest = split(list_ref[TOTALS, 0])
    held = listed_run(held, 0, whole, LONG)
    listed_drain(listed_run(held, done, rest, SHORT))

    @pl.loop(0, COLS)
    def _(k):
        for yy in range(SIDE):
            here = pl.ds((k * SIDE + yy) * U, U)
            mass = arow_ref[here, 3, :]
            for w in range(3):
                pulled = rows_ref[k, yy, w] * mass - arow_ref[here, w, :]
                prow_ref[k, yy, w] = pulled * (-1.0 / 512.0)

    @pl.loop(0, SIDE)
    def _(zz):
        for yy in range(SIDE):
            here = pl.ds(4 * yy + zz, U, stride=ROWS)
            mass = acol_ref[here, 4, :]
            for w in range(3):
                pulled = cols_ref[zz, yy, w] * mass - 2.0 * acol_ref[here, w, :]
                pcol_ref[zz, yy, w] = pulled * (-1.0 / 512.0)


def pairs_call(listing, bounds, rows, cols, left, lrow):
    return pl.pallas_call(
        pair_kernel,
        out_shape=[jax.ShapeDtypeStruct(rows.shape, F32), jax.ShapeDtypeStruct(cols.shape, F32)],
        in_specs=[SMEM] + [VMEM] * 5, out_specs=[VMEM] * 2,
        scratch_shapes=[
            pltpu.VMEM((SIDE, U, 24, BEADS), F32),
            pltpu.VMEM((NC + PAD + 2, 2 * LABELS, BEADS), BF16),
            pltpu.VMEM((NC + 1, 2 * LABELS, BEADS), BF16),
            pltpu.VMEM((NR, 8, BEADS), F32),
            pltpu.VMEM((NC + PAD + 2, 8, BEADS), F32),
        ],
        compiler_params=pltpu.CompilerParams(vmem_limit_bytes=32 << 20),
        name="pairs",
    )(listing, bounds, rows, cols, left, lrow)


def on_device(coords, chrom_lengths, band_counts, inter_pairs, inter_counts):
    part = coords.shape[1:]
    lens = chrom_lengths.reshape(1, -1)
    flipped = jnp.transpose(inter_pairs, (0, 2, 1))
    sems = 2 * SIDE + COLS + SIDE * (SIDE + COLS)
    rows, cols, listing, bounds, left, lrow = pl.pallas_call(
        gather_kernel,
        out_shape=[jax.ShapeDtypeStruct((COLS, SIDE) + part, F32), jax.ShapeDtypeStruct((SIDE, SIDE) + part, F32),
                   jax.ShapeDtypeStruct((LINES, 128), I32), jax.ShapeDtypeStruct((2, LABELS, BEADS), I32),
                   jax.ShapeDtypeStruct((NR, BEADS, 128), BF16), jax.ShapeDtypeStruct((NR, 16, BEADS), BF16)],
        in_specs=[HBM] * 5, out_specs=[VMEM] * 6,
        scratch_shapes=[
            pltpu.VMEM(lens.shape, I32),
            pltpu.VMEM(flipped.shape[1:], I32),
            pltpu.VMEM(inter_counts.shape, I32),
            pltpu.VMEM((3, 32, 128), I32),
            pltpu.VMEM((SIDE, U, 24, BEADS), F32),
            pltpu.VMEM((COLS,) + band_counts.shape, I32),
            pltpu.SemaphoreType.DMA((sems,)),
            pltpu.SemaphoreType.DMA((sems,)),
            pltpu.SemaphoreType.DMA((6,)),
        ],
        compiler_params=pltpu.CompilerParams(collective_id=0, has_side_effects=True, vmem_limit_bytes=24 << 20),
        name="gather",
    )(*[pltpu.with_memory_space_constraint(v, pltpu.HBM)
        for v in (coords, band_counts, lens, flipped, inter_counts)])
    prow, pcol = pairs_call(listing, bounds, rows, cols, left, lrow)
    return pl.pallas_call(
        scatter_kernel,
        out_shape=jax.ShapeDtypeStruct(coords.shape, F32),
        in_specs=[VMEM] * 2, out_specs=VMEM,
        scratch_shapes=[
            pltpu.VMEM((SIDE + COLS - 2, SIDE) + part, F32),
            pltpu.VMEM((2, SIDE) + part, F32),
            pltpu.VMEM((SIDE - 1,) + part, F32),
            pltpu.VMEM((SIDE - 1,) + part, F32),
            pltpu.SemaphoreType.DMA((SIDE * (SIDE + COLS) + SIDE,)),
            pltpu.SemaphoreType.DMA((SIDE * (SIDE + COLS) + SIDE,)),
            pltpu.SemaphoreType.DMA((2,)),
        ],
        compiler_params=pltpu.CompilerParams(collective_id=1, has_side_effects=True, vmem_limit_bytes=24 << 20),
        name="scatter",
    )(prow, pcol)


def solution(mesh):
    placed = (P(None, None, None, ("row", "col")), P(), P(None, None, ("row", "col"), None), P(), P())
    return jax.shard_map(on_device, mesh=mesh, in_specs=placed,
                         out_specs=P(None, None, None, ("row", "col")), check_vma=False)
```

```python
import jax
import jax.numpy as jnp
from jax import lax
from jax.experimental import pallas as pl
from jax.experimental.pallas import tpu as pltpu
from jax.sharding import PartitionSpec as P

MESH = pl.DeviceIdType.MESH
ROWS, COLS, SIDE = 16, 8, 4
U, BEADS = 8, 128
CAP = 256
LABELS = 48
NR, NC = SIDE * COLS * U, ROWS * U
UNITS = 2 * NR
PAD = 4
WIDE = 4
LONG, SHORT = 16, 4
BIG = 64.0
F32, BF16, I32 = jnp.float32, jnp.bfloat16, jnp.int32
HBM = pl.BlockSpec(memory_space=pltpu.HBM)
VMEM = pl.BlockSpec(memory_space=pltpu.VMEM)
SMEM = pl.BlockSpec(memory_space=pltpu.SMEM)
NT = (((1,), (1,)), ((), ()))
LISTED, TOTALS, WIDTHS, PLACE, TALLY, UNIT, LINES = 0, 16, 17, 19, 24, 88, 96


def iota(shape, axis):
    return lax.broadcasted_iota(I32, shape, axis)


def flag(x):
    return x.astype(F32).astype(BF16)


def chrom_bounds(lens_ref):
    lens = jnp.broadcast_to(lens_ref[...], (LABELS, lens_ref.shape[1]))
    sub, lane = iota(lens.shape, 0), iota(lens.shape, 1)
    ends = jnp.sum(jnp.where(lane <= sub, lens, 0), axis=1, keepdims=True)
    starts = jnp.sum(jnp.where(lane < sub, lens, 0), axis=1, keepdims=True)
    return starts, ends


def compact(mine, values, slots):
    count = mine.shape[0]
    a, b = iota((128, 128), 0), iota((128, 128), 1)
    within = jnp.dot(flag(mine), flag(a <= b), preferred_element_type=F32)
    total = jnp.dot(flag(mine), jnp.ones((128, 128), BF16), preferred_element_type=F32)
    lower = flag(iota((count, count), 1) < iota((count, count), 0))
    offset = jnp.dot(lower, total.astype(BF16), preferred_element_type=F32)
    place = jnp.where(mine, (offset + within).astype(I32) - 1, -1)
    values = [v.astype(F32) for v in values] + [mine.astype(F32)]
    slot = iota((slots, 128), 0)
    pad = jnp.zeros((16 - len(values), 128), F32)
    acc = jnp.zeros((16, slots), F32)
    for lo in range(0, count, 8):
        span = range(lo, min(lo + 8, count))
        hot = jnp.concatenate([flag(place[e:e + 1] == slot) for e in span], axis=1)
        rows = [jnp.concatenate([v[e:e + 1] for v in values] + [pad], axis=0) for e in span]
        acc = acc + lax.dot_general(jnp.concatenate(rows, axis=1).astype(BF16), hot, NT,
                                    preferred_element_type=F32)
    return acc[0:8]


def make_list(y, z, c, pairs_ref, count_ref, stage_ref, out_ref):
    for t in range(32):
        lane = slice(t * 128, t * 128 + 128)
        stage_ref[0, t:t + 1, :] = pairs_ref[0:1, lane]
        stage_ref[1, t:t + 1, :] = pairs_ref[1:2, lane]
        block = count_ref[:, lane]
        stage_ref[2, t:t + 1, :] = jnp.sum(jnp.where(iota(block.shape, 0) == y, block, 0), axis=0, keepdims=True)
    first, second, counts = stage_ref[0], stage_ref[1], stage_ref[2]
    mine = (((first >> 3) & 3) == z) & ((second & 7) == c)
    at = (first & 7) * 32 + ((first >> 5) & 3) * 8 + (first >> 7)
    acc = compact(mine, [at, second >> 3, counts], CAP)
    spare = jnp.where(iota((8, CAP), 0) == 1, NC * (1.0 - acc[3:4]), 0.0)
    found = (acc + spare).astype(I32)
    out_ref[LISTED:LISTED + 8, :] = found[:, 0:128]
    out_ref[LISTED + 8:LISTED + 16, :] = found[:, 128:256]
    listed = jnp.sum(found[3:4].astype(F32), axis=1, keepdims=True).astype(I32)
    out_ref[TOTALS:TOTALS + 1, :] = jnp.where(iota((1, 128), 1) == 0, listed, out_ref[TOTALS:TOTALS + 1, :])


def make_units(z, c, lens_ref, out_ref, bounds_ref):
    starts, ends = chrom_bounds(lens_ref)
    bounds_ref[0] = jnp.broadcast_to(starts, (LABELS, BEADS))
    bounds_ref[1] = jnp.broadcast_to(ends, (LABELS, BEADS))
    widths = []
    for i in range(2):
        at = iota((1, 128), 1) + i * 128
        k = at >> 5
        block = (at & 7) * 128 + (((at >> 3) & 3) * 4 + z) * 8 + k
        last = jnp.broadcast_to(block * 128 + 127, (LABELS, 128))
        stop = jnp.min(jnp.where(ends > last, ends, 1 << 20), axis=0, keepdims=True)
        far = jnp.minimum(jnp.minimum((stop - 1) >> 7, block + 31), 1023)
        widths.append(((far - block - ((c - k) & 7)) >> 3) + 1)
    width = jnp.concatenate(widths + widths, axis=0)
    entry = iota((4, 128), 0) * 128 + iota((4, 128), 1)
    near = (entry < NR) & (width > 0) & (((entry >> 5) & 7) != c)
    live = near | ((entry >= NR) & (width > 2))
    acc = compact(live, [entry >> 2, entry & 3], UNITS)
    units = acc[0:1] * 4.0 + acc[1:2] + UNITS * (1.0 - acc[2:3])
    for i in range(4):
        out_ref[UNIT + i:UNIT + i + 1, :] = units[:, i * 128:i * 128 + 128].astype(I32)
    out_ref[UNIT + 4:UNIT + 8, :] = jnp.zeros((4, 128), I32)
    active = jnp.sum(acc[2:3], axis=1, keepdims=True).astype(I32)
    lane = iota((1, 128), 1)
    out_ref[TOTALS:TOTALS + 1, :] = jnp.broadcast_to(active, (1, 128))
    out_ref[WIDTHS:WIDTHS + 2, :] = jnp.zeros((2, 128), I32)
    out_ref[PLACE:PLACE + 1, :] = jnp.where(lane == 0, z, c)
    out_ref[PLACE + 1:TALLY, :] = jnp.zeros((4, 128), I32)


def greet(r, c):
    y, z = r // SIDE, lax.rem(r, SIDE)
    peers = [(r, lax.rem(c + d, COLS)) for d in range(1, COLS)]
    peers += [(lax.rem(y + d, SIDE) * SIDE + z, c) for d in range(1, SIDE)]
    peers += [(y * SIDE + lax.rem(z + d, SIDE), c) for d in range(1, SIDE)]
    barrier = pltpu.get_barrier_semaphore()
    for peer in peers:
        pl.semaphore_signal(barrier, 1, device_id=peer, device_id_type=MESH)
    pl.semaphore_wait(barrier, len(peers))


def split3(x):
    a = x.astype(BF16).astype(F32)
    b = (x - a).astype(BF16).astype(F32)
    return a, b, (x - a) - b


def points_of(x, y, z):
    c = 0.75 - 0.25 * (x * x + y * y + z * z)
    return split3(x), split3(y), split3(z), split3(c)


def turn_rows(k, z, rows_ref, bounds_ref, tile_ref, left_ref, lrow_ref):
    starts, ends = bounds_ref[0], bounds_ref[1]
    lanes = iota((LABELS, BEADS), 1)
    for yy in range(SIDE):
        parts = points_of(rows_ref[k, yy, 0], rows_ref[k, yy, 1], rows_ref[k, yy, 2])
        for q in range(3):
            for w in range(4):
                value = parts[w][q]
                tile_ref[yy, :, 8 * q + w, :] = 0.5 * value if w < 3 else value
    for yy in range(SIDE):
        for u in range(U):
            at = (k * SIDE + yy) * U + u
            tiles = [tile_ref[yy, u, 8 * q:8 * q + 8] for q in range(3)]
            full = jnp.concatenate([tiles[j] for j in (0, 0, 1, 0, 2, 1)], axis=0).astype(BF16)
            bead = lanes + (u * 128 + (4 * yy + z) * 8 + k) * BEADS
            hot = jnp.where((bead >= starts) & (bead < ends), 1.0, 0.0).astype(BF16)
            lrow_ref[at] = jnp.concatenate(tiles[:2], axis=0).astype(BF16)
            left_ref[at] = jnp.concatenate([full, hot, jnp.zeros((32, 128), BF16)], axis=0).T


def gather_kernel(coords, counts, lens, pairs, inter, rows, cols, list_ref, bounds_ref, left_ref, lrow_ref,
                  lens_ref, pairs_ref, inter_ref, stage_ref, tile_ref, tallies, send, recv, local):
    r, c = lax.axis_index("row"), lax.axis_index("col")
    y, z = r // SIDE, lax.rem(r, SIDE)
    taken = [pltpu.make_async_copy(pairs.at[y], pairs_ref, local.at[0]),
             pltpu.make_async_copy(inter, inter_ref, local.at[1]),
             pltpu.make_async_copy(lens, lens_ref, local.at[5])]
    kept = [pltpu.make_async_copy(coords.at[y], rows.at[c, y], local.at[2]),
            pltpu.make_async_copy(counts.at[y], tallies.at[c, y], local.at[3])]
    for copy in kept + taken:
        copy.start()
    greet(r, c)

    def push(source, target, n, peer):
        return pltpu.make_async_remote_copy(source, target, send.at[n], recv.at[n],
                                            device_id=peer, device_id_type=MESH)

    early, talks = [], []
    for d in (1, 3, 2):
        to = lax.rem(y + d, SIDE)
        peer = (to * SIDE + z, c)
        early.append(push(coords.at[to], rows.at[c, y], d, peer))
        talks.append(push(counts.at[to], tallies.at[c, y], SIDE + d, peer))
    for copy in early:
        copy.start()
    late, across = [], []

    def spread(step):
        part = lax.rem(y + SIDE - step, SIDE)
        source = rows.at[c, part] if step else coords.at[y]
        base = 2 * SIDE + COLS + step * (SIDE + COLS)
        copies = [push(source, rows.at[c, part], base + SIDE + d, (r, lax.rem(c + d, COLS)))
                  for d in (4, 2, 6, 1, 3, 5, 7)]
        copies += [push(source, cols.at[z, part], base + d, (y * SIDE + lax.rem(z + d, SIDE), c))
                   for d in (1, 3, 2)]
        for copy in copies:
            copy.start()
        across.extend(copies[:COLS - 1])
        late.extend(copies[COLS - 1:])

    spread(0)
    for copy in talks:
        copy.start()
    taken[2].wait()
    make_units(z, c, lens_ref, list_ref, bounds_ref)
    for v in range(SIDE):
        for u in range(U):
            for q in range(3):
                tile_ref[v, u, 8 * q:8 * q + 8] = jnp.zeros((8, 128), F32)
    for v in range(SIDE):
        tile_ref[v, :, 4, :] = jnp.ones((8, 128), F32)
    for step, copy in zip((1, 3, 2), early):
        copy.wait_recv()
        spread(step)
    for copy in kept:
        copy.wait()
    same = pltpu.make_async_copy(rows.at[c], cols.at[z], local.at[4])
    same.start()
    for copy in talks:
        copy.wait_recv()
    talk = [push(tallies.at[c], tallies.at[c], 2 * SIDE + d, (r, lax.rem(c + d, COLS))) for d in range(1, COLS)]
    for copy in talk:
        copy.start()
    for copy in taken[:2]:
        copy.wait()
    make_list(y, z, c, pairs_ref, inter_ref, stage_ref, list_ref)
    turn_rows(c, z, rows, bounds_ref, tile_ref, left_ref, lrow_ref)

    def land(d, carry):
        k = lax.rem(c + COLS - d, COLS)
        for step in range(SIDE):
            n = 2 * SIDE + COLS + step * (SIDE + COLS) + SIDE + d
            push(coords.at[0], rows.at[k, lax.rem(y + SIDE - step, SIDE)], n, (r, lax.rem(c + d, COLS))).wait_recv()
        turn_rows(k, z, rows, bounds_ref, tile_ref, left_ref, lrow_ref)
        return carry

    lax.fori_loop(1, COLS, land, 0)
    for copy in talk:
        copy.wait_recv()
    for k in range(COLS):
        for yy in range(SIDE):
            for u in range(U):
                at = TALLY + k * 8 + yy * 2 + u // 4
                list_ref[at:at + 1, (u % 4) * 32:(u % 4) * 32 + 32] = tallies[k, yy, u]
    for copy in early + talks + talk + across:
        copy.wait_send()
    for copy in late:
        copy.wait()
    same.wait()


def scatter_kernel(rows, cols, out, land, own, total, last, send, recv, local):
    r, c = lax.axis_index("row"), lax.axis_index("col")
    y, z = r // SIDE, lax.rem(r, SIDE)
    kept = [pltpu.make_async_copy(rows.at[c], own.at[0], local.at[0]),
            pltpu.make_async_copy(cols.at[z], own.at[1], local.at[1])]
    for copy in kept:
        copy.start()
    greet(r, c)
    copies = []

    def push(source, target, n, peer):
        return pltpu.make_async_remote_copy(source, target, send.at[n], recv.at[n],
                                            device_id=peer, device_id_type=MESH)

    order = (2, 1, 3, 0)
    for turn in order:
        part, base = lax.rem(y + turn, SIDE), turn * (SIDE + COLS)
        group = []
        for d in (4, 2, 6, 1, 3, 5, 7):
            to = lax.rem(c + d, COLS)
            group.append(push(rows.at[to, part], land.at[SIDE - 2 + d, part], base + SIDE + d, (r, to)))
        for d in (1, 3, 2):
            to = lax.rem(z + d, SIDE)
            group.append(push(cols.at[to, part], land.at[d - 1, part], base + d, (y * SIDE + to, c)))
        for copy in group:
            copy.start()
        copies.append(group)
    for copy in kept:
        copy.wait()
    second = []
    for turn, group in zip(order, copies):
        part = lax.rem(y + turn, SIDE)
        for copy in group:
            copy.wait_recv()
        sums = [own[0, part] + own[1, part]] + [land[d, part] for d in range(SIDE + COLS - 2)]
        while len(sums) > 1:
            sums = [a + b for a, b in zip(sums[::2], sums[1::2])] + sums[len(sums) - len(sums) % 2:]
        if turn == 0:
            out[y] = sums[0]
        else:
            total[turn - 1] = sums[0]
            copy = push(total.at[turn - 1], last.at[turn - 1], SIDE * (SIDE + COLS) + turn, (part * SIDE + z, c))
            copy.start()
            second.append((turn, copy))
    for turn, copy in second:
        copy.wait_recv()
        out[lax.rem(y + SIDE - turn, SIDE)] = last[turn - 1]
    for copy in [copy for group in copies for copy in group] + [copy for _, copy in second]:
        copy.wait_send()


def pair_kernel(list_ref, bounds_ref, rows_ref, cols_ref, left_ref, lrow_ref, prow_ref, pcol_ref,
                tile_ref, same_ref, differ_ref, arow_ref, acol_ref):
    z, c = list_ref[PLACE, 0], list_ref[PLACE, 1]
    starts, ends = bounds_ref[0], bounds_ref[1]
    lanes = iota((LABELS, BEADS), 1)
    one = jnp.ones((8, 128), F32)
    nil = jnp.zeros((8, 128), F32)

    def hot_of(block):
        bead = lanes + block * BEADS
        return (bead >= starts) & (bead < ends)

    for v in range(SIDE):
        for u in range(U):
            for q in range(3):
                tile_ref[v, u, 8 * q:8 * q + 8] = nil

    for v in range(SIDE):
        tile_ref[v, :, 3, :] = one

    @pl.loop(0, SIDE)
    def _(zz):
        for yy in range(SIDE):
            parts = points_of(cols_ref[zz, yy, 0], cols_ref[zz, yy, 1], cols_ref[zz, yy, 2])
            for q in range(3):
                for w in range(4):
                    tile_ref[yy, :, 8 * q + (w if w < 3 else 4), :] = parts[w][q]
        for yy in range(SIDE):
            for u in range(U):
                at = u * ROWS + 4 * yy + zz
                tiles = [tile_ref[yy, u, 8 * q:8 * q + 8] for q in range(3)]
                full = jnp.concatenate([tiles[i] for i in (0, 1, 0, 2, 0, 1)], axis=0).astype(BF16)
                hot = hot_of(at * 8 + c)
                same_ref[at, 0:LABELS] = full
                differ_ref[at, 0:LABELS] = full
                same_ref[at, LABELS:] = jnp.where(hot, 0.0, -BIG).astype(BF16)
                differ_ref[at, LABELS:] = jnp.where(hot, -BIG, 0.0).astype(BF16)

    apart = jnp.concatenate([jnp.zeros((LABELS, BEADS), BF16), jnp.full((LABELS, BEADS), -BIG, BF16)], axis=0)
    for p in range(PAD):
        same_ref[NC + p] = apart
    differ_ref[NC] = apart

    @pl.loop(0, (NC + PAD) // 4)
    def _(i):
        for j in range(4):
            acol_ref[i * 4 + j] = nil

    @pl.loop(0, NR // 8)
    def _(i):
        for j in range(8):
            arow_ref[i * 8 + j] = nil

    triangle = iota((128, 128), 0) < iota((128, 128), 1)
    empty = jnp.zeros((16, 128), BF16)

    def finish(z, diagonal=False):
        t = jnp.tanh(z)
        if diagonal:
            t = jnp.concatenate([jnp.where(triangle, t[:, :128], -1.0), t[:, 128:]], axis=1)
        return jnp.sum(t, axis=0, keepdims=True), (1.0 - t * t).astype(BF16)

    def weigh(sums, n):
        expect = 0.5 + (0.5 * (16384.0 + jnp.sum(sums, axis=1, keepdims=True))) / 128.0
        n = jnp.full((1, 128), n, I32).astype(F32)
        return jnp.broadcast_to(1.0 - n / jnp.broadcast_to(expect, (1, 128)), (8, 128))

    def unit_drain(g, sums, at, start, counts):
        far = [same_ref[start + m, 0:16] for m in range(2)]
        o = jnp.dot(lrow_ref[at], g, preferred_element_type=F32)
        spread = jnp.concatenate([jnp.concatenate([far[0], empty], axis=1),
                                  jnp.concatenate([empty, far[1]], axis=1)], axis=0)
        p = lax.dot_general(spread, g, NT, preferred_element_type=F32)
        w = [weigh(sums[:, m * 128:m * 128 + 128], counts[m]) for m in range(2)]
        arow_ref[at] += w[0] * (p[0:8] + p[8:16]) + w[1] * (p[16:24] + p[24:32])
        for m in range(2):
            lane = slice(m * 128, m * 128 + 128)
            acol_ref[start + m] += w[m] * (o[0:8, lane] + o[8:16, lane])

    def run(held, unit_at, trips, turns, diagonal):
        def body(it, held):
            for q in range(turns):
                zs, now = [], []
                for i in range(WIDE):
                    entry = unit_at((it * turns + q) * WIDE + i)
                    at, half = entry & (NR - 1), entry >> 8
                    k, u = at >> 5, at & 7
                    start = u * ROWS + 4 * ((at >> 3) & 3) + z + jnp.where(k > c, 1, 0) + 2 * half
                    start = jnp.where(entry < UNITS, start, NC)
                    lane = (at & 3) * 32 + ((c - k) & 7) + 16 * half
                    counts = [list_ref[TALLY + (at >> 2), lane + 8 * m] for m in range(2)]
                    right = jnp.concatenate([same_ref[start], same_ref[start + 1]], axis=1)
                    zs.append(jnp.dot(left_ref[at, :, 0:2 * LABELS], right, preferred_element_type=F32))
                    now.append((at, start, counts))
                for entry in held:
                    unit_drain(*entry)
                done = [finish(v, diagonal) for v in zs]
                held = [(done[i][1], done[i][0]) + now[i] for i in range(WIDE)]
            return held

        return lax.fori_loop(0, trips, body, held)

    def split(count):
        whole = count // (WIDE * LONG)
        done = whole * (WIDE * LONG)
        return whole, done, (count - done + WIDE * SHORT - 1) // (WIDE * SHORT)

    zero = jnp.int32(0)
    held = [(jnp.zeros((128, 256), BF16), jnp.zeros((1, 256), F32), zero, zero, [zero, zero])
            for _ in range(WIDE)]
    held = run(held, lambda i: c * (SIDE * U) + i, 1, SIDE * U // WIDE, True)
    whole, done, rest = split(list_ref[TOTALS, 1])
    held = run(held, lambda i: list_ref[UNIT + (i >> 7), i & 127], whole, LONG, False)
    held = run(held, lambda i: list_ref[UNIT + ((i + done) >> 7), (i + done) & 127], rest, SHORT, False)
    for entry in held:
        unit_drain(*entry)

    def listed_drain(held):
        for lo in range(0, WIDE, 2):
            pair = held[lo:lo + 2]
            near = jnp.concatenate([lrow_ref[p[2]] for p in pair], axis=0)
            far = jnp.concatenate([differ_ref[p[3], 0:16] for p in pair], axis=0)
            o = jnp.dot(near, jnp.concatenate([p[0] for p in pair], axis=1), preferred_element_type=F32)
            v = lax.dot_general(far, jnp.concatenate([p[0] for p in pair], axis=0), NT,
                                preferred_element_type=F32)
            for m, p in enumerate(pair):
                lane, at = slice(m * 128, m * 128 + 128), m * 16
                w = weigh(p[1], p[4])
                arow_ref[p[2]] += w * (v[at:at + 8, lane] + v[at + 8:at + 16, lane])
                acol_ref[p[3]] += w * (o[at:at + 8, lane] + o[at + 8:at + 16, lane])

    def listed_run(held, offset, trips, laps):
        def body(it, held):
            for q in range(laps):
                zs, now = [], []
                for i in range(WIDE):
                    slot = offset + (it * laps + q) * WIDE + i
                    line, lane = LISTED + (slot >> 7) * 8, slot & 127
                    at, to, n = [list_ref[line + f, lane] for f in range(3)]
                    zs.append(jnp.dot(left_ref[at, :, 0:2 * LABELS], differ_ref[to], preferred_element_type=F32))
                    now.append((at, to, n))
                listed_drain(held)
                done = [finish(v) for v in zs]
                held = [(done[i][1], done[i][0]) + now[i] for i in range(WIDE)]
            return held

        return lax.fori_loop(0, trips, body, held)

    held = [(jnp.zeros((128, 128), BF16), jnp.zeros((1, 128), F32), zero, zero, zero) for _ in range(WIDE)]
    whole, done, rest = split(list_ref[TOTALS, 0])
    held = listed_run(held, 0, whole, LONG)
    listed_drain(listed_run(held, done, rest, SHORT))

    @pl.loop(0, COLS)
    def _(k):
        for yy in range(SIDE):
            here = pl.ds((k * SIDE + yy) * U, U)
            mass = arow_ref[here, 3, :]
            for w in range(3):
                pulled = rows_ref[k, yy, w] * mass - arow_ref[here, w, :]
                prow_ref[k, yy, w] = pulled * (-1.0 / 512.0)

    @pl.loop(0, SIDE)
    def _(zz):
        for yy in range(SIDE):
            here = pl.ds(4 * yy + zz, U, stride=ROWS)
            mass = acol_ref[here, 4, :]
            for w in range(3):
                pulled = cols_ref[zz, yy, w] * mass - 2.0 * acol_ref[here, w, :]
                pcol_ref[zz, yy, w] = pulled * (-1.0 / 512.0)


def pairs_call(listing, bounds, rows, cols, left, lrow):
    return pl.pallas_call(
        pair_kernel,
        out_shape=[jax.ShapeDtypeStruct(rows.shape, F32), jax.ShapeDtypeStruct(cols.shape, F32)],
        in_specs=[SMEM] + [VMEM] * 5, out_specs=[VMEM] * 2,
        scratch_shapes=[
            pltpu.VMEM((SIDE, U, 24, BEADS), F32),
            pltpu.VMEM((NC + PAD + 2, 2 * LABELS, BEADS), BF16),
            pltpu.VMEM((NC + 1, 2 * LABELS, BEADS), BF16),
            pltpu.VMEM((NR, 8, BEADS), F32),
            pltpu.VMEM((NC + PAD + 2, 8, BEADS), F32),
        ],
        compiler_params=pltpu.CompilerParams(vmem_limit_bytes=32 << 20),
        name="pairs",
    )(listing, bounds, rows, cols, left, lrow)


def on_device(coords, chrom_lengths, band_counts, inter_pairs, inter_counts):
    part = coords.shape[1:]
    lens = chrom_lengths.reshape(1, -1)
    flipped = jnp.transpose(inter_pairs, (0, 2, 1))
    sems = 2 * SIDE + COLS + SIDE * (SIDE + COLS)
    rows, cols, listing, bounds, left, lrow = pl.pallas_call(
        gather_kernel,
        out_shape=[jax.ShapeDtypeStruct((COLS, SIDE) + part, F32), jax.ShapeDtypeStruct((SIDE, SIDE) + part, F32),
                   jax.ShapeDtypeStruct((LINES, 128), I32), jax.ShapeDtypeStruct((2, LABELS, BEADS), I32),
                   jax.ShapeDtypeStruct((NR, BEADS, 128), BF16), jax.ShapeDtypeStruct((NR, 16, BEADS), BF16)],
        in_specs=[HBM] * 5, out_specs=[VMEM] * 6,
        scratch_shapes=[
            pltpu.VMEM(lens.shape, I32),
            pltpu.VMEM(flipped.shape[1:], I32),
            pltpu.VMEM(inter_counts.shape, I32),
            pltpu.VMEM((3, 32, 128), I32),
            pltpu.VMEM((SIDE, U, 24, BEADS), F32),
            pltpu.VMEM((COLS,) + band_counts.shape, I32),
            pltpu.SemaphoreType.DMA((sems,)),
            pltpu.SemaphoreType.DMA((sems,)),
            pltpu.SemaphoreType.DMA((6,)),
        ],
        compiler_params=pltpu.CompilerParams(collective_id=0, has_side_effects=True, vmem_limit_bytes=24 << 20),
        name="gather",
    )(*[pltpu.with_memory_space_constraint(v, pltpu.HBM)
        for v in (coords, band_counts, lens, flipped, inter_counts)])
    prow, pcol = pairs_call(listing, bounds, rows, cols, left, lrow)
    return pl.pallas_call(
        scatter_kernel,
        out_shape=jax.ShapeDtypeStruct(coords.shape, F32),
        in_specs=[VMEM] * 2, out_specs=VMEM,
        scratch_shapes=[
            pltpu.VMEM((SIDE + COLS - 2, SIDE) + part, F32),
            pltpu.VMEM((2, SIDE) + part, F32),
            pltpu.VMEM((SIDE - 1,) + part, F32),
            pltpu.VMEM((SIDE - 1,) + part, F32),
            pltpu.SemaphoreType.DMA((SIDE * (SIDE + COLS) + SIDE,)),
            pltpu.SemaphoreType.DMA((SIDE * (SIDE + COLS) + SIDE,)),
            pltpu.SemaphoreType.DMA((2,)),
        ],
        compiler_params=pltpu.CompilerParams(collective_id=1, has_side_effects=True, vmem_limit_bytes=24 << 20),
        name="scatter",
    )(prow, pcol)


def solution(mesh):
    placed = (P(None, None, None, ("row", "col")), P(), P(None, None, ("row", "col"), None), P(), P())
    return jax.shard_map(on_device, mesh=mesh, in_specs=placed,
                         out_specs=P(None, None, None, ("row", "col")), check_vma=False)
```
